32 devices in a mesh: row: 4 (over y, x), ctx: 8 (over z, core).
Axes of the slice: x: 2, y: 2, z: 4, core: 2. Of those that a mesh axis runs over, the one named last changes fastest.
Arguments:
- inputs: bfloat16 [4, 1024, 1024], P('row', 'ctx'), may hold values from -6 to 6
- lengths: int32 [4], P('row'), may hold values from 1 to 1024, 3328 in all
- gain_attn: float32 [1024], replicated, may hold values from 0.25 to 1.75
- w_fact: bfloat16 [1024, 800], replicated, may hold values from -0.25 to 0.25
- w_out: bfloat16 [1024, 1024], replicated, may hold values from -1.5 to 1.5
- gain_ffn: float32 [1024], replicated, may hold values from 0.25 to 1.75
- w_gate: bfloat16 [1024, 2816], replicated, may hold values from -0.1875 to 0.1875
- w_up: bfloat16 [1024, 2816], replicated, may hold values from -0.1875 to 0.1875
- w_down: bfloat16 [2816, 1024], replicated, may hold values from -0.109375 to 0.109375
- cotangent: bfloat16 [4, 1024, 1024], P('row', 'ctx'), may hold values from -6 to 6
Outputs:
- block_out: bfloat16 [4, 1024, 1024], P('row', 'ctx')
- grad_inputs: float32 [4, 1024, 1024], P('row', 'ctx')
- grad_gain_attn: float32 [1024], replicated
- grad_w_fact: float32 [1024, 800], P('ctx', 'row')
- grad_w_out: float32 [1024, 1024], P('ctx', 'row')
- grad_gain_ffn: float32 [1024], replicated
- grad_w_gate: float32 [1024, 2816], P('ctx', 'row')
- grad_w_up: float32 [1024, 2816], P('ctx', 'row')
- grad_w_down: float32 [2816, 1024], P('ctx', 'row')
The draws below stay inside these ranges and needn't reach their ends.
Inputs may be any that keep to these rules, and one draw needn't show every extreme that they name: `lengths`: the longest row is full.
All inputs are finite; a program needn't handle non-finite values. No bound on the sum of `lengths` on one device may be relied on, other than what follows from the above.
Results may differ from the reference program's by a relative error of at most 0.015.
The reference program's roundings to bfloat16 on the way count: a program that leaves them out, or rounds other values in their place, can miss the bound.
Values may be sent and summed in bfloat16 or wider, within the bound.
No kernel may reach another device: no remote copies, remote signals or barrier semaphores. Data moves between devices by JAX's collectives and lax.ppermute only.
A program may use at most 384 MiB of HBM per device.

```python
import math
from functools import partial
import jax
import jax.numpy as jnp
import numpy as np
from jax import lax

D = 1024
H = 16
DH = 64
RQ = 6
RK = 2
FF = 2816
NF = 800
SLOTS = 1024
ROWS = 4
N_CTX = 8


def level_of(rng, dims, shards, least, high):
    loudness, own = 1.0, jax.random.fold_in(rng, 6)
    for position, parts in shards:
        draws = jnp.exp(jax.random.uniform(jax.random.fold_in(own, position), (parts,), jnp.float32, least / len(shards), high / len(shards)))
        loudness = loudness * jnp.repeat(draws, dims[position] // parts).reshape([-1 if axis == position else 1 for axis in range(len(dims))])
    return loudness


def split_up(count, total, bound, slope):
    weights = [(1 << 20) // math.isqrt(standing ** slope) + 1 for standing in range(2, count + 1)]
    rest, given = total - bound - (count - 1), [1] * (count - 1)
    while rest > 0:
        candidates = [i for i in range(count - 1) if given[i] < bound]
        pool, remaining = sum([weights[i] for i in candidates]), rest
        for i in candidates:
            extra = min(bound - given[i], max(1, remaining * weights[i] // pool), rest)
            given[i] = given[i] + extra
            rest = rest - extra
    return np.array([bound] + given)


def ragged(rng, amount, total, bound, lean):
    if amount == 2:
        one = jax.random.randint(rng, (), max(1, total - bound), min(bound, total - 1) + 1)
        return jnp.stack([one, total - one])
    sizes = jnp.asarray(split_up(amount, total, bound, lean), jnp.int32)
    twos = (amount - 1) // 2
    source_of, taker = sizes[1:1 + 2 * twos:2], sizes[2:2 + 2 * twos:2]
    slack = jnp.minimum(source_of - 1, bound - taker)
    moved = jax.random.randint(jax.random.fold_in(rng, 1), (twos,), 0, 1 << 20) % (slack + 1)
    sizes = sizes.at[1:1 + 2 * twos:2].set(source_of - moved).at[2:2 + 2 * twos:2].set(taker + moved)
    return sizes[jax.random.permutation(jax.random.fold_in(rng, 2), amount)]


def scatter_about(own_key, shape, spread, most, shards=(), kind=jnp.bfloat16):
    drawn = spread * jax.random.normal(own_key, shape, jnp.float32)
    if shards:
        drawn = drawn * level_of(own_key, shape, shards, -0.22, 0.18)
    return jnp.clip(drawn, -most, most).astype(kind)


def setup_inputs(seed: int = 0) -> dict:
    splits = jax.random.split(jax.random.key(seed), 11)
    return {
        "inputs": scatter_about(splits[0], (ROWS, SLOTS, D), 1.0, 6.0, ((0, 4), (1, 8))),
        "lengths": ragged(splits[1], ROWS, ROWS * SLOTS * 13 // 16, SLOTS, 2).astype(jnp.int32),
        "gain_attn": jnp.clip(1.0 + 0.15 * jax.random.normal(splits[2], (D,), jnp.float32), 0.25, 1.75),
        "w_fact": scatter_about(splits[3], (D, NF), (D // 2) ** -0.5, 0.25),
        "w_out": scatter_about(splits[4], (H * DH, D), (H * DH // 64) ** -0.5, 1.5),
        "gain_ffn": jnp.clip(1.0 + 0.15 * jax.random.normal(splits[5], (D,), jnp.float32), 0.25, 1.75),
        "w_gate": scatter_about(splits[6], (D, FF), D ** -0.5, 0.1875),
        "w_up": scatter_about(splits[7], (D, FF), D ** -0.5, 0.1875),
        "w_down": scatter_about(splits[8], (FF, D), FF ** -0.5, 0.109375),
        "cotangent": scatter_about(splits[9], (ROWS, SLOTS, D), 1.0, 6.0, ((0, 4), (1, 8))),
    }


@jax.custom_vjp
def low(v):
    return lax.optimization_barrier(v.astype(jnp.bfloat16)).astype(jnp.float32)

@jax.custom_vjp
def low_back(v):
    return v

def low_keep(v):
    return (low(v), None)

def low_pass(kept, grad):
    return (grad,)

def back_keep(v):
    return (v, None)

def back_low(kept, grad):
    return (low(grad),)
low.defvjp(low_keep, low_pass)
low_back.defvjp(back_keep, back_low)

def slot_position(index, block_len, slots_all):
    block_id = index // (2 * block_len)
    within = index % (2 * block_len)
    return jnp.where(within < block_len, block_id * block_len + within, (slots_all // block_len - 1 - block_id) * block_len + within - block_len)

def rope_angles(positions, head_dim):
    half_dim = head_dim // 2
    frequency = jnp.exp(-jnp.log(10000.0) * (2.0 * jnp.arange(half_dim, dtype=jnp.float32)) / head_dim)
    angles = positions.astype(jnp.float32)[:, None] * frequency[None, :]
    return (jnp.cos(angles)[:, None, :], jnp.sin(angles)[:, None, :])

def rotate(vectors, cosine, sine):
    half_dim = vectors.shape[-1] // 2
    upper_half = vectors[..., :half_dim]
    lower_half = vectors[..., half_dim:]
    return jnp.concatenate([upper_half * cosine - lower_half * sine, lower_half * cosine + upper_half * sine], axis=-1)

def inv_rms(values):
    return lax.rsqrt(lax.optimization_barrier(jnp.mean(values * values, axis=-1, keepdims=True)) + 1e-06)

def attend_row(positions, row_item):
    queries, kv_a, kv_b, length = row_item
    highest = lax.Precision.HIGHEST
    key_rows = low(jnp.einsum('tsh,tsd->thd', kv_a[:, :RK], kv_b[:, :RK], precision=highest) / RK)
    value_rows = low(jnp.einsum('tsh,tsd->thd', kv_a[:, RK:], kv_b[:, RK:], precision=highest) / RK)
    scores = low_back(jnp.einsum('qhd,khd->hqk', queries, key_rows, precision=highest) * DH ** (-0.5))
    allowed = (positions[None, :] <= positions[:, None]) & (positions[None, :] < length)
    scores = jnp.where(allowed[None], scores, -1e+30)
    row_max = lax.optimization_barrier(jnp.max(scores, axis=-1, keepdims=True))
    exponent = jnp.exp(scores - row_max)
    probability = low(exponent / lax.optimization_barrier(jnp.sum(exponent, axis=-1, keepdims=True)))
    return jnp.einsum('hqk,khd->qhd', probability, value_rows, precision=highest)

def block_span():
    return SLOTS // (2 * N_CTX)

def forward(lengths, inputs, gain_attn, w_fact, w_out, gain_ffn, w_gate, w_up, w_down):
    highest = lax.Precision.HIGHEST
    positions = slot_position(jnp.arange(SLOTS, dtype=jnp.int32), block_span(), SLOTS)
    cosine, sine = rope_angles(positions, DH)
    rows_count = inputs.shape[0]
    h_one = low(inputs * inv_rms(inputs) * gain_attn)
    factors = low_back(jnp.einsum('rtd,df->rtf', h_one, w_fact, precision=highest))
    start_k = RQ * (H + DH)
    start_b = start_k + 2 * RK * H
    query_a = factors[..., :RQ * H].reshape(rows_count, SLOTS, RQ, H)
    query_b = rotate(factors[..., RQ * H:start_k].reshape(rows_count, SLOTS, RQ, DH), cosine, sine)
    kv_a = low(factors[..., start_k:start_b].reshape(rows_count, SLOTS, 2 * RK, H))
    raw_b = factors[..., start_b:].reshape(rows_count, SLOTS, 2 * RK, DH)
    kv_b = low(jnp.concatenate([rotate(raw_b[:, :, :RK], cosine, sine), raw_b[:, :, RK:]], axis=2))
    queries = low(jnp.einsum('rtsh,rtsd->rthd', query_a, query_b, precision=highest) / RQ)
    mixed = lax.map(jax.checkpoint(partial(attend_row, positions)), (queries, kv_a, kv_b, lengths))
    mixed = low_back(low(mixed.reshape(rows_count, SLOTS, H * DH)))
    residual = inputs + low_back(jnp.einsum('rtc,cd->rtd', mixed, w_out, precision=highest))
    h_two = low(residual * inv_rms(residual) * gain_ffn)
    gate_pre = low_back(jnp.einsum('rtd,df->rtf', h_two, w_gate, precision=highest))
    upward = low_back(jnp.einsum('rtd,df->rtf', h_two, w_up, precision=highest))
    hidden = low(jax.nn.silu(gate_pre) * upward)
    return residual + jnp.einsum('rtf,fd->rtd', hidden, w_down, precision=highest)

def reference(inputs, lengths, gain_attn, w_fact, w_out, gain_ffn, w_gate, w_up, w_down, cotangent):
    block_out, pull_back = jax.vjp(partial(forward, lengths), inputs.astype(jnp.float32), gain_attn.astype(jnp.float32), w_fact.astype(jnp.float32), w_out.astype(jnp.float32), gain_ffn.astype(jnp.float32), w_gate.astype(jnp.float32), w_up.astype(jnp.float32), w_down.astype(jnp.float32))
    positions = slot_position(jnp.arange(SLOTS, dtype=jnp.int32), block_span(), SLOTS)
    valid_mask = (positions[None, :] < lengths[:, None]).astype(jnp.float32)
    grads = pull_back(cotangent.astype(jnp.float32) * valid_mask[:, :, None])
    return (block_out.astype(jnp.bfloat16), grads[0], grads[1], grads[2], grads[3], grads[4], grads[5], grads[6], grads[7])
```

```python
import functools

import jax
import jax.numpy as jnp
from jax import lax
from jax.experimental import pallas as pl
from jax.experimental.pallas import tpu as pltpu
from jax.sharding import PartitionSpec as P

H = 16
DH = 64
RQ = 6
RK = 2
EPS = 1e-06
QA = RQ * H
QF = RQ * (H + DH)
KA = 2 * RK * H
KB = 2 * RK * DH
KF = KA + KB
SCALE = DH ** (-0.5)
F32 = jnp.float32
BF16 = jnp.bfloat16
VMEM_BYTES = 56 * 1024 * 1024

NN = (((1,), (0,)), ((), ()))
NT = (((1,), (1,)), ((), ()))


def mm(a, b, dims=NN):
    return lax.dot_general(a, b, dims, preferred_element_type=F32)


def vmem():
    return pl.BlockSpec(memory_space=pltpu.VMEM)


def smem():
    return pl.BlockSpec(memory_space=pltpu.SMEM)


def hbm():
    return pl.BlockSpec(memory_space=pl.ANY)


def call(kernel, outs, ins, args, scratch=(), flops=0, moved=0, name=None):
    return pl.pallas_call(
        kernel,
        out_shape=[jax.ShapeDtypeStruct(s, d) for s, d in outs],
        in_specs=ins,
        out_specs=[vmem() for _ in outs],
        scratch_shapes=list(scratch),
        compiler_params=pltpu.CompilerParams(vmem_limit_bytes=VMEM_BYTES),
        cost_estimate=pl.CostEstimate(flops=flops, transcendentals=0, bytes_accessed=moved),
        name=name,
    )(*args)


def slot_position(index, block_len, slots_all):
    block_id = index // (2 * block_len)
    within = index % (2 * block_len)
    return jnp.where(
        within < block_len,
        block_id * block_len + within,
        (slots_all // block_len - 1 - block_id) * block_len + within - block_len,
    )


def rope_angles(positions):
    frequency = jnp.exp(
        -jnp.log(10000.0) * (2.0 * jnp.arange(DH // 2, dtype=F32)) / DH
    )
    angles = frequency[:, None] * positions.astype(F32)[None, :]
    return jnp.cos(angles), jnp.sin(angles)


def turn(rows, cosine, sine):
    half = DH // 2
    upper, lower = rows[:half], rows[half:]
    return jnp.concatenate([upper * cosine - lower * sine, lower * cosine + upper * sine], axis=0)


def turn_back(rows, cosine, sine):
    half = DH // 2
    upper, lower = rows[:half], rows[half:]
    return jnp.concatenate([upper * cosine + lower * sine, lower * cosine - upper * sine], axis=0)


def swap(value, axis, k):
    size = lax.axis_size(axis)
    return lax.ppermute(value, axis, [(j, j ^ k) for j in range(size)])


def tree_sum(parts):
    parts = list(parts)
    while len(parts) > 1:
        parts = [parts[i] + parts[i + 1] for i in range(0, len(parts), 2)]
    return parts[0]


def factor_kernel(
    x_ref, cot_ref, valid_ref, gain_ref, wf_ref, cos_ref, sin_ref,
    hg_ref, s1_ref, q_ref, qt_ref, qf_ref, kv_ref, ft,
):
    width = x_ref.shape[1]
    x = x_ref[...].astype(F32)
    s1 = lax.rsqrt(jnp.mean(x * x, axis=1, keepdims=True) + EPS)
    s1_ref[...] = s1
    h1 = (x * s1 * gain_ref[...]).astype(BF16)
    hg_ref[:, :width] = h1
    hg_ref[:, width:] = (cot_ref[...].astype(F32) * valid_ref[...]).astype(BF16)
    ft[:wf_ref.shape[1], :] = mm(h1, wf_ref[...]).T
    cosine, sine = cos_ref[...], sin_ref[...]
    kv_ref[:KA, :] = ft[QF:QF + KA, :].astype(BF16)
    for r in range(2 * RK):
        rows = ft[QF + KA + r * DH:QF + KA + (r + 1) * DH, :]
        if r < RK:
            rows = turn(rows, cosine, sine)
        kv_ref[KA + r * DH:KA + (r + 1) * DH, :] = rows.astype(BF16)
    qf_ref[:QA, :] = ft[:QA, :]
    for r in range(RQ):
        qf_ref[QA + r * DH:QA + (r + 1) * DH, :] = turn(ft[QA + r * DH:QA + (r + 1) * DH, :], cosine, sine)
    for h in range(H):
        total = None
        for r in range(RQ):
            term = qf_ref[r * H + h:r * H + h + 1, :] * qf_ref[QA + r * DH:QA + (r + 1) * DH, :]
            total = term if total is None else total + term
        ft[h * DH:(h + 1) * DH, :] = total / RQ
    qt = ft[:H * DH, :]
    qt_ref[...] = qt.astype(BF16)
    q_ref[...] = qt.T.astype(BF16)


def project(x, cot, valid, gain, w_fact, cosine, sine):
    tokens, width = x.shape
    nf = w_fact.shape[1]
    return call(
        factor_kernel,
        [((tokens, 2 * width), BF16), ((tokens, 1), F32), ((tokens, H * DH), BF16), ((H * DH, tokens), BF16),
         ((QF, tokens), F32), ((KF, tokens), BF16)],
        [vmem()] * 7,
        (x, cot, valid, gain, w_fact, cosine, sine),
        [pltpu.VMEM((max(nf, H * DH), tokens), F32)],
        2 * tokens * width * nf, 2 * width * nf, "factors",
    )


def load_factors(pieces, a_rows, b_rows):
    at = 0
    for piece in pieces:
        n = piece.shape[1]
        a_rows[:, at:at + n] = piece[:KA, :].astype(F32)
        b_rows[:, at:at + n] = piece[KA:, :].astype(F32)
        at += n


def expand_pair(pair, side, a_rows, b_rows):
    halves = []
    for sub in range(2):
        total = None
        for r in range(RK):
            a = a_rows[pl.ds((side * RK + r) * H + 2 * pair + sub, 1), :]
            term = a * b_rows[(side * RK + r) * DH:(side * RK + r + 1) * DH, :]
            total = term if total is None else total + term
        halves.append((total * (1.0 / RK)).astype(BF16))
    return jnp.concatenate(halves, axis=0)


def stack_pair(rows):
    lane = lax.broadcasted_iota(jnp.int32, rows.shape, 1)
    zero = jnp.zeros_like(rows)
    return jnp.concatenate([jnp.where(lane < DH, rows, zero), jnp.where(lane < DH, zero, rows)], axis=0)


def pair_lanes(pair):
    return pl.ds(pl.multiple_of(pair * 2 * DH, 2 * DH), 2 * DH)


def attend_kernel(n_pieces, *refs):
    q_ref, bias_ref, wo_ref, x_ref, gain_ref = refs[:5]
    pieces = refs[5:5 + n_pieces]
    mh_ref, resid_ref, lse_ref, a_rows, b_rows, mixed = refs[5 + n_pieces:]
    tokens, width = x_ref.shape
    load_factors(pieces, a_rows, b_rows)
    bias = bias_ref[...]
    bias = jnp.concatenate([bias, bias], axis=0)

    def step(pair, carry):
        keys = expand_pair(pair, 0, a_rows, b_rows)
        values = expand_pair(pair, 1, a_rows, b_rows)
        q = stack_pair(q_ref[:, pair_lanes(pair)])
        scores = mm(q, keys) * SCALE + bias
        top = jnp.max(scores, axis=1, keepdims=True)
        exponent = jnp.exp(scores - top)
        total = jnp.sum(exponent, axis=1, keepdims=True)
        probs = (exponent * (1.0 / total)).astype(BF16)
        lse_ref[pair] = top + jnp.log(total)
        out = mm(probs, values, NT)
        lane = lax.broadcasted_iota(jnp.int32, (tokens, 2 * DH), 1)
        mixed[:, pair_lanes(pair)] = jnp.where(lane < DH, out[:tokens], out[tokens:]).astype(BF16)
        return carry

    lax.fori_loop(0, H // 2, step, 0)
    mh_ref[:, :width] = mixed[...]
    resid = x_ref[...].astype(F32) + mm(mixed[...], wo_ref[...])
    resid_ref[...] = resid
    s2 = lax.rsqrt(jnp.mean(resid * resid, axis=1, keepdims=True) + EPS)
    mh_ref[:, width:] = (resid * s2 * gain_ref[...]).astype(BF16)


def attend(q, bias, w_out, x, gain, pieces):
    tokens, width = x.shape
    slots = sum(p.shape[1] for p in pieces)
    return call(
        functools.partial(attend_kernel, len(pieces)),
        [((tokens, 2 * width), BF16), ((tokens, width), F32), ((H // 2, 2 * tokens, 1), F32)],
        [vmem()] * (5 + len(pieces)),
        (q, bias, w_out, x, gain, *pieces),
        [pltpu.VMEM((KA, slots), F32), pltpu.VMEM((KB, slots), F32), pltpu.VMEM((tokens, H * DH), BF16)],
        4 * tokens * slots * H * DH, 2 * width * width, "attend",
    )


def attend_back_kernel(n_pieces, *refs):
    q_ref, qt_ref, gm_ref, gmt_ref, lse_ref, bias_ref, qf_ref, cos_ref, sin_ref = refs[:9]
    pieces = refs[9:9 + n_pieces]
    gq_ref, gkv_ref, a_rows, b_rows, ga_rows, gb_rows, gqb_rows = refs[9 + n_pieces:]
    tokens = q_ref.shape[0]
    load_factors(pieces, a_rows, b_rows)
    gb_rows[...] = jnp.zeros_like(gb_rows)
    gqb_rows[...] = jnp.zeros_like(gqb_rows)

    def spread(rows):
        top = lax.broadcasted_iota(jnp.int32, rows.shape, 0) < DH
        zero = jnp.zeros_like(rows)
        return jnp.concatenate([jnp.where(top, rows, zero), jnp.where(top, zero, rows)], axis=1)

    def step(pair, carry):
        keys = expand_pair(pair, 0, a_rows, b_rows)
        values = expand_pair(pair, 1, a_rows, b_rows)
        rows = pl.ds(pl.multiple_of(pair * 2 * DH, 2 * DH), 2 * DH)
        both = (
            stack_pair(q_ref[:, pair_lanes(pair)]), stack_pair(gm_ref[:, pair_lanes(pair)]),
            spread(qt_ref[rows, :]), spread(gmt_ref[rows, :]), lse_ref[pair],
        )
        takes = [slice(0, 2 * tokens)] if keys.shape[1] <= 2048 else [slice(0, tokens), slice(tokens, 2 * tokens)]
        grad_q, grad_k, grad_v = [], None, None
        for take in takes:
            q, g, qt, gt, lse = both[0][take], both[1][take], both[2][:, take], both[3][:, take], both[4][take]
            heads = q.shape[0] // tokens
            scores = mm(q, keys) * SCALE + jnp.concatenate([bias_ref[...]] * heads, axis=0)
            probs = jnp.exp(scores - lse)
            grad_probs = mm(g, values)
            inner = jnp.sum(probs * grad_probs, axis=1, keepdims=True)
            grad_scores = (probs * (grad_probs - inner)).astype(BF16)
            grad_q.append(mm(keys, grad_scores, NT) * SCALE)
            gk, gv = mm(qt, grad_scores) * SCALE, mm(gt, probs.astype(BF16))
            grad_k, grad_v = (gk, gv) if grad_k is None else (grad_k + gk, grad_v + gv)
        grad_q = jnp.concatenate(grad_q, axis=1)
        for sub in range(2):
            head = 2 * pair + sub
            part = slice(sub * DH, (sub + 1) * DH)
            for side, grad in ((0, grad_k[part]), (1, grad_v[part])):
                for r in range(RK):
                    s = side * RK + r
                    row = pl.ds(s * H + head, 1)
                    seg = slice(s * DH, (s + 1) * DH)
                    ga_rows[row, :] = jnp.sum(grad * b_rows[seg, :], axis=0, keepdims=True) * (1.0 / RK)
                    gb_rows[seg, :] += grad * (a_rows[row, :] * (1.0 / RK))
            dq = grad_q[part, sub * tokens:(sub + 1) * tokens]
            for r in range(RQ):
                row = pl.ds(r * H + head, 1)
                seg = slice(QA + r * DH, QA + (r + 1) * DH)
                gq_ref[row, :] = jnp.sum(dq * qf_ref[seg, :], axis=0, keepdims=True) * (1.0 / RQ)
                gqb_rows[r * DH:(r + 1) * DH, :] += dq * (qf_ref[row, :] * (1.0 / RQ))
        return carry

    lax.fori_loop(0, H // 2, step, 0)
    cosine, sine = cos_ref[...], sin_ref[...]
    for r in range(RQ):
        gq_ref[QA + r * DH:QA + (r + 1) * DH, :] = turn_back(gqb_rows[r * DH:(r + 1) * DH, :], cosine, sine)
    at = 0
    for j in range(n_pieces):
        n = pieces[j].shape[1]
        m, k = j % 2, j // 2
        gkv_ref[m, k, :KA, :] = ga_rows[:, at:at + n].astype(BF16)
        gkv_ref[m, k, KA:, :] = gb_rows[:, at:at + n].astype(BF16)
        at += n


def attend_back(q, qt, gm, gmt, lse, bias, qf, cosine, sine, pieces):
    tokens = q.shape[0]
    slots = sum(p.shape[1] for p in pieces)
    n = len(pieces)
    return call(
        functools.partial(attend_back_kernel, n),
        [((QF, tokens), F32), ((2, n // 2, KF, slots // n), BF16)],
        [vmem()] * (9 + n),
        (q, qt, gm, gmt, lse, bias, qf, cosine, sine, *pieces),
        [pltpu.VMEM((KA, slots), F32), pltpu.VMEM((KB, slots), F32), pltpu.VMEM((KA, slots), F32),
         pltpu.VMEM((KB, slots), F32), pltpu.VMEM((RQ * DH, tokens), F32)],
        10 * tokens * slots * H * DH, 4 * tokens * slots, "attend_back",
    )


def ffn_kernel(
    place_ref, h2_ref, go_ref, wg_ref, wu_ref, wd_ref, resid_ref, gain_ref, wo_ref,
    out_ref, gain_grad_ref, gres_ref, gm_ref, gmt_ref, gbx_ref, branch, grad_h2, gb_rows,
):
    step = pl.program_id(0)

    @pl.when(step == 0)
    def _():
        branch[...] = jnp.zeros_like(branch)
        grad_h2[...] = jnp.zeros_like(grad_h2)

    h2, go = h2_ref[...], go_ref[...]
    gate, up = mm(h2, wg_ref[...]), mm(h2, wu_ref[...])
    grad_hidden = mm(go, wd_ref[...], NT)
    sig = jax.nn.sigmoid(gate)
    silu = gate * sig
    hidden = (silu * up).astype(BF16)
    grad_gate = (grad_hidden * up * sig * (1.0 + gate * (1.0 - sig))).astype(BF16)
    grad_up = (grad_hidden * silu).astype(BF16)
    branch[...] += mm(hidden, wd_ref[...])
    grad_h2[...] += mm(grad_gate, wg_ref[...], NT) + mm(grad_up, wu_ref[...], NT)

    @pl.when(step == pl.num_programs(0) - 1)
    def _():
        resid = resid_ref[...]
        out_ref[...] = (resid + branch[...]).astype(BF16)
        s2 = lax.rsqrt(jnp.mean(resid * resid, axis=1, keepdims=True) + EPS)
        n2 = resid * s2
        gh = grad_h2[...]
        gain_grad_ref[...] = jnp.sum(gh * n2, axis=0, keepdims=True)
        g2 = gh * gain_ref[...]
        gres = go_ref[...].astype(F32) + s2 * (g2 - n2 * jnp.mean(g2 * n2, axis=1, keepdims=True))
        gres_ref[...] = gres
        gb = gres.astype(BF16)
        gm = mm(gb, wo_ref[...], NT)
        gm_ref[...] = gm.astype(BF16)
        gmt_ref[...] = gm.T.astype(BF16)
        gb_rows[...] = gres.T.astype(BF16)
        n_rows, _, part, _ = gbx_ref.shape
        for k in range(n_rows):
            for m in range(2):
                block = (place_ref[0] ^ k) * 2 + (place_ref[1] ^ m)
                gbx_ref[k, m] = gb_rows[pl.ds(pl.multiple_of(block * part, part), part), :]


def feed_forward(place, mh, hg, w_gate, w_up, w_down, resid, gain, w_out, n_rows, chunk):
    tokens, width = resid.shape
    ff = w_gate.shape[1]
    part = width // (2 * n_rows)
    one = lambda j, p: (0, 0)
    second = lambda j, p: (0, 1)
    return pl.pallas_call(
        ffn_kernel,
        grid_spec=pltpu.PrefetchScalarGridSpec(
            num_scalar_prefetch=1,
            grid=(ff // chunk,),
            in_specs=[
                pl.BlockSpec((tokens, width), second),
                pl.BlockSpec((tokens, width), second),
                pl.BlockSpec((width, chunk), lambda j, p: (0, j)),
                pl.BlockSpec((width, chunk), lambda j, p: (0, j)),
                pl.BlockSpec((chunk, width), lambda j, p: (j, 0)),
                pl.BlockSpec((tokens, width), one),
                pl.BlockSpec((1, width), one),
                pl.BlockSpec((width, width), one),
            ],
            out_specs=[
                pl.BlockSpec((tokens, width), one),
                pl.BlockSpec((1, width), one),
                pl.BlockSpec((tokens, width), one),
                pl.BlockSpec((tokens, width), one),
                pl.BlockSpec((width, tokens), one),
                pl.BlockSpec((n_rows, 2, part, tokens), lambda j, p: (0, 0, 0, 0)),
            ],
            scratch_shapes=[
                pltpu.VMEM((tokens, width), F32),
                pltpu.VMEM((tokens, width), F32),
                pltpu.VMEM((width, tokens), BF16),
            ],
        ),
        out_shape=[
            jax.ShapeDtypeStruct((tokens, width), BF16),
            jax.ShapeDtypeStruct((1, width), F32),
            jax.ShapeDtypeStruct((tokens, width), F32),
            jax.ShapeDtypeStruct((tokens, width), BF16),
            jax.ShapeDtypeStruct((width, tokens), BF16),
            jax.ShapeDtypeStruct((n_rows, 2, part, tokens), BF16),
        ],
        compiler_params=pltpu.CompilerParams(vmem_limit_bytes=VMEM_BYTES),
        cost_estimate=pl.CostEstimate(
            flops=12 * tokens * width * ff, transcendentals=tokens * ff, bytes_accessed=6 * width * ff
        ),
        name="feed_forward",
    )(place, mh, hg, w_gate, w_up, w_down, resid, gain, w_out)


def weight_kernel(n_pieces, ordered, *refs):
    place_ref, wg_ref, wu_ref, wd_ref = refs[:4]
    mh_pieces = refs[4:4 + n_pieces]
    hg_pieces = refs[4 + n_pieces:4 + 2 * n_pieces]
    gb_pieces = refs[4 + 2 * n_pieces:4 + 2 * n_pieces + 2]
    up_ref, down_ref, h2s, gos, mixs, gbs, sems = refs[4 + 2 * n_pieces + 2:]
    tokens, width = mh_pieces[0].shape[0], h2s.shape[1]
    ff = wd_ref.shape[0]
    groups = []
    for s, (slab, pieces, col) in enumerate(((h2s, mh_pieces, 1), (gos, hg_pieces, 1), (mixs, mh_pieces, 0))):
        copies = []
        for j, piece in enumerate(pieces):
            copies.append(pltpu.make_async_copy(
                piece.at[:, pl.ds(col * width, width)], slab.at[pl.ds(j * tokens, tokens), :], sems.at[s, j]))
        groups.append(copies)
    for copies in groups:
        for copy in copies:
            copy.start()
    wgt = wg_ref[...].T
    wut = wu_ref[...].T
    for j in range(n_pieces):
        half = n_pieces // 2
        gbs[:, j * tokens:(j + 1) * tokens] = gb_pieces[j // half][j % half]
    for copy in groups[0]:
        copy.wait()
    gate = mm(wgt, h2s[...], NT)
    up = mm(wut, h2s[...], NT)
    for copy in groups[1]:
        copy.wait()
    grad_hidden = mm(wd_ref[...], gos[...], NT)
    sig = jax.nn.sigmoid(gate)
    silu = gate * sig
    hidden = (silu * up).astype(BF16)
    grad_gate = (grad_hidden * up * sig * (1.0 + gate * (1.0 - sig))).astype(BF16)
    grad_up = (grad_hidden * silu).astype(BF16)
    for copy in groups[2]:
        copy.wait()
    n_z = up_ref.shape[0]
    cols = width // n_z
    half = cols // 2
    for slot, k in enumerate(halving_order(n_z)):
        if ordered:
            z = place_ref[2] ^ k
            core = place_ref[1]
            first = pl.ds(pl.multiple_of(z * cols + core * half, half), half)
            other = pl.ds(pl.multiple_of(z * cols + (1 - core) * half, half), half)
            straight = pl.ds(pl.multiple_of(z * cols, cols), cols)
            pick = lambda slab: jnp.concatenate([slab[:, first], slab[:, other]], axis=1)
        else:
            straight = slice(slot * cols, (slot + 1) * cols)
            pick = lambda slab: slab[:, straight]
        h2c = pick(h2s)
        up_ref[slot, :ff, :] = mm(grad_gate, h2c).astype(BF16)
        up_ref[slot, ff:, :] = mm(grad_up, h2c).astype(BF16)
        down_ref[slot, :ff, :] = mm(hidden, gos[:, straight]).astype(BF16)
        down_ref[slot, ff:, :] = mm(gbs[...], pick(mixs)).astype(BF16)


def halving_order(n):
    order = [0]
    k = n // 2
    while k >= 1:
        order = order + [o | k for o in order]
        k //= 2
    return order


def halve(value, axis, unit, n):
    k = 1
    total = value.astype(F32)
    while n > 1:
        n //= 2
        got = swap(total[n:].astype(BF16), axis, unit * k)
        total = total[:n] + got.astype(F32)
        k *= 2
    return total[0]


def weight_grads(place, wg, wu, wd, mh_pieces, hg_pieces, gb_pieces, n_z, ordered):
    n = len(mh_pieces)
    tokens = mh_pieces[0].shape[0]
    width, ff = wg.shape
    part = gb_pieces[0].shape[1]
    cols = width // n_z
    total = n * tokens
    return call(
        functools.partial(weight_kernel, n, ordered),
        [((n_z, 2 * ff, cols), BF16), ((n_z, ff + part, cols), BF16)],
        [smem(), vmem(), vmem(), vmem()] + [hbm()] * (2 * n) + [vmem()] * 2,
        (place, wg, wu, wd, *mh_pieces, *hg_pieces, *gb_pieces),
        [pltpu.VMEM((total, width), BF16), pltpu.VMEM((total, width), BF16), pltpu.VMEM((total, width), BF16),
         pltpu.VMEM((part, total), BF16), pltpu.SemaphoreType.DMA((3, n))],
        12 * total * width * ff, 6 * width * ff + 6 * total * width, "weight_grads",
    )


def input_kernel(
    place_ref, gq_ref, own_ref, got_ref, wf_ref, x_ref, s1_ref, gain_ref, gres_ref, cos_ref, sin_ref,
    gfx_ref, gin_ref, gain_grad_ref, gf,
):
    cosine, sine = cos_ref[...], sin_ref[...]
    n_got = got_ref.shape[0]
    kv = own_ref[...].astype(F32)
    for k in range(n_got):
        kv = kv + got_ref[k].astype(F32)
    gf[:QF, :] = gq_ref[...]
    gf[QF:QF + KA, :] = kv[:KA]
    for r in range(2 * RK):
        rows = kv[KA + r * DH:KA + (r + 1) * DH]
        if r < RK:
            rows = turn_back(rows, cosine, sine)
        gf[QF + KA + r * DH:QF + KA + (r + 1) * DH, :] = rows
    n_rows, part, _ = gfx_ref.shape
    for k in range(n_rows):
        block = place_ref[0] ^ k
        gfx_ref[k] = gf[pl.ds(pl.multiple_of(block * part, 8), part), :].astype(BF16)
    grad = gf[...].T.astype(BF16)
    grad_h1 = mm(grad, wf_ref[...], NT)
    s1 = s1_ref[...]
    n1 = x_ref[...].astype(F32) * s1
    gain_grad_ref[...] = jnp.sum(grad_h1 * n1, axis=0, keepdims=True)
    g1 = grad_h1 * gain_ref[...]
    gin_ref[...] = gres_ref[...] + s1 * (g1 - n1 * jnp.mean(g1 * n1, axis=1, keepdims=True))


def input_grads(place, gq, own, got, w_fact, x, s1, gain, gres, cosine, sine, n_rows):
    tokens, width = x.shape
    nf = w_fact.shape[1]
    return call(
        input_kernel,
        [((n_rows, nf // n_rows, tokens), BF16), ((tokens, width), F32), ((1, width), F32)],
        [smem()] + [vmem()] * 10,
        (place, gq, own, got, w_fact, x, s1, gain, gres, cosine, sine),
        [pltpu.VMEM((nf, tokens), F32)],
        2 * tokens * width * nf, 2 * width * nf, "input_grads",
    )


def fact_kernel(n_pieces, ordered, *refs):
    place_ref = refs[0]
    hg_pieces = refs[1:1 + n_pieces]
    gf_pieces = refs[1 + n_pieces:1 + 2 * n_pieces]
    out_ref, h1s, gfs = refs[1 + 2 * n_pieces:]
    tokens = gf_pieces[0].shape[1]
    n_z, _, cols = out_ref.shape
    for j in range(n_pieces):
        gfs[:, j * tokens:(j + 1) * tokens] = gf_pieces[j][...]
        for k in range(n_z):
            if ordered:
                block = (place_ref[2] ^ k) * 2 + place_ref[1]
                where = pl.ds(pl.multiple_of(block * cols, cols), cols)
                h1s[j * tokens:(j + 1) * tokens, k * cols:(k + 1) * cols] = hg_pieces[j][:, where]
            else:
                h1s[j * tokens:(j + 1) * tokens, k * cols:(k + 1) * cols] = hg_pieces[j][:, k * cols:(k + 1) * cols]
    full = mm(gfs[...], h1s[...]).astype(BF16)
    for k in range(n_z):
        out_ref[k] = full[:, k * cols:(k + 1) * cols]


def fact_grads(place, hg_pieces, gf_pieces, n_z, cols, ordered):
    n = len(hg_pieces)
    part, tokens = gf_pieces[0].shape
    return call(
        functools.partial(fact_kernel, n, ordered),
        [((n_z, part, cols), BF16)],
        [smem()] + [vmem()] * (2 * n),
        (place, *hg_pieces, *gf_pieces),
        [pltpu.VMEM((n * tokens, n_z * cols), BF16), pltpu.VMEM((part, n * tokens), BF16)],
        2 * n * tokens * part * n_z * cols, 0, "fact_grads",
    )[0]


def body(inputs, lengths, gain_attn, w_fact, w_out, gain_ffn, w_gate, w_up, w_down, cotangent):
    seqs, local_len, width = inputs.shape
    tokens = seqs * local_len
    n_rows, n_ctx = lax.axis_size("row"), lax.axis_size("ctx")
    n_z = n_ctx // 2
    row, ctx = lax.axis_index("row"), lax.axis_index("ctx")
    z, core = ctx // 2, ctx % 2
    slots_all = local_len * n_ctx
    block_len = local_len // 2
    ff = w_gate.shape[1]
    ff_part = ff // (2 * n_rows)
    place = jnp.stack([row, core, z]).astype(jnp.int32)

    within = jnp.arange(local_len, dtype=jnp.int32)
    local_pos = jnp.tile(slot_position(ctx * local_len + within, block_len, slots_all), seqs)
    local_seq = jnp.repeat(jnp.arange(seqs, dtype=jnp.int32), local_len)
    cosine, sine = rope_angles(local_pos)
    valid = (local_pos < jnp.repeat(lengths, local_len)).astype(F32)[:, None]
    piece_of = jnp.arange(n_ctx, dtype=jnp.int32) ^ ctx
    key_pos = jnp.tile(
        slot_position(piece_of[:, None] * local_len + within[None, :], block_len, slots_all)[:, None, :], (1, seqs, 1)
    ).reshape(-1)
    key_seq = jnp.tile(local_seq, n_ctx)
    key_len = jnp.tile(jnp.repeat(lengths, local_len), n_ctx)
    allowed = (
        (key_pos[None, :] <= local_pos[:, None])
        & (key_pos < key_len)[None, :]
        & (key_seq[None, :] == local_seq[:, None])
    )
    bias = jnp.where(allowed, 0.0, -1e30).astype(F32)

    x = inputs.reshape(tokens, width)
    cot = cotangent.reshape(tokens, width)
    gain_one, gain_two = gain_attn[None, :], gain_ffn[None, :]

    hg, s1, q, qt, qf, kv = project(x, cot, valid, gain_one, w_fact, cosine, sine)

    z_kv = [kv] + [swap(kv, "ctx", 2 * k) for k in range(1, n_z)]
    kv_pieces = []
    for part in z_kv:
        kv_pieces += [part, swap(part, "ctx", 1)]

    def spread(value):
        same = [value] + [swap(value, "row", k) for k in range(1, n_rows)]
        return same + [swap(part, "ctx", 1) for part in same]

    hg_pieces = spread(hg)
    mh, resid, lse = attend(q, bias, w_out, x, gain_two, kv_pieces)
    mh_pieces = spread(mh)
    block_out, gain_two_part, gres, gm, gmt, gbx = feed_forward(
        place, mh, hg, w_gate, w_up, w_down, resid, gain_two, w_out, n_rows, 256
    )
    gb_same = [gbx[0]] + [swap(gbx[k], "row", k) for k in range(1, n_rows)]
    gb_own = jnp.stack([part[0] for part in gb_same])
    gb_other = swap(jnp.stack([part[1] for part in gb_same]), "ctx", 1)

    at = (row * 2 + core) * ff_part
    wg_part = lax.dynamic_slice(w_gate, (0, at), (width, ff_part))
    wu_part = lax.dynamic_slice(w_up, (0, at), (width, ff_part))
    wd_part = lax.dynamic_slice(w_down, (at, 0), (ff_part, width))
    per = n_ctx // (2 * n_rows)
    ordered = (width // n_ctx) % 128 == 0 and per == 1
    up_parts, down_parts = weight_grads(
        place, wg_part, wu_part, wd_part, mh_pieces, hg_pieces, (gb_own, gb_other), n_z, ordered
    )
    if not ordered:
        turns = jnp.asarray(halving_order(n_z), jnp.int32) ^ z
        cores = jnp.arange(2, dtype=jnp.int32) ^ core

        def own_first(parts):
            blocks = parts.reshape(n_z, parts.shape[1], 2, width // n_ctx)
            return jnp.take(blocks, cores, axis=2).reshape(parts.shape)

        up_parts = own_first(jnp.take(up_parts, turns, axis=0))
        out_parts = own_first(jnp.take(down_parts[:, ff_part:], turns, axis=0))
        down_parts = down_parts[:, :ff_part].transpose(1, 0, 2).reshape(per, ff_part // per, n_rows, width // n_rows)
        down_parts = jnp.take(down_parts.transpose(0, 2, 1, 3).reshape(n_z, ff_part // per, -1), turns, axis=0)

    gq, gkv = attend_back(q, qt, gm, gmt, lse, bias, qf, cosine, sine, kv_pieces)
    gkv_z = (gkv[0].astype(F32) + swap(gkv[1], "ctx", 1).astype(F32)).astype(BF16)
    got = jnp.stack([swap(gkv_z[k], "ctx", 2 * k) for k in range(1, n_z)])
    gfx, grad_inputs, gain_one_part = input_grads(
        place, gq, gkv_z[0], got, w_fact, x, s1, gain_one, gres, cosine, sine, n_rows
    )

    gains = jnp.concatenate([gain_one_part, gain_two_part], axis=0)
    gf_same = [gfx[0]] + [swap(gfx[k], "row", k) for k in range(1, n_rows)]
    gains = tree_sum([gains] + [swap(gains, "row", k) for k in range(1, n_rows)])
    gf_pieces = gf_same + [swap(part, "ctx", 1) for part in gf_same]
    gains = gains + swap(gains, "ctx", 1)
    fact_cols = width // n_ctx
    fact_parts = fact_grads(place, hg_pieces, gf_pieces, n_z if ordered else n_ctx, fact_cols, ordered)
    if not ordered:
        fact_parts = jnp.take(fact_parts, (jnp.arange(n_z, dtype=jnp.int32) ^ z) * 2 + core, axis=0)
    grad_fact = tree_sum(
        [fact_parts[0].astype(F32)] + [swap(fact_parts[k], "ctx", 2 * k).astype(F32) for k in range(1, n_z)]
    ).T
    gains = tree_sum([gains] + [swap(gains, "ctx", 2 * k) for k in range(1, n_z)])

    up_total = halve(up_parts, "ctx", 2, n_z)
    down_total = halve(down_parts, "ctx", 2, n_z)
    if ordered:
        down_total, out_total = down_total[:ff_part], down_total[ff_part:]
    else:
        out_total = halve(out_parts, "ctx", 2, n_z)
    half = width // n_ctx
    mine = jnp.concatenate([up_total[:, :half], out_total[:, :half]], axis=0)
    other = jnp.concatenate([up_total[:, half:], out_total[:, half:]], axis=0)
    other = swap(other.astype(BF16), "ctx", 1).astype(F32)
    first = jnp.where(core == 0, mine, other)
    second = jnp.where(core == 0, other, mine)

    def columns(lo, hi):
        return jnp.concatenate([first[lo:hi], second[lo:hi]], axis=0).T

    grad_gate = columns(0, ff_part)
    grad_up = columns(ff_part, 2 * ff_part)
    grad_out = columns(2 * ff_part, first.shape[0])

    moves = []
    for r in range(n_rows):
        for c in range(2):
            for p in range(n_z):
                b, s = p // n_rows, p % n_rows
                moves.append((r * n_ctx + 2 * p + c, s * n_ctx + (r * 2 + c) * per + b))
    grad_down = lax.ppermute(down_total.astype(BF16), ("row", "ctx"), moves).astype(F32)

    return (
        block_out.reshape(inputs.shape),
        grad_inputs.reshape(inputs.shape),
        gains[0],
        grad_fact,
        grad_out,
        gains[1],
        grad_gate,
        grad_up,
        grad_down,
    )


def solution(mesh):
    placed = (P("row", "ctx", None), P("row"), P(), P(), P(), P(), P(), P(), P(), P("row", "ctx", None))
    return jax.shard_map(
        body,
        mesh=mesh,
        in_specs=placed,
        out_specs=(
            P("row", "ctx", None), P("row", "ctx", None), P(), P("ctx", "row"), P("ctx", "row"), P(),
            P("ctx", "row"), P("ctx", "row"), P("ctx", "row"),
        ),
        check_vma=False,
    )
```

```python
import functools

import jax
import jax.numpy as jnp
from jax import lax
from jax.experimental import pallas as pl
from jax.experimental.pallas import tpu as pltpu
from jax.sharding import Mesh
from jax.sharding import PartitionSpec as P

H = 16
DH = 64
RQ = 6
RK = 2
EPS = 1e-06
QA = RQ * H
QF = RQ * (H + DH)
KA = 2 * RK * H
KB = 2 * RK * DH
KF = KA + KB
SCALE = DH ** (-0.5)
F32 = jnp.float32
BF16 = jnp.bfloat16
VMEM_BYTES = 56 * 1024 * 1024

NN = (((1,), (0,)), ((), ()))
NT = (((1,), (1,)), ((), ()))


def mm(a, b, dims=NN):
    return lax.dot_general(a, b, dims, preferred_element_type=F32)


def vmem():
    return pl.BlockSpec(memory_space=pltpu.VMEM)


def smem():
    return pl.BlockSpec(memory_space=pltpu.SMEM)


def hbm():
    return pl.BlockSpec(memory_space=pltpu.HBM)


def call(kernel, outs, ins, args, scratch=(), flops=0, moved=0, name=None):
    return pl.pallas_call(
        kernel,
        out_shape=[jax.ShapeDtypeStruct(s, d) for s, d in outs],
        in_specs=ins,
        out_specs=[vmem() for _ in outs],
        scratch_shapes=list(scratch),
        compiler_params=pltpu.CompilerParams(vmem_limit_bytes=VMEM_BYTES),
        cost_estimate=pl.CostEstimate(flops=flops, transcendentals=0, bytes_accessed=moved),
        name=name,
    )(*args)


def slot_position(index, block_len, slots_all):
    block_id = index // (2 * block_len)
    within = index % (2 * block_len)
    return jnp.where(
        within < block_len,
        block_id * block_len + within,
        (slots_all // block_len - 1 - block_id) * block_len + within - block_len,
    )


def turn(rows, cosine, sine):
    half = DH // 2
    upper, lower = rows[:half], rows[half:]
    return jnp.concatenate([upper * cosine - lower * sine, lower * cosine + upper * sine], axis=0)


def turn_back(rows, cosine, sine):
    half = DH // 2
    upper, lower = rows[:half], rows[half:]
    return jnp.concatenate([upper * cosine + lower * sine, lower * cosine - upper * sine], axis=0)


ROW = ("r1", "r0")
CTX = ("z", "core")
GROUP = ("r1", "r0", "core")


def swap(value, axis, k):
    size = lax.axis_size(axis)
    return lax.ppermute(value, axis, [(j, j ^ k) for j in range(size)])


def tree_sum(parts):
    parts = list(parts)
    while len(parts) > 1:
        parts = [parts[i] + parts[i + 1] for i in range(0, len(parts), 2)]
    return parts[0]


def factor_kernel(
    x_ref, cot_ref, valid_ref, gain_ref, wft_ref, pos_ref,
    hg_ref, s1_ref, q_ref, qt_ref, qf_ref, kv_ref, cos_ref, sin_ref, ft,
):
    x = x_ref[...].astype(F32)
    s1 = lax.rsqrt(jnp.mean(x * x, axis=1, keepdims=True) + EPS)
    s1_ref[...] = s1
    h1 = (x * s1 * gain_ref[...]).astype(BF16)
    hg_ref[:, :x.shape[1]] = h1
    hg_ref[:, x.shape[1]:] = (cot_ref[...].astype(F32) * valid_ref[...]).astype(BF16)
    half = lax.broadcasted_iota(jnp.int32, cos_ref.shape, 0).astype(F32)
    angles = pos_ref[...] * jnp.exp(-jnp.log(10000.0) * (2.0 * half) / DH)
    cosine, sine = jnp.cos(angles), jnp.sin(angles)
    cos_ref[...] = cosine
    sin_ref[...] = sine
    ft[:wft_ref.shape[0], :] = mm(wft_ref[...], h1, NT)
    kv_ref[:KA, :] = ft[QF:QF + KA, :].astype(BF16)
    for r in range(2 * RK):
        rows = ft[QF + KA + r * DH:QF + KA + (r + 1) * DH, :]
        if r < RK:
            rows = turn(rows, cosine, sine)
        kv_ref[KA + r * DH:KA + (r + 1) * DH, :] = rows.astype(BF16)
    qf_ref[:QA, :] = ft[:QA, :]
    for r in range(RQ):
        qf_ref[QA + r * DH:QA + (r + 1) * DH, :] = turn(ft[QA + r * DH:QA + (r + 1) * DH, :], cosine, sine)
    for h in range(H):
        total = None
        for r in range(RQ):
            term = qf_ref[r * H + h:r * H + h + 1, :] * qf_ref[QA + r * DH:QA + (r + 1) * DH, :]
            total = term if total is None else total + term
        ft[h * DH:(h + 1) * DH, :] = total / RQ
    qt = ft[:H * DH, :]
    qt_ref[...] = qt.astype(BF16)
    q_ref[...] = qt.T.astype(BF16)


def project(x, cot, valid, gain, w_fact_t, pos):
    tokens, width = x.shape
    nf = w_fact_t.shape[0]
    angles = ((DH // 2, tokens), F32)
    return call(
        factor_kernel,
        [((tokens, 2 * width), BF16), ((tokens, 1), F32), ((tokens, H * DH), BF16),
         ((H * DH, tokens), BF16), ((QF, tokens), F32), ((KF, tokens), BF16), angles, angles],
        [vmem()] * 6,
        (x, cot, valid, gain, w_fact_t, pos),
        [pltpu.VMEM((max(nf, H * DH), tokens), F32)],
        2 * tokens * width * nf, 2 * width * nf, "factors",
    )


def load_factors(pieces, a_rows, b_rows):
    at = 0
    for piece in pieces:
        n = piece.shape[1]
        a_rows[:, at:at + n] = piece[:KA, :].astype(F32)
        b_rows[:, at:at + n] = piece[KA:, :].astype(F32)
        at += n


def expand_pair(pair, side, a_rows, b_rows):
    halves = []
    for sub in range(2):
        total = None
        for r in range(RK):
            a = a_rows[pl.ds((side * RK + r) * H + 2 * pair + sub, 1), :]
            term = a * b_rows[(side * RK + r) * DH:(side * RK + r + 1) * DH, :]
            total = term if total is None else total + term
        halves.append((total * (1.0 / RK)).astype(BF16))
    return jnp.concatenate(halves, axis=0)


def stack_pair(rows):
    lane = lax.broadcasted_iota(jnp.int32, rows.shape, 1)
    zero = jnp.zeros_like(rows)
    return jnp.concatenate([jnp.where(lane < DH, rows, zero), jnp.where(lane < DH, zero, rows)], axis=0)


def pair_lanes(pair):
    return pl.ds(pl.multiple_of(pair * 2 * DH, 2 * DH), 2 * DH)


def attend_kernel(n_pieces, *refs):
    q_ref, bias_ref, wo_ref, x_ref, gain_ref = refs[:5]
    pieces = refs[5:5 + n_pieces]
    h2_ref, mixed, resid_ref, lse_ref, a_rows, b_rows = refs[5 + n_pieces:]
    tokens, width = x_ref.shape
    load_factors(pieces, a_rows, b_rows)
    bias = bias_ref[...]
    bias = jnp.concatenate([bias, bias], axis=0)

    def step(pair, carry):
        keys = expand_pair(pair, 0, a_rows, b_rows)
        values = expand_pair(pair, 1, a_rows, b_rows)
        q = stack_pair(q_ref[:, pair_lanes(pair)])
        scores = mm(q, keys) * SCALE + bias
        top = jnp.max(scores, axis=1, keepdims=True)
        exponent = jnp.exp(scores - top)
        total = jnp.sum(exponent, axis=1, keepdims=True)
        probs = (exponent * (1.0 / total)).astype(BF16)
        lse_ref[pair] = top + jnp.log(total)
        out = mm(probs, values, NT)
        lane = lax.broadcasted_iota(jnp.int32, (tokens, 2 * DH), 1)
        mixed[:, pair_lanes(pair)] = jnp.where(lane < DH, out[:tokens], out[tokens:]).astype(BF16)
        return carry

    lax.fori_loop(0, H // 2, step, 0)
    resid = x_ref[...].astype(F32) + mm(mixed[...], wo_ref[...])
    resid_ref[...] = resid
    s2 = lax.rsqrt(jnp.mean(resid * resid, axis=1, keepdims=True) + EPS)
    h2_ref[...] = (resid * s2 * gain_ref[...]).astype(BF16)


def attend(q, bias, w_out, x, gain, pieces):
    tokens, width = x.shape
    slots = sum(p.shape[1] for p in pieces)
    return call(
        functools.partial(attend_kernel, len(pieces)),
        [((tokens, width), BF16), ((tokens, H * DH), BF16), ((tokens, width), F32), ((H // 2, 2 * tokens, 1), F32)],
        [vmem()] * (5 + len(pieces)),
        (q, bias, w_out, x, gain, *pieces),
        [pltpu.VMEM((KA, slots), F32), pltpu.VMEM((KB, slots), F32)],
        4 * tokens * slots * H * DH, 2 * width * width, "attend",
    )


def attend_back_kernel(n_pieces, *refs):
    q_ref, qt_ref, gm_ref, gmt_ref, lse_ref, bias_ref, qf_ref, cos_ref, sin_ref = refs[:9]
    pieces = refs[9:9 + n_pieces]
    gq_ref, own_ref, send_ref, a_rows, b_rows, ga_rows, gb_rows, gqb_rows = refs[9 + n_pieces:]
    tokens = q_ref.shape[0]
    load_factors(pieces, a_rows, b_rows)
    gb_rows[...] = jnp.zeros_like(gb_rows)
    gqb_rows[...] = jnp.zeros_like(gqb_rows)

    def spread(rows):
        top = lax.broadcasted_iota(jnp.int32, rows.shape, 0) < DH
        zero = jnp.zeros_like(rows)
        return jnp.concatenate([jnp.where(top, rows, zero), jnp.where(top, zero, rows)], axis=1)

    def step(pair, carry):
        keys = expand_pair(pair, 0, a_rows, b_rows)
        values = expand_pair(pair, 1, a_rows, b_rows)
        rows = pl.ds(pl.multiple_of(pair * 2 * DH, 2 * DH), 2 * DH)
        both = (
            stack_pair(q_ref[:, pair_lanes(pair)]), stack_pair(gm_ref[:, pair_lanes(pair)]),
            spread(qt_ref[rows, :]), spread(gmt_ref[rows, :]), lse_ref[pair],
        )
        takes = [slice(0, 2 * tokens)] if keys.shape[1] <= 2048 else [slice(0, tokens), slice(tokens, 2 * tokens)]
        grad_q, grad_k, grad_v = [], None, None
        for take in takes:
            q, g, qt, gt, lse = both[0][take], both[1][take], both[2][:, take], both[3][:, take], both[4][take]
            heads = q.shape[0] // tokens
            scores = mm(q, keys) * SCALE + jnp.concatenate([bias_ref[...]] * heads, axis=0)
            probs = jnp.exp(scores - lse)
            grad_probs = mm(g, values)
            inner = jnp.sum(probs * grad_probs, axis=1, keepdims=True)
            grad_scores = (probs * (grad_probs - inner)).astype(BF16)
            grad_q.append(mm(keys, grad_scores, NT) * SCALE)
            gk, gv = mm(qt, grad_scores) * SCALE, mm(gt, probs.astype(BF16))
            grad_k, grad_v = (gk, gv) if grad_k is None else (grad_k + gk, grad_v + gv)
        grad_q = jnp.concatenate(grad_q, axis=1)
        for sub in range(2):
            head = 2 * pair + sub
            part = slice(sub * DH, (sub + 1) * DH)
            for side, grad in ((0, grad_k[part]), (1, grad_v[part])):
                for r in range(RK):
                    s = side * RK + r
                    row = pl.ds(s * H + head, 1)
                    seg = slice(s * DH, (s + 1) * DH)
                    ga_rows[row, :] = jnp.sum(grad * b_rows[seg, :], axis=0, keepdims=True) * (1.0 / RK)
                    gb_rows[seg, :] += grad * (a_rows[row, :] * (1.0 / RK))
            dq = grad_q[part, sub * tokens:(sub + 1) * tokens]
            for r in range(RQ):
                row = pl.ds(r * H + head, 1)
                seg = slice(QA + r * DH, QA + (r + 1) * DH)
                gq_ref[row, :] = jnp.sum(dq * qf_ref[seg, :], axis=0, keepdims=True) * (1.0 / RQ)
                gqb_rows[r * DH:(r + 1) * DH, :] += dq * (qf_ref[row, :] * (1.0 / RQ))
        return carry

    lax.fori_loop(0, H // 2, step, 0)
    cosine, sine = cos_ref[...], sin_ref[...]
    for r in range(RQ):
        gq_ref[QA + r * DH:QA + (r + 1) * DH, :] = turn_back(gqb_rows[r * DH:(r + 1) * DH, :], cosine, sine)
    at = 0
    for j in range(n_pieces):
        n = pieces[j].shape[1]
        out_ref = send_ref if j % 2 else own_ref
        out_ref[j // 2, :KA, :] = ga_rows[:, at:at + n].astype(BF16)
        out_ref[j // 2, KA:, :] = gb_rows[:, at:at + n].astype(BF16)
        at += n


def attend_back(q, qt, gm, gmt, lse, bias, qf, cosine, sine, pieces):
    tokens = q.shape[0]
    slots = sum(p.shape[1] for p in pieces)
    n = len(pieces)
    return call(
        functools.partial(attend_back_kernel, n),
        [((QF, tokens), F32)] + [((n // 2, KF, slots // n), BF16)] * 2,
        [vmem()] * (9 + n),
        (q, qt, gm, gmt, lse, bias, qf, cosine, sine, *pieces),
        [pltpu.VMEM((KA, slots), F32), pltpu.VMEM((KB, slots), F32), pltpu.VMEM((KA, slots), F32),
         pltpu.VMEM((KB, slots), F32), pltpu.VMEM((RQ * DH, tokens), F32)],
        10 * tokens * slots * H * DH, 4 * tokens * slots, "attend_back",
    )


def hidden_kernel(go_ref, wd_ref, out_ref):
    out_ref[...] = mm(go_ref[...], wd_ref[...], NT)


def hidden_grads(hg, w_down):
    tokens, width = hg.shape[0], hg.shape[1] // 2
    ff = w_down.shape[0]
    chunk = max(c for c in range(128, ff + 1, 128) if ff % c == 0 and c <= ff // 2)
    return pl.pallas_call(
        hidden_kernel,
        grid=(ff // chunk,),
        in_specs=[pl.BlockSpec((tokens, width), lambda j: (0, 1)), pl.BlockSpec((chunk, width), lambda j: (j, 0))],
        out_specs=pl.BlockSpec((tokens, chunk), lambda j: (0, j)),
        out_shape=jax.ShapeDtypeStruct((tokens, ff), F32),
        compiler_params=pltpu.CompilerParams(vmem_limit_bytes=VMEM_BYTES),
        cost_estimate=pl.CostEstimate(
            flops=2 * tokens * width * ff, transcendentals=0, bytes_accessed=2 * width * ff + 4 * tokens * ff
        ),
        name="hidden_grads",
    )(hg, w_down)


def column_kernel(place_ref, wg_ref, wu_ref, wgt_ref, wut_ref, window, turned, sems):
    span = window.shape[2]
    part, width = wgt_ref.shape
    at = (place_ref[0] * 2 + place_ref[1]) * part
    start = jnp.minimum(at // 128 * 128, wg_ref.shape[1] - span)
    cols = pl.ds(pl.multiple_of(start, 128), span)
    copies = [
        pltpu.make_async_copy(ref.at[:, cols], window.at[i], sems.at[i]) for i, ref in enumerate((wg_ref, wu_ref))
    ]
    for copy in copies:
        copy.start()
    for i, out_ref in enumerate((wgt_ref, wut_ref)):
        copies[i].wait()
        turned[...] = window[i].T
        out_ref[...] = turned[pl.ds(pl.multiple_of(at - start, 32), part), :]


def own_columns(place, w_gate, w_up, part):
    width, ff = w_gate.shape
    span = min(ff, -(-part // 128) * 128 + 128)
    return call(
        column_kernel,
        [((part, width), BF16)] * 2,
        [smem(), hbm(), hbm()],
        (place, w_gate, w_up),
        [pltpu.VMEM((2, width, span), BF16), pltpu.VMEM((span, width), BF16), pltpu.SemaphoreType.DMA((2,))],
        0, 4 * width * span, "own_columns",
    )


def ffn_kernel(
    place_ref, h2_ref, hg_ref, gh_ref, resid_ref, gain_ref, mixed_ref, wg_hbm, wu_hbm, wd_hbm, wo_hbm, *refs,
):
    out_ref, gain_grad_ref, gres_ref, gm_ref, gmt_ref = refs[:5]
    mgx_refs, (branch, grad_h2, gb_cols, wg, wu, wd, wo, sems) = refs[5:-8], refs[-8:]
    width, ff = wg.shape
    n_chunks = sems.shape[1]
    chunk = ff // n_chunks
    copies = []
    for j in range(n_chunks):
        part = pl.ds(j * chunk, chunk)
        copies.append([
            pltpu.make_async_copy(wg_hbm.at[:, part], wg.at[:, part], sems.at[0, j]),
            pltpu.make_async_copy(wu_hbm.at[:, part], wu.at[:, part], sems.at[1, j]),
            pltpu.make_async_copy(wd_hbm.at[part, :], wd.at[part, :], sems.at[2, j]),
        ])
    wo_copy = pltpu.make_async_copy(wo_hbm, wo, sems.at[3, 0])
    for group in copies:
        for copy in group:
            copy.start()
    wo_copy.start()
    h2 = h2_ref[...]
    for j in range(n_chunks):
        for copy in copies[j]:
            copy.wait()
        part = slice(j * chunk, (j + 1) * chunk)
        gate, up = mm(h2, wg[:, part]), mm(h2, wu[:, part])
        grad_hidden = gh_ref[:, part]
        sig = jax.nn.sigmoid(gate)
        silu = gate * sig
        hidden = (silu * up).astype(BF16)
        grad_gate = (grad_hidden * up * sig * (1.0 + gate * (1.0 - sig))).astype(BF16)
        grad_up = (grad_hidden * silu).astype(BF16)
        more_branch = mm(hidden, wd[part, :])
        more_grad = mm(grad_gate, wg[:, part], NT) + mm(grad_up, wu[:, part], NT)
        if j == 0:
            branch[...] = more_branch
            grad_h2[...] = more_grad
        else:
            branch[...] += more_branch
            grad_h2[...] += more_grad
    resid = resid_ref[...]
    out_ref[...] = (resid + branch[...]).astype(BF16)
    s2 = lax.rsqrt(jnp.mean(resid * resid, axis=1, keepdims=True) + EPS)
    n2 = resid * s2
    gh = grad_h2[...]
    gain_grad_ref[...] = jnp.sum(gh * n2, axis=0, keepdims=True)
    g2 = gh * gain_ref[...]
    gres = hg_ref[:, width:].astype(F32) + s2 * (g2 - n2 * jnp.mean(g2 * n2, axis=1, keepdims=True))
    gres_ref[...] = gres
    gb = gres.astype(BF16)
    gb_cols[...] = gb
    wo_copy.wait()
    gm = mm(gb, wo[...], NT)
    gm_ref[...] = gm.astype(BF16)
    gmt_ref[...] = gm.T.astype(BF16)
    for k, mgx_ref in enumerate(mgx_refs):
        cols = mgx_ref.shape[1] - width
        mgx_ref[:, :width] = mixed_ref[...]
        mgx_ref[:, width:] = gb_cols[:, pl.ds(pl.multiple_of((place_ref[0] ^ k) * cols, cols), cols)]


def feed_forward(place, h2, hg, gh, w_gate, w_up, w_down, resid, gain, w_out, mixed, n_rows):
    tokens, width = resid.shape
    ff = w_gate.shape[1]
    chunk = 256 if ff % 256 == 0 else 128
    return call(
        ffn_kernel,
        [((tokens, width), BF16), ((1, width), F32), ((tokens, width), F32), ((tokens, width), BF16),
         ((width, tokens), BF16)] + [((tokens, width + width // n_rows), BF16)] * n_rows,
        [smem()] + [vmem()] * 6 + [hbm()] * 4,
        (place, h2, hg, gh, resid, gain, mixed, w_gate, w_up, w_down, w_out),
        [pltpu.VMEM((tokens, width), F32), pltpu.VMEM((tokens, width), F32), pltpu.VMEM((tokens, width), BF16),
         pltpu.VMEM((width, ff), BF16), pltpu.VMEM((width, ff), BF16), pltpu.VMEM((ff, width), BF16),
         pltpu.VMEM((width, width), BF16), pltpu.SemaphoreType.DMA((4, ff // chunk))],
        10 * tokens * width * ff, 6 * width * ff, "feed_forward",
    )


def weight_kernel(n_pieces, ordered, place_ref, wgt_ref, wut_ref, wd_ref, *refs):
    h2_pieces, hg_pieces = refs[:n_pieces], refs[n_pieces:2 * n_pieces]
    up_keep, up_send, down_keep, down_send, h2s, gos, wds, sems = refs[2 * n_pieces:]
    tokens, width = h2_pieces[0].shape
    ff = wgt_ref.shape[0]
    groups = [[], []]
    for j in range(n_pieces):
        rows = pl.ds(j * tokens, tokens)
        groups[0].append(pltpu.make_async_copy(h2_pieces[j], h2s.at[rows, :], sems.at[0, j]))
        groups[1].append(pltpu.make_async_copy(
            hg_pieces[j].at[:, pl.ds(width, width)], gos.at[rows, :], sems.at[1, j]))
    at = pl.multiple_of((place_ref[0] * 2 + place_ref[1]) * ff, 32)
    groups[1].append(pltpu.make_async_copy(wd_ref.at[pl.ds(at, ff), :], wds, sems.at[1, n_pieces]))
    for group in groups:
        for copy in group:
            copy.start()
    for copy in groups[0]:
        copy.wait()
    gate = mm(wgt_ref[...], h2s[...], NT)
    up = mm(wut_ref[...], h2s[...], NT)
    for copy in groups[1]:
        copy.wait()
    grad_hidden = mm(wds[...], gos[...], NT)
    sig = jax.nn.sigmoid(gate)
    silu = gate * sig
    hidden = (silu * up).astype(BF16)
    grad_gate = (grad_hidden * up * sig * (1.0 + gate * (1.0 - sig))).astype(BF16)
    grad_up = (grad_hidden * silu).astype(BF16)
    kept = up_keep.shape[0]
    n_z = 2 * kept
    cols = width // n_z
    half = cols // 2
    for slot, k in enumerate(halving_order(n_z)):
        up_ref, down_ref, i = (up_keep, down_keep, slot) if slot < kept else (up_send, down_send, slot - kept)
        if ordered:
            z, core = place_ref[2] ^ k, place_ref[1]
            first = pl.ds(pl.multiple_of(z * cols + core * half, half), half)
            other = pl.ds(pl.multiple_of(z * cols + (1 - core) * half, half), half)
            straight = pl.ds(pl.multiple_of(z * cols, cols), cols)
            h2c = jnp.concatenate([h2s[:, first], h2s[:, other]], axis=1)
        else:
            straight = slice(slot * cols, (slot + 1) * cols)
            h2c = h2s[:, straight]
        up_ref[i, :ff, :] = mm(grad_gate, h2c).astype(BF16)
        up_ref[i, ff:, :] = mm(grad_up, h2c).astype(BF16)
        down_ref[i] = mm(hidden, gos[:, straight]).astype(BF16)


def halving_order(n):
    order = [0]
    k = n // 2
    while k >= 1:
        order = order + [o | k for o in order]
        k //= 2
    return order


def halve(keep, got, axis, k):
    while True:
        total = keep.astype(F32) + got.astype(F32)
        n = total.shape[0]
        if n == 1:
            return total[0]
        k *= 2
        keep, got = total[:n // 2], swap(total[n // 2:].astype(BF16), axis, k)


def weight_grads(place, wgt, wut, w_down, h2_pieces, hg_pieces, n_z, ordered):
    n = len(h2_pieces)
    tokens = h2_pieces[0].shape[0]
    ff, width = wgt.shape
    total = n * tokens
    up, down = ((n_z // 2, 2 * ff, width // n_z), BF16), ((n_z // 2, ff, width // n_z), BF16)
    return call(
        functools.partial(weight_kernel, n, ordered),
        [up, up, down, down],
        [smem(), vmem(), vmem(), hbm()] + [hbm()] * (2 * n),
        (place, wgt, wut, w_down, *h2_pieces, *hg_pieces),
        [pltpu.VMEM((total, width), BF16), pltpu.VMEM((total, width), BF16), pltpu.VMEM((ff, width), BF16),
         pltpu.SemaphoreType.DMA((2, n + 1))],
        12 * total * width * ff, 6 * width * ff + 4 * total * width, "weight_grads",
    )


def own_cut(ordered, place_ref, k, cols):
    if not ordered:
        return slice(k * cols, (k + 1) * cols)
    return pl.ds(pl.multiple_of(((place_ref[2] ^ k) * 2 + place_ref[1]) * cols, cols), cols)


def out_kernel(n_pieces, n_out, ordered, place_ref, mine_ref, other_ref, *refs):
    hg_pieces = refs[:n_pieces]
    out_refs, (h1_ref, wide, thin, sems) = refs[n_pieces:-4], refs[-4:]
    cols = out_refs[0].shape[1]
    n_rows, tokens, both = mine_ref.shape
    part = thin.shape[1]
    copies = []
    for j, piece in enumerate(hg_pieces):
        for k in range(n_out):
            copies.append(pltpu.make_async_copy(
                piece.at[:, own_cut(ordered, place_ref, k, cols)],
                h1_ref.at[pl.ds(j * tokens, tokens), pl.ds(k * cols, cols)], sems.at[j, k]))
    if ordered:
        for copy in copies:
            copy.start()
    for i, ref in enumerate((mine_ref, other_ref)):
        for j in range(n_rows):
            rows = slice((i * n_rows + j) * tokens, (i * n_rows + j + 1) * tokens)
            thin[rows, :] = ref[j, :, both - part:]
            for k in range(n_out):
                wide[rows, k * cols:(k + 1) * cols] = ref[j, :, own_cut(ordered, place_ref, k, cols)]
    full = mm(thin[...].T, wide[...]).astype(BF16)
    for k in range(n_out):
        out_refs[k][...] = full[:, k * cols:(k + 1) * cols]
    if ordered:
        for copy in copies:
            copy.wait()


def out_grads(place, mine, other, hg_pieces, width, n_out, cols, ordered):
    n = len(hg_pieces)
    n_rows, tokens, both = mine.shape
    part = both - width
    total = 2 * n_rows * tokens
    *parts, h1_slab = call(
        functools.partial(out_kernel, n, n_out, ordered),
        [((part, cols), BF16)] * n_out + [((total, n_out * cols), BF16)],
        [smem(), vmem(), vmem()] + [hbm()] * n,
        (place, mine, other, *hg_pieces),
        [pltpu.VMEM((total, n_out * cols), BF16), pltpu.VMEM((total, part), BF16), pltpu.SemaphoreType.DMA((n, n_out))],
        2 * total * part * n_out * cols, 4 * total * n_out * cols, "out_grads",
    )
    if not ordered:
        h1_slab = jnp.concatenate([piece[:, :width] for piece in hg_pieces], axis=0)
    return parts, h1_slab


def fact_kernel(n_out, head, ordered, h1_ref, mine_ref, other_ref, *refs):
    carried, out_refs, thin = refs[:n_out], refs[n_out:-1], refs[-1]
    cols = out_refs[0].shape[1]
    tokens = mine_ref.shape[2]
    rows = mine_ref.shape[1]
    parts = [ref[j] for ref in (mine_ref, other_ref) for j in range(ref.shape[0])]
    for j, part in enumerate(parts):
        thin[:, j * tokens:(j + 1) * tokens] = part[head:, :]
    full = mm(thin[...], h1_ref[...]).astype(BF16)
    for k in range(n_out):
        out_refs[k][head:rows, :] = full[:, k * cols:(k + 1) * cols]
        out_refs[k][rows:, :] = carried[k][...]
    if ordered:
        half = head // 2
        gains = tree_sum([p[:half].astype(F32) + p[half:head].astype(F32) for p in parts])
        high = gains.astype(BF16)
        low = (gains - high.astype(F32)).astype(BF16)
        for k in range(n_out):
            out_refs[k][:half, :] = high
            out_refs[k][half:head, :] = low


def fact_grads(h1_slab, mine, other, carried, head, ordered):
    n_rows, rows, tokens = mine.shape
    n_out = len(carried)
    part, cols = carried[0].shape
    total = 2 * n_rows * tokens
    return call(
        functools.partial(fact_kernel, n_out, head, ordered),
        [((rows + part, cols), BF16)] * n_out,
        [vmem()] * (3 + n_out),
        (h1_slab, mine, other, *carried),
        [pltpu.VMEM((rows - head, total), BF16)],
        2 * total * rows * n_out * cols, 2 * total * n_out * cols, "fact_grads",
    )


def input_kernel(
    n_parts, place_ref, gq_ref, *refs,
):
    parts = refs[:n_parts]
    wft_ref, x_ref, s1_ref, gain_ref, gres_ref, gain_two_ref, cos_ref, sin_ref = refs[n_parts:n_parts + 8]
    gin_ref, *gfx_refs = refs[n_parts + 8:-2]
    gf, gains = refs[-2:]
    cosine, sine = cos_ref[...], sin_ref[...]
    kv = tree_sum([part[...].astype(F32) for part in parts])
    gf[:QF, :] = gq_ref[...]
    gf[QF:QF + KA, :] = kv[:KA]
    for r in range(2 * RK):
        rows = kv[KA + r * DH:KA + (r + 1) * DH]
        if r < RK:
            rows = turn_back(rows, cosine, sine)
        gf[QF + KA + r * DH:QF + KA + (r + 1) * DH, :] = rows
    grad = gf[...].T.astype(BF16)
    grad_h1 = mm(grad, wft_ref[...])
    s1 = s1_ref[...]
    n1 = x_ref[...].astype(F32) * s1
    gain_one = jnp.sum(grad_h1 * n1, axis=0, keepdims=True)
    gain_two = gain_two_ref[...]
    g1 = grad_h1 * gain_ref[...]
    gin_ref[...] = gres_ref[...] + s1 * (g1 - n1 * jnp.mean(g1 * n1, axis=1, keepdims=True))
    tokens, width = x_ref.shape
    half = gains.shape[0]
    for i in range(half // 2):
        gains[i:i + 1, :] = gain_one[:, i * tokens:(i + 1) * tokens]
        gains[half // 2 + i:half // 2 + i + 1, :] = gain_two[:, i * tokens:(i + 1) * tokens]
    high = gains[...].astype(BF16)
    low = (gains[...] - high.astype(F32)).astype(BF16)
    for k, gfx_ref in enumerate(gfx_refs):
        part = gfx_ref.shape[0] - 2 * half
        gfx_ref[:half, :] = high
        gfx_ref[half:2 * half, :] = low
        gfx_ref[2 * half:, :] = gf[pl.ds(pl.multiple_of((place_ref[0] ^ k) * part, 8), part), :].astype(BF16)


def input_grads(place, gq, parts, w_fact_t, x, s1, gain, gres, gain_two, cosine, sine, n_rows):
    tokens, width = x.shape
    nf = w_fact_t.shape[0]
    half = 2 * width // tokens
    return call(
        functools.partial(input_kernel, len(parts)),
        [((tokens, width), F32)] + [((2 * half + nf // n_rows, tokens), BF16)] * n_rows,
        [smem()] + [vmem()] * (9 + len(parts)),
        (place, gq, *parts, w_fact_t, x, s1, gain, gres, gain_two, cosine, sine),
        [pltpu.VMEM((nf, tokens), F32), pltpu.VMEM((half, tokens), F32)],
        2 * tokens * width * nf, 2 * width * nf, "input_grads",
    )


def after(values, *others):
    flat, tree = jax.tree.flatten((values, others))
    return jax.tree.unflatten(tree, lax.optimization_barrier(flat))[0]


def body(inputs, lengths, gain_attn, w_fact, w_out, gain_ffn, w_gate, w_up, w_down, cotangent):
    seqs, local_len, width = inputs.shape
    tokens = seqs * local_len
    n_rows, n_ctx = lax.axis_size(ROW), lax.axis_size(CTX)
    n_z = n_ctx // 2
    row, ctx = lax.axis_index(ROW), lax.axis_index(CTX)
    z, core = ctx // 2, ctx % 2
    slots_all = local_len * n_ctx
    block_len = local_len // 2
    ff = w_gate.shape[1]
    ff_part = ff // (2 * n_rows)
    own_cols = width // n_ctx
    per = n_ctx // (2 * n_rows)
    ordered = own_cols % 128 == 0 and per == 1 and tokens == 128
    n_out = n_z if ordered else n_ctx
    place = jnp.stack([row, core, z]).astype(jnp.int32)

    within = jnp.arange(local_len, dtype=jnp.int32)
    local_pos = jnp.tile(slot_position(ctx * local_len + within, block_len, slots_all), seqs)
    local_seq = jnp.repeat(jnp.arange(seqs, dtype=jnp.int32), local_len)
    valid = (local_pos < jnp.repeat(lengths, local_len)).astype(F32)[:, None]
    piece_of = jnp.arange(n_ctx, dtype=jnp.int32) ^ ctx
    key_pos = jnp.tile(
        slot_position(piece_of[:, None] * local_len + within[None, :], block_len, slots_all)[:, None, :], (1, seqs, 1)
    ).reshape(-1)
    key_seq = jnp.tile(local_seq, n_ctx)
    key_len = jnp.tile(jnp.repeat(lengths, local_len), n_ctx)
    allowed = (
        (key_pos[None, :] <= local_pos[:, None])
        & (key_pos < key_len)[None, :]
        & (key_seq[None, :] == local_seq[:, None])
    )
    bias = jnp.where(allowed, 0.0, -1e30).astype(F32)

    x = inputs.reshape(tokens, width)
    gain_one, gain_two = gain_attn[None, :], gain_ffn[None, :]
    w_fact_t = w_fact.T

    def others(values, axis, n):
        return [swap(values[k], axis, k) for k in range(1, n)]

    def along_core(values):
        return list(values) + [swap(value, "core", 1) for value in values]

    def both_cores(values):
        mine = jnp.stack(values)
        return [mine, swap(mine, "core", 1)]

    hg, s1, q, qt, qf, kv, cosine, sine = project(
        x, cotangent.reshape(tokens, width), valid, gain_one, w_fact_t, local_pos.astype(F32)[None, :]
    )
    kv_z = [kv] + others([kv] * n_z, "z", n_z)
    gh = hidden_grads(hg, w_down)
    kv_z = after(kv_z, gh)
    kv_pieces = []
    for part in kv_z:
        kv_pieces += [part, swap(part, "core", 1)]
    wgt, wut = own_columns(place, w_gate, w_up, ff_part)
    hg_same = [hg] + others([hg] * n_rows, ROW, n_rows)
    h2, mixed, resid, lse = attend(after(q, wgt), bias, w_out, x, gain_two, kv_pieces)
    h2_same = [h2] + others([h2] * n_rows, ROW, n_rows)
    hg_pieces = along_core(after(hg_same, h2))
    block_out, gain_two_part, gres, gm, gmt, *mgx = feed_forward(
        place, h2, after(hg, hg_same), gh, w_gate, w_up, w_down, resid, gain_two, w_out, mixed, n_rows
    )
    h2_pieces = along_core(after(h2_same, gm))
    up_keep, up_send, down_keep, down_send = weight_grads(
        place, wgt, wut, w_down, h2_pieces, hg_pieces, n_z, ordered
    )
    if not ordered:
        turns = jnp.asarray(halving_order(n_z), jnp.int32) ^ z
        cores = jnp.arange(2, dtype=jnp.int32) ^ core
        up = jnp.take(jnp.concatenate([up_keep, up_send]), turns, axis=0)
        up = jnp.take(up.reshape(n_z, 2 * ff_part, 2, own_cols), cores, axis=2).reshape(up.shape)
        down = jnp.concatenate([down_keep, down_send]).transpose(1, 0, 2)
        down = down.reshape(per, ff_part // per, n_rows, width // n_rows).transpose(0, 2, 1, 3)
        down = jnp.take(down.reshape(n_z, ff_part // per, width // n_rows), turns, axis=0)
        up_keep, up_send, down_keep, down_send = up[:n_z // 2], up[n_z // 2:], down[:n_z // 2], down[n_z // 2:]

    up_got, down_got = swap(up_send, "z", 1), swap(down_send, "z", 1)
    mg_same = [mgx[0]] + others(after(mgx, up_send), ROW, n_rows)
    gq, gkv_own, gkv_send = attend_back(q, qt, after(gm, up_send), gmt, lse, bias, qf, cosine, sine, kv_pieces)
    gkv_send, mg_same, up_got, down_got = lax.optimization_barrier((gkv_send, mg_same, up_got, down_got))
    gkv_got = swap(gkv_send, "core", 1)
    gkv_z = [(gkv_own[k].astype(F32) + gkv_got[k].astype(F32)).astype(BF16) for k in range(n_z)]
    kv_parts = [gkv_z[0]] + others(gkv_z, "z", n_z)

    def own_blocks(parts):
        if ordered:
            return parts
        parts = jnp.take(jnp.stack(parts), (jnp.arange(n_z, dtype=jnp.int32) ^ z) * 2 + core, axis=0)
        return [parts[k] for k in range(n_z)]

    out_parts, h1_slab = out_grads(place, *both_cores(mg_same), hg_pieces, width, n_out, own_cols, ordered)
    gq = after(gq, out_parts)
    up_keep, down_keep = after((up_keep, down_keep), gkv_z)
    grad_inputs, *gfx = input_grads(
        place, gq, kv_parts, w_fact_t, x, s1, gain_one, gres, gain_two_part, cosine, sine, n_rows
    )
    up_total = halve(up_keep, up_got, "z", 1)
    down_total = halve(down_keep, down_got, "z", 1)
    head = gfx[0].shape[0] - w_fact.shape[1] // n_rows
    gf_all = both_cores([gfx[0]] + others(gfx, ROW, n_rows))
    tail_parts = own_blocks(fact_grads(h1_slab, *gf_all, out_parts, head, ordered))
    tail_got = others(tail_parts, "z", n_z)

    up_total, down_total = after((up_total, down_total), tail_parts)
    mine, other = up_total[:, :own_cols], swap(up_total[:, own_cols:].astype(BF16), "core", 1).astype(F32)
    first = jnp.where(core == 0, mine, other)
    second = jnp.where(core == 0, other, mine)
    grad_gate = jnp.concatenate([first[:ff_part], second[:ff_part]], axis=0).T
    grad_up = jnp.concatenate([first[ff_part:], second[ff_part:]], axis=0).T

    moves = []
    for r in range(n_rows):
        for c in range(2):
            for p in range(n_z):
                b, s = p // n_rows, p % n_rows
                moves.append((r * n_ctx + 2 * p + c, s * n_ctx + (r * 2 + c) * per + b))
    grad_down = lax.ppermute(down_total.astype(BF16), ROW + CTX, moves).astype(F32)

    tail_got = after(tail_got, grad_gate, grad_up)
    tail = tree_sum([part.astype(F32) for part in [tail_parts[0]] + tail_got])
    rows = gfx[0].shape[0]
    grad_fact, grad_out = tail[head:rows].T, tail[rows:].T
    if ordered:
        gains = (tail[:head // 2] + tail[head // 2:head]).reshape(2, width)
    else:
        sums = gfx[0][:head // 2].astype(F32) + gfx[0][head // 2:head].astype(F32)
        gains = lax.psum(sums, ROW + CTX).reshape(2, width)

    return (
        block_out.reshape(inputs.shape),
        grad_inputs.reshape(inputs.shape),
        gains[0],
        grad_fact,
        grad_out,
        gains[1],
        grad_gate,
        grad_up,
        grad_down,
    )


def solution(mesh):
    n_rows, n_ctx = mesh.shape["row"], mesh.shape["ctx"]
    fine = Mesh(mesh.devices.reshape(n_rows // 2, 2, n_ctx // 2, 2), ROW + CTX)
    placed = (P(ROW, CTX, None), P(ROW), P(), P(), P(), P(), P(), P(), P(), P(ROW, CTX, None))
    return jax.shard_map(
        body,
        mesh=fine,
        in_specs=placed,
        out_specs=(
            P(ROW, CTX, None), P(ROW, CTX, None), P(), P(CTX, ROW), P(CTX, ROW), P(), P(CTX, ROW), P(CTX, ROW),
            P(CTX, ROW),
        ),
        check_vma=False,
    )
```

```python
import functools

import jax
import jax.numpy as jnp
from jax import lax
from jax.experimental import pallas as pl
from jax.experimental.pallas import tpu as pltpu
from jax.sharding import Mesh
from jax.sharding import PartitionSpec as P

H = 16
DH = 64
RQ = 6
RK = 2
EPS = 1e-06
QA = RQ * H
QF = RQ * (H + DH)
KA = 2 * RK * H
KB = 2 * RK * DH
KF = KA + KB
SCALE = DH ** (-0.5)
F32 = jnp.float32
BF16 = jnp.bfloat16
VMEM_BYTES = 56 * 1024 * 1024

NN = (((1,), (0,)), ((), ()))
NT = (((1,), (1,)), ((), ()))


def mm(a, b, dims=NN):
    return lax.dot_general(a, b, dims, preferred_element_type=F32)


def vmem():
    return pl.BlockSpec(memory_space=pltpu.VMEM)


def smem():
    return pl.BlockSpec(memory_space=pltpu.SMEM)


def hbm():
    return pl.BlockSpec(memory_space=pltpu.HBM)


def call(kernel, outs, ins, args, scratch=(), flops=0, moved=0, name=None):
    return pl.pallas_call(
        kernel,
        out_shape=[jax.ShapeDtypeStruct(s, d) for s, d in outs],
        in_specs=ins,
        out_specs=[vmem() for _ in outs],
        scratch_shapes=list(scratch),
        compiler_params=pltpu.CompilerParams(vmem_limit_bytes=VMEM_BYTES),
        cost_estimate=pl.CostEstimate(flops=flops, transcendentals=0, bytes_accessed=moved),
        name=name,
    )(*args)


def slot_position(index, block_len, slots_all):
    block_id = index // (2 * block_len)
    within = index % (2 * block_len)
    return jnp.where(
        within < block_len,
        block_id * block_len + within,
        (slots_all // block_len - 1 - block_id) * block_len + within - block_len,
    )


def turn(rows, cosine, sine):
    half = DH // 2
    upper, lower = rows[:half], rows[half:]
    return jnp.concatenate([upper * cosine - lower * sine, lower * cosine + upper * sine], axis=0)


def turn_back(rows, cosine, sine):
    half = DH // 2
    upper, lower = rows[:half], rows[half:]
    return jnp.concatenate([upper * cosine + lower * sine, lower * cosine - upper * sine], axis=0)


ROW = ("r1", "r0")
CTX = ("z", "core")
GROUP = ("r1", "r0", "core")


def swap(value, axis, k):
    size = lax.axis_size(axis)
    return lax.ppermute(value, axis, [(j, j ^ k) for j in range(size)])


def tree_sum(parts):
    parts = list(parts)
    while len(parts) > 1:
        parts = [parts[i] + parts[i + 1] for i in range(0, len(parts), 2)]
    return parts[0]


def factor_kernel(
    x_ref, cot_ref, valid_ref, gain_ref, wft_ref, pos_ref,
    hg_ref, s1_ref, q_ref, qt_ref, qf_ref, kv_ref, cos_ref, sin_ref, ft,
):
    x = x_ref[...].astype(F32)
    s1 = lax.rsqrt(jnp.mean(x * x, axis=1, keepdims=True) + EPS)
    s1_ref[...] = s1
    h1 = (x * s1 * gain_ref[...]).astype(BF16)
    hg_ref[:, :x.shape[1]] = h1
    hg_ref[:, x.shape[1]:] = (cot_ref[...].astype(F32) * valid_ref[...]).astype(BF16)
    half = lax.broadcasted_iota(jnp.int32, cos_ref.shape, 0).astype(F32)
    angles = pos_ref[...] * jnp.exp(-jnp.log(10000.0) * (2.0 * half) / DH)
    cosine, sine = jnp.cos(angles), jnp.sin(angles)
    cos_ref[...] = cosine
    sin_ref[...] = sine
    ft[:wft_ref.shape[0], :] = mm(wft_ref[...], h1, NT)
    kv_ref[:KA, :] = ft[QF:QF + KA, :].astype(BF16)
    for r in range(2 * RK):
        rows = ft[QF + KA + r * DH:QF + KA + (r + 1) * DH, :]
        if r < RK:
            rows = turn(rows, cosine, sine)
        kv_ref[KA + r * DH:KA + (r + 1) * DH, :] = rows.astype(BF16)
    qf_ref[:QA, :] = ft[:QA, :]
    for r in range(RQ):
        qf_ref[QA + r * DH:QA + (r + 1) * DH, :] = turn(ft[QA + r * DH:QA + (r + 1) * DH, :], cosine, sine)
    for h in range(H):
        total = None
        for r in range(RQ):
            term = qf_ref[r * H + h:r * H + h + 1, :] * qf_ref[QA + r * DH:QA + (r + 1) * DH, :]
            total = term if total is None else total + term
        ft[h * DH:(h + 1) * DH, :] = total / RQ
    qt = ft[:H * DH, :]
    qt_ref[...] = qt.astype(BF16)
    q_ref[...] = qt.T.astype(BF16)


def project(x, cot, valid, gain, w_fact_t, pos):
    tokens, width = x.shape
    nf = w_fact_t.shape[0]
    angles = ((DH // 2, tokens), F32)
    return call(
        factor_kernel,
        [((tokens, 2 * width), BF16), ((tokens, 1), F32), ((tokens, H * DH), BF16),
         ((H * DH, tokens), BF16), ((QF, tokens), F32), ((KF, tokens), BF16), angles, angles],
        [vmem()] * 6,
        (x, cot, valid, gain, w_fact_t, pos),
        [pltpu.VMEM((max(nf, H * DH), tokens), F32)],
        2 * tokens * width * nf, 2 * width * nf, "factors",
    )


def load_factors(pieces, a_rows, b_rows):
    at = 0
    for piece in pieces:
        n = piece.shape[1]
        a_rows[:, at:at + n] = piece[:KA, :].astype(F32)
        b_rows[:, at:at + n] = piece[KA:, :].astype(F32)
        at += n


def expand_pair(pair, side, a_rows, b_rows):
    halves = []
    for sub in range(2):
        total = None
        for r in range(RK):
            a = a_rows[pl.ds((side * RK + r) * H + 2 * pair + sub, 1), :]
            term = a * b_rows[(side * RK + r) * DH:(side * RK + r + 1) * DH, :]
            total = term if total is None else total + term
        halves.append((total * (1.0 / RK)).astype(BF16))
    return jnp.concatenate(halves, axis=0)


def stack_pair(rows):
    lane = lax.broadcasted_iota(jnp.int32, rows.shape, 1)
    zero = jnp.zeros_like(rows)
    return jnp.concatenate([jnp.where(lane < DH, rows, zero), jnp.where(lane < DH, zero, rows)], axis=0)


def pair_lanes(pair):
    return pl.ds(pl.multiple_of(pair * 2 * DH, 2 * DH), 2 * DH)


def attend_kernel(n_pieces, *refs):
    q_ref, bias_ref, wo_ref, x_ref, gain_ref = refs[:5]
    pieces = refs[5:5 + n_pieces]
    h2_ref, mixed, resid_ref, lse_ref, a_rows, b_rows = refs[5 + n_pieces:]
    tokens, width = x_ref.shape
    load_factors(pieces, a_rows, b_rows)
    bias = bias_ref[...]
    bias = jnp.concatenate([bias, bias], axis=0)

    def step(pair, carry):
        keys = expand_pair(pair, 0, a_rows, b_rows)
        values = expand_pair(pair, 1, a_rows, b_rows)
        q = stack_pair(q_ref[:, pair_lanes(pair)])
        scores = mm(q, keys) * SCALE + bias
        top = jnp.max(scores, axis=1, keepdims=True)
        exponent = jnp.exp(scores - top)
        total = jnp.sum(exponent, axis=1, keepdims=True)
        probs = (exponent * (1.0 / total)).astype(BF16)
        lse_ref[pair] = top + jnp.log(total)
        out = mm(probs, values, NT)
        lane = lax.broadcasted_iota(jnp.int32, (tokens, 2 * DH), 1)
        mixed[:, pair_lanes(pair)] = jnp.where(lane < DH, out[:tokens], out[tokens:]).astype(BF16)
        return carry

    lax.fori_loop(0, H // 2, step, 0)
    resid = x_ref[...].astype(F32) + mm(mixed[...], wo_ref[...])
    resid_ref[...] = resid
    s2 = lax.rsqrt(jnp.mean(resid * resid, axis=1, keepdims=True) + EPS)
    h2_ref[...] = (resid * s2 * gain_ref[...]).astype(BF16)


def attend(q, bias, w_out, x, gain, pieces):
    tokens, width = x.shape
    slots = sum(p.shape[1] for p in pieces)
    return call(
        functools.partial(attend_kernel, len(pieces)),
        [((tokens, width), BF16), ((tokens, H * DH), BF16), ((tokens, width), F32), ((H // 2, 2 * tokens, 1), F32)],
        [vmem()] * (5 + len(pieces)),
        (q, bias, w_out, x, gain, *pieces),
        [pltpu.VMEM((KA, slots), F32), pltpu.VMEM((KB, slots), F32)],
        4 * tokens * slots * H * DH, 2 * width * width, "attend",
    )


def attend_back_kernel(n_pieces, *refs):
    q_ref, qt_ref, gm_ref, gmt_ref, lse_ref, bias_ref, qf_ref, cos_ref, sin_ref = refs[:9]
    pieces = refs[9:9 + n_pieces]
    gq_ref, own_ref, send_ref, a_rows, b_rows, ga_rows, gb_rows, gqb_rows = refs[9 + n_pieces:]
    tokens = q_ref.shape[0]
    load_factors(pieces, a_rows, b_rows)
    gb_rows[...] = jnp.zeros_like(gb_rows)
    gqb_rows[...] = jnp.zeros_like(gqb_rows)

    def spread(rows):
        top = lax.broadcasted_iota(jnp.int32, rows.shape, 0) < DH
        zero = jnp.zeros_like(rows)
        return jnp.concatenate([jnp.where(top, rows, zero), jnp.where(top, zero, rows)], axis=1)

    def step(pair, carry):
        keys = expand_pair(pair, 0, a_rows, b_rows)
        values = expand_pair(pair, 1, a_rows, b_rows)
        rows = pl.ds(pl.multiple_of(pair * 2 * DH, 2 * DH), 2 * DH)
        both = (
            stack_pair(q_ref[:, pair_lanes(pair)]), stack_pair(gm_ref[:, pair_lanes(pair)]),
            spread(qt_ref[rows, :]), spread(gmt_ref[rows, :]), lse_ref[pair],
        )
        takes = [slice(0, 2 * tokens)] if keys.shape[1] <= 2048 else [slice(0, tokens), slice(tokens, 2 * tokens)]
        grad_q, grad_k, grad_v = [], None, None
        for take in takes:
            q, g, qt, gt, lse = both[0][take], both[1][take], both[2][:, take], both[3][:, take], both[4][take]
            heads = q.shape[0] // tokens
            scores = mm(q, keys) * SCALE + jnp.concatenate([bias_ref[...]] * heads, axis=0)
            probs = jnp.exp(scores - lse)
            grad_probs = mm(g, values)
            inner = jnp.sum(probs * grad_probs, axis=1, keepdims=True)
            grad_scores = (probs * (grad_probs - inner)).astype(BF16)
            grad_q.append(mm(keys, grad_scores, NT) * SCALE)
            gk, gv = mm(qt, grad_scores) * SCALE, mm(gt, probs.astype(BF16))
            grad_k, grad_v = (gk, gv) if grad_k is None else (grad_k + gk, grad_v + gv)
        grad_q = jnp.concatenate(grad_q, axis=1)
        for sub in range(2):
            head = 2 * pair + sub
            part = slice(sub * DH, (sub + 1) * DH)
            for side, grad in ((0, grad_k[part]), (1, grad_v[part])):
                for r in range(RK):
                    s = side * RK + r
                    row = pl.ds(s * H + head, 1)
                    seg = slice(s * DH, (s + 1) * DH)
                    ga_rows[row, :] = jnp.sum(grad * b_rows[seg, :], axis=0, keepdims=True) * (1.0 / RK)
                    gb_rows[seg, :] += grad * (a_rows[row, :] * (1.0 / RK))
            dq = grad_q[part, sub * tokens:(sub + 1) * tokens]
            for r in range(RQ):
                row = pl.ds(r * H + head, 1)
                seg = slice(QA + r * DH, QA + (r + 1) * DH)
                gq_ref[row, :] = jnp.sum(dq * qf_ref[seg, :], axis=0, keepdims=True) * (1.0 / RQ)
                gqb_rows[r * DH:(r + 1) * DH, :] += dq * (qf_ref[row, :] * (1.0 / RQ))
        return carry

    lax.fori_loop(0, H // 2, step, 0)
    cosine, sine = cos_ref[...], sin_ref[...]
    for r in range(RQ):
        gq_ref[QA + r * DH:QA + (r + 1) * DH, :] = turn_back(gqb_rows[r * DH:(r + 1) * DH, :], cosine, sine)
    at = 0
    for j in range(n_pieces):
        n = pieces[j].shape[1]
        out_ref = send_ref if j % 2 else own_ref
        out_ref[j // 2, :KA, :] = ga_rows[:, at:at + n].astype(BF16)
        out_ref[j // 2, KA:, :] = gb_rows[:, at:at + n].astype(BF16)
        at += n


def attend_back(q, qt, gm, gmt, lse, bias, qf, cosine, sine, pieces):
    tokens = q.shape[0]
    slots = sum(p.shape[1] for p in pieces)
    n = len(pieces)
    return call(
        functools.partial(attend_back_kernel, n),
        [((QF, tokens), F32)] + [((n // 2, KF, slots // n), BF16)] * 2,
        [vmem()] * (9 + n),
        (q, qt, gm, gmt, lse, bias, qf, cosine, sine, *pieces),
        [pltpu.VMEM((KA, slots), F32), pltpu.VMEM((KB, slots), F32), pltpu.VMEM((KA, slots), F32),
         pltpu.VMEM((KB, slots), F32), pltpu.VMEM((RQ * DH, tokens), F32)],
        10 * tokens * slots * H * DH, 4 * tokens * slots, "attend_back",
    )


def hidden_kernel(go_ref, wd_ref, out_ref):
    out_ref[...] = mm(go_ref[...], wd_ref[...], NT)


def hidden_grads(hg, w_down):
    tokens, width = hg.shape[0], hg.shape[1] // 2
    ff = w_down.shape[0]
    chunk = max(c for c in range(128, ff + 1, 128) if ff % c == 0 and c <= ff // 2)
    return pl.pallas_call(
        hidden_kernel,
        grid=(ff // chunk,),
        in_specs=[pl.BlockSpec((tokens, width), lambda j: (0, 1)), pl.BlockSpec((chunk, width), lambda j: (j, 0))],
        out_specs=pl.BlockSpec((tokens, chunk), lambda j: (0, j)),
        out_shape=jax.ShapeDtypeStruct((tokens, ff), F32),
        compiler_params=pltpu.CompilerParams(vmem_limit_bytes=VMEM_BYTES),
        cost_estimate=pl.CostEstimate(
            flops=2 * tokens * width * ff, transcendentals=0, bytes_accessed=2 * width * ff + 4 * tokens * ff
        ),
        name="hidden_grads",
    )(hg, w_down)


def ffn_kernel(
    place_ref, h2_ref, hg_ref, gh_ref, resid_ref, gain_ref, mixed_ref, wg_hbm, wu_hbm, wd_hbm, wo_hbm, *refs,
):
    out_ref, gain_grad_ref, gres_ref, gm_ref, gmt_ref = refs[:5]
    mgx_refs, (branch, grad_h2, gb_cols, wg, wu, wd, wo, sems) = refs[5:-8], refs[-8:]
    width, ff = wg.shape
    n_chunks = sems.shape[1]
    chunk = ff // n_chunks
    copies = []
    for j in range(n_chunks):
        part = pl.ds(j * chunk, chunk)
        copies.append([
            pltpu.make_async_copy(wg_hbm.at[:, part], wg.at[:, part], sems.at[0, j]),
            pltpu.make_async_copy(wu_hbm.at[:, part], wu.at[:, part], sems.at[1, j]),
            pltpu.make_async_copy(wd_hbm.at[part, :], wd.at[part, :], sems.at[2, j]),
        ])
    wo_copy = pltpu.make_async_copy(wo_hbm, wo, sems.at[3, 0])
    for group in copies:
        for copy in group:
            copy.start()
    wo_copy.start()
    h2 = h2_ref[...]
    for j in range(n_chunks):
        for copy in copies[j]:
            copy.wait()
        part = slice(j * chunk, (j + 1) * chunk)
        gate, up = mm(h2, wg[:, part]), mm(h2, wu[:, part])
        grad_hidden = gh_ref[:, part]
        sig = jax.nn.sigmoid(gate)
        silu = gate * sig
        hidden = (silu * up).astype(BF16)
        grad_gate = (grad_hidden * up * sig * (1.0 + gate * (1.0 - sig))).astype(BF16)
        grad_up = (grad_hidden * silu).astype(BF16)
        more_branch = mm(hidden, wd[part, :])
        more_grad = mm(grad_gate, wg[:, part], NT) + mm(grad_up, wu[:, part], NT)
        if j == 0:
            branch[...] = more_branch
            grad_h2[...] = more_grad
        else:
            branch[...] += more_branch
            grad_h2[...] += more_grad
    resid = resid_ref[...]
    out_ref[...] = (resid + branch[...]).astype(BF16)
    s2 = lax.rsqrt(jnp.mean(resid * resid, axis=1, keepdims=True) + EPS)
    n2 = resid * s2
    gh = grad_h2[...]
    gain_grad_ref[...] = jnp.sum(gh * n2, axis=0, keepdims=True)
    g2 = gh * gain_ref[...]
    gres = hg_ref[:, width:].astype(F32) + s2 * (g2 - n2 * jnp.mean(g2 * n2, axis=1, keepdims=True))
    gres_ref[...] = gres
    gb = gres.astype(BF16)
    gb_cols[...] = gb
    wo_copy.wait()
    gm = mm(gb, wo[...], NT)
    gm_ref[...] = gm.astype(BF16)
    gmt_ref[...] = gm.T.astype(BF16)
    tokens = gb.shape[0]
    for k, mgx_ref in enumerate(mgx_refs):
        cols = mgx_ref.shape[1]
        for i in range(width // cols):
            mgx_ref[i * tokens:(i + 1) * tokens, :] = mixed_ref[:, i * cols:(i + 1) * cols]
        mgx_ref[width // cols * tokens:, :] = gb_cols[:, pl.ds(pl.multiple_of((place_ref[0] ^ k) * cols, cols), cols)]


def feed_forward(place, h2, hg, gh, w_gate, w_up, w_down, resid, gain, w_out, mixed, n_rows):
    tokens, width = resid.shape
    ff = w_gate.shape[1]
    chunk = 256 if ff % 256 == 0 else 128
    return call(
        ffn_kernel,
        [((tokens, width), BF16), ((1, width), F32), ((tokens, width), F32), ((tokens, width), BF16),
         ((width, tokens), BF16)] + [((tokens * (n_rows + 1), width // n_rows), BF16)] * n_rows,
        [smem()] + [vmem()] * 6 + [hbm()] * 4,
        (place, h2, hg, gh, resid, gain, mixed, w_gate, w_up, w_down, w_out),
        [pltpu.VMEM((tokens, width), F32), pltpu.VMEM((tokens, width), F32), pltpu.VMEM((tokens, width), BF16),
         pltpu.VMEM((width, ff), BF16), pltpu.VMEM((width, ff), BF16), pltpu.VMEM((ff, width), BF16),
         pltpu.VMEM((width, width), BF16), pltpu.SemaphoreType.DMA((4, ff // chunk))],
        10 * tokens * width * ff, 6 * width * ff, "feed_forward",
    )


def weight_kernel(n_pieces, ordered, place_ref, wg_ref, wu_ref, wd_ref, go_other, *refs):
    n_rows = n_pieces // 2
    h2_pieces, hg_same, mgx = refs[:n_pieces], refs[n_pieces:n_pieces + n_rows], refs[n_pieces + n_rows:2 * n_pieces]
    up_keep, up_send, *row_refs = refs[2 * n_pieces:-6]
    h2s, gos, wds, window, turned, sems = refs[-6:]
    tokens, width = h2_pieces[0].shape
    ff, span = wds.shape[0], window.shape[2]
    at = (place_ref[0] * 2 + place_ref[1]) * ff
    start = jnp.minimum(at // 128 * 128, wg_ref.shape[1] - span)
    cut = pl.ds(pl.multiple_of(start, 128), span)
    groups = [[pltpu.make_async_copy(ref.at[:, cut], window.at[i], sems.at[2, i])] for i, ref in enumerate((wg_ref, wu_ref))]
    groups += [[], []]
    for j in range(n_pieces):
        rows = pl.ds(j * tokens, tokens)
        groups[2].append(pltpu.make_async_copy(h2_pieces[j], h2s.at[rows, :], sems.at[0, j]))
        half = n_pieces // 2
        go = hg_same[j].at[:, pl.ds(width, width)] if j < half else go_other.at[j - half]
        groups[3].append(pltpu.make_async_copy(go, gos.at[rows, :], sems.at[1, j]))
    groups[3].append(pltpu.make_async_copy(
        wd_ref.at[pl.ds(pl.multiple_of(at, 32), ff), :], wds, sems.at[1, n_pieces]))
    groups.append([
        pltpu.make_async_copy(mgx[k], row_refs[k].at[pl.ds(ff, mgx[k].shape[0]), :], sems.at[3, k]) for k in range(n_rows)
    ])
    for group in groups:
        for copy in group:
            copy.start()
    own = pl.ds(pl.multiple_of(at - start, 32), ff)
    for i in range(2):
        groups[i][0].wait()
        turned[i] = window[i].T
    for copy in groups[2]:
        copy.wait()
    gate = mm(turned[0, own, :], h2s[...], NT)
    up = mm(turned[1, own, :], h2s[...], NT)
    for copy in groups[3]:
        copy.wait()
    grad_hidden = mm(wds[...], gos[...], NT)
    sig = jax.nn.sigmoid(gate)
    silu = gate * sig
    hidden = (silu * up).astype(BF16)
    grad_gate = (grad_hidden * up * sig * (1.0 + gate * (1.0 - sig))).astype(BF16)
    grad_up = (grad_hidden * silu).astype(BF16)
    kept = up_keep.shape[0]
    n_z = 2 * kept
    cols = width // n_z
    half = cols // 2
    for slot, k in enumerate(halving_order(n_z)):
        up_ref, i = (up_keep, slot) if slot < kept else (up_send, slot - kept)
        if ordered:
            z, core = place_ref[2] ^ k, place_ref[1]
            first = pl.ds(pl.multiple_of(z * cols + core * half, half), half)
            other = pl.ds(pl.multiple_of(z * cols + (1 - core) * half, half), half)
            h2c = jnp.concatenate([h2s[:, first], h2s[:, other]], axis=1)
        else:
            h2c = h2s[:, slot * cols:(slot + 1) * cols]
        up_ref[i, :ff, :] = mm(grad_gate, h2c).astype(BF16)
        up_ref[i, ff:, :] = mm(grad_up, h2c).astype(BF16)
    for k, row_ref in enumerate(row_refs):
        cols = row_ref.shape[1]
        row_ref[:ff, :] = mm(hidden, gos[:, pl.ds(pl.multiple_of((place_ref[0] ^ k) * cols, cols), cols)]).astype(BF16)
    for copy in groups[4]:
        copy.wait()


def halving_order(n):
    order = [0]
    k = n // 2
    while k >= 1:
        order = order + [o | k for o in order]
        k //= 2
    return order


def weight_grads(place, w_gate, w_up, w_down, h2_pieces, hg_same, go_other, mgx, n_z, ordered):
    n = len(h2_pieces)
    tokens, width = h2_pieces[0].shape
    ff = w_gate.shape[1] // n
    span = min(w_gate.shape[1], -(-ff // 128) * 128 + 128)
    total = n * tokens
    return call(
        functools.partial(weight_kernel, n, ordered),
        [((n_z // 2, 2 * ff, width // n_z), BF16)] * 2 + [((ff + p.shape[0], p.shape[1]), BF16) for p in mgx],
        [smem()] + [hbm()] * (4 + 2 * n),
        (place, w_gate, w_up, w_down, go_other, *h2_pieces, *hg_same, *mgx),
        [pltpu.VMEM((total, width), BF16), pltpu.VMEM((total, width), BF16), pltpu.VMEM((ff, width), BF16),
         pltpu.VMEM((2, width, span), BF16), pltpu.VMEM((2, span, width), BF16), pltpu.SemaphoreType.DMA((4, n + 1))],
        12 * total * width * ff, 6 * width * ff + 4 * total * width, "weight_grads",
    )


def own_cut(ordered, place_ref, k, cols):
    if not ordered:
        return slice(k * cols, (k + 1) * cols)
    return pl.ds(pl.multiple_of(((place_ref[2] ^ k) * 2 + place_ref[1]) * cols, cols), cols)


def slab_kernel(n_out, ordered, place_ref, h1_other, *refs):
    *hg_same, h1_ref, sems = refs
    n_same = len(hg_same)
    tokens = h1_other.shape[1]
    cols = h1_ref.shape[1] // n_out
    copies = []
    for j in range(2 * n_same):
        piece = hg_same[j] if j < n_same else h1_other.at[j - n_same]
        for k in range(n_out):
            copies.append(pltpu.make_async_copy(
                piece.at[:, own_cut(ordered, place_ref, k, cols)],
                h1_ref.at[pl.ds(j * tokens, tokens), pl.ds(k * cols, cols)], sems.at[j, k]))
    for copy in copies:
        copy.start()
    for copy in copies:
        copy.wait()


def own_slab(place, hg_same, h1_other, n_out, cols, ordered):
    n, tokens, width = h1_other.shape
    if not ordered:
        return jnp.concatenate([piece[:, :width] for piece in hg_same] + [h1_other.reshape(-1, width)], axis=0)
    return call(
        functools.partial(slab_kernel, n_out, ordered),
        [((2 * n * tokens, n_out * cols), BF16)],
        [smem()] + [hbm()] * (1 + n),
        (place, h1_other, *hg_same),
        [pltpu.SemaphoreType.DMA((2 * n, n_out))],
        0, 4 * n * tokens * n_out * cols, "own_slab",
    )[0]


def out_kernel(n_out, ordered, place_ref, mine_ref, other_ref, keep_ref, send_ref, wide, thin):
    kept, _, cols = keep_ref.shape
    offsets = halving_order(n_out) if ordered else list(range(n_out))
    n_rows, _, part = mine_ref.shape
    tokens = wide.shape[0] // (2 * n_rows)
    per_block = part // cols
    for i, ref in enumerate((mine_ref, other_ref)):
        for j in range(n_rows):
            rows = slice((i * n_rows + j) * tokens, (i * n_rows + j + 1) * tokens)
            thin[rows, :] = ref[j, n_rows * tokens:, :]
            for i_out, k in enumerate(offsets):
                if ordered:
                    where = pl.ds(pl.multiple_of((place_ref[2] ^ k) * tokens, tokens), tokens)
                    cut = pl.ds(pl.multiple_of(place_ref[1] * cols, cols), cols)
                else:
                    where = slice(k // per_block * tokens, (k // per_block + 1) * tokens)
                    cut = slice(k % per_block * cols, (k % per_block + 1) * cols)
                wide[rows, i_out * cols:(i_out + 1) * cols] = ref[j, where, cut]
    full = mm(thin[...].T, wide[...]).astype(BF16)
    for k in range(kept):
        keep_ref[k] = full[:, k * cols:(k + 1) * cols]
        send_ref[k] = full[:, (kept + k) * cols:(kept + k + 1) * cols]


def out_grads(place, mine, other, tokens, n_out, cols, ordered):
    n_rows, both, part = mine.shape
    total = 2 * n_rows * tokens
    return call(
        functools.partial(out_kernel, n_out, ordered),
        [((n_out // 2, part, cols), BF16)] * 2,
        [smem(), vmem(), vmem()],
        (place, mine, other),
        [pltpu.VMEM((total, n_out * cols), BF16), pltpu.VMEM((total, part), BF16)],
        2 * total * part * n_out * cols, 4 * n_rows * both * part, "out_grads",
    )


def fact_kernel(head, ordered, h1_ref, mine_ref, other_ref, *refs):
    out_refs, thin = refs[:-1], refs[-1]
    cols = out_refs[0].shape[1]
    tokens = mine_ref.shape[2]
    parts = [ref[j] for ref in (mine_ref, other_ref) for j in range(ref.shape[0])]
    for j, part in enumerate(parts):
        thin[:, j * tokens:(j + 1) * tokens] = part[head:, :]
    full = mm(thin[...], h1_ref[...]).astype(BF16)
    for k, out_ref in enumerate(out_refs):
        out_ref[head:, :] = full[:, k * cols:(k + 1) * cols]
    if ordered:
        half = head // 2
        gains = tree_sum([p[:half].astype(F32) + p[half:head].astype(F32) for p in parts])
        high = gains.astype(BF16)
        low = (gains - high.astype(F32)).astype(BF16)
        for out_ref in out_refs:
            out_ref[:half, :] = high
            out_ref[half:head, :] = low


def fact_grads(h1_slab, mine, other, head, n_out, ordered):
    n_rows, rows, tokens = mine.shape
    total = 2 * n_rows * tokens
    cols = h1_slab.shape[1] // n_out
    return call(
        functools.partial(fact_kernel, head, ordered),
        [((rows, cols), BF16)] * n_out,
        [vmem()] * 3,
        (h1_slab, mine, other),
        [pltpu.VMEM((rows - head, total), BF16)],
        2 * total * rows * n_out * cols, 2 * total * n_out * cols, "fact_grads",
    )


def input_kernel(
    n_parts, place_ref, gq_ref, *refs,
):
    parts = refs[:n_parts]
    wft_ref, x_ref, s1_ref, gain_ref, gres_ref, gain_two_ref, cos_ref, sin_ref = refs[n_parts:n_parts + 8]
    gin_ref, *gfx_refs = refs[n_parts + 8:-2]
    gf, gains = refs[-2:]
    cosine, sine = cos_ref[...], sin_ref[...]
    kv = tree_sum([part[...].astype(F32) for part in parts])
    gf[:QF, :] = gq_ref[...]
    gf[QF:QF + KA, :] = kv[:KA]
    for r in range(2 * RK):
        rows = kv[KA + r * DH:KA + (r + 1) * DH]
        if r < RK:
            rows = turn_back(rows, cosine, sine)
        gf[QF + KA + r * DH:QF + KA + (r + 1) * DH, :] = rows
    grad = gf[...].T.astype(BF16)
    grad_h1 = mm(grad, wft_ref[...])
    s1 = s1_ref[...]
    n1 = x_ref[...].astype(F32) * s1
    gain_one = jnp.sum(grad_h1 * n1, axis=0, keepdims=True)
    gain_two = gain_two_ref[...]
    g1 = grad_h1 * gain_ref[...]
    gin_ref[...] = gres_ref[...] + s1 * (g1 - n1 * jnp.mean(g1 * n1, axis=1, keepdims=True))
    tokens, width = x_ref.shape
    half = gains.shape[0]
    for i in range(half // 2):
        gains[i:i + 1, :] = gain_one[:, i * tokens:(i + 1) * tokens]
        gains[half // 2 + i:half // 2 + i + 1, :] = gain_two[:, i * tokens:(i + 1) * tokens]
    high = gains[...].astype(BF16)
    low = (gains[...] - high.astype(F32)).astype(BF16)
    for k, gfx_ref in enumerate(gfx_refs):
        part = gfx_ref.shape[0] - 2 * half
        gfx_ref[:half, :] = high
        gfx_ref[half:2 * half, :] = low
        gfx_ref[2 * half:, :] = gf[pl.ds(pl.multiple_of((place_ref[0] ^ k) * part, 8), part), :].astype(BF16)


def input_grads(place, gq, parts, w_fact_t, x, s1, gain, gres, gain_two, cosine, sine, n_rows):
    tokens, width = x.shape
    nf = w_fact_t.shape[0]
    half = 2 * width // tokens
    return call(
        functools.partial(input_kernel, len(parts)),
        [((tokens, width), F32)] + [((2 * half + nf // n_rows, tokens), BF16)] * n_rows,
        [smem()] + [vmem()] * (9 + len(parts)),
        (place, gq, *parts, w_fact_t, x, s1, gain, gres, gain_two, cosine, sine),
        [pltpu.VMEM((nf, tokens), F32), pltpu.VMEM((half, tokens), F32)],
        2 * tokens * width * nf, 2 * width * nf, "input_grads",
    )


def after(values, *others):
    flat, tree = jax.tree.flatten((values, others))
    return jax.tree.unflatten(tree, lax.optimization_barrier(flat))[0]


def body(inputs, lengths, gain_attn, w_fact, w_out, gain_ffn, w_gate, w_up, w_down, cotangent):
    seqs, local_len, width = inputs.shape
    tokens = seqs * local_len
    n_rows, n_ctx = lax.axis_size(ROW), lax.axis_size(CTX)
    n_z = n_ctx // 2
    row, ctx = lax.axis_index(ROW), lax.axis_index(CTX)
    z, core = ctx // 2, ctx % 2
    slots_all = local_len * n_ctx
    block_len = local_len // 2
    ff = w_gate.shape[1]
    ff_part = ff // (2 * n_rows)
    own_cols = width // n_ctx
    per = n_ctx // (2 * n_rows)
    ordered = own_cols % 128 == 0 and per == 1 and tokens == 128
    n_out = n_z if ordered else n_ctx
    place = jnp.stack([row, core, z]).astype(jnp.int32)

    within = jnp.arange(local_len, dtype=jnp.int32)
    local_pos = jnp.tile(slot_position(ctx * local_len + within, block_len, slots_all), seqs)
    local_seq = jnp.repeat(jnp.arange(seqs, dtype=jnp.int32), local_len)
    valid = (local_pos < jnp.repeat(lengths, local_len)).astype(F32)[:, None]
    piece_of = jnp.arange(n_ctx, dtype=jnp.int32) ^ ctx
    key_pos = jnp.tile(
        slot_position(piece_of[:, None] * local_len + within[None, :], block_len, slots_all)[:, None, :], (1, seqs, 1)
    ).reshape(-1)
    key_seq = jnp.tile(local_seq, n_ctx)
    key_len = jnp.tile(jnp.repeat(lengths, local_len), n_ctx)
    allowed = (
        (key_pos[None, :] <= local_pos[:, None])
        & (key_pos < key_len)[None, :]
        & (key_seq[None, :] == local_seq[:, None])
    )
    bias = jnp.where(allowed, 0.0, -1e30).astype(F32)

    x = inputs.reshape(tokens, width)
    gain_one, gain_two = gain_attn[None, :], gain_ffn[None, :]
    w_fact_t = w_fact.T

    def others(values, axis, n):
        return [swap(values[k], axis, k) for k in range(1, n)]

    def along_core(values):
        return list(values) + [swap(value, "core", 1) for value in values]

    def both_cores(values):
        mine = jnp.stack(values)
        return [mine, swap(mine, "core", 1)]

    hg, s1, q, qt, qf, kv, cosine, sine = project(
        x, cotangent.reshape(tokens, width), valid, gain_one, w_fact_t, local_pos.astype(F32)[None, :]
    )
    kv_z = [kv] + others([kv] * n_z, "z", n_z)
    gh = hidden_grads(hg, w_down)
    kv_z = after(kv_z, gh)
    kv_pieces = []
    for part in kv_z:
        kv_pieces += [part, swap(part, "core", 1)]
    hg_same = [hg] + others([hg] * n_rows, ROW, n_rows)
    h2, mixed, resid, lse = attend(q, bias, w_out, x, gain_two, kv_pieces)
    h2_same = [h2] + others([h2] * n_rows, ROW, n_rows)
    hg_same = after(hg_same, h2)
    go_other = swap(jnp.stack([part[:, width:] for part in hg_same]), "core", 1)
    block_out, gain_two_part, gres, gm, gmt, *mgx = feed_forward(
        place, h2, after(hg, hg_same), gh, w_gate, w_up, w_down, resid, gain_two, w_out, mixed, n_rows
    )
    h2_pieces = along_core(after(h2_same, gm, go_other))
    up_keep, up_send, *row_out = weight_grads(
        place, w_gate, w_up, w_down, h2_pieces, hg_same, go_other, mgx, n_z, ordered
    )
    if not ordered:
        turns = jnp.asarray(halving_order(n_z), jnp.int32) ^ z
        cores = jnp.arange(2, dtype=jnp.int32) ^ core
        up = jnp.take(jnp.concatenate([up_keep, up_send]), turns, axis=0)
        up = jnp.take(up.reshape(n_z, 2 * ff_part, 2, own_cols), cores, axis=2).reshape(up.shape)
        up_keep, up_send = up[:n_z // 2], up[n_z // 2:]

    up_got = swap(up_send, "z", 1)
    row_same = [row_out[0]] + others(row_out, ROW, n_rows)
    gm_in, hg_same = after((gm, hg_same), up_send)
    h1_other = swap(jnp.stack([part[:, :width] for part in hg_same]), "core", 1)
    gq, gkv_own, gkv_send = attend_back(q, qt, gm_in, gmt, lse, bias, qf, cosine, sine, kv_pieces)
    gkv_send, h1_other, up_got = lax.optimization_barrier((gkv_send, h1_other, up_got))
    gkv_got = swap(gkv_send, "core", 1)
    row_same = after(row_same, gkv_got)
    gkv_z = [(gkv_own[k].astype(F32) + gkv_got[k].astype(F32)).astype(BF16) for k in range(n_z)]
    kv_parts = [gkv_z[0]] + others(gkv_z, "z", n_z)
    mg_mine, mg_other = both_cores([part[ff_part:] for part in row_same])
    if ordered:
        down = jnp.stack([part[:ff_part] for part in row_same])
        down = jnp.take(down, jnp.asarray(halving_order(n_z), jnp.int32) ^ z ^ row, axis=0)
        down_keep, down_send = down[:n_z // 2], down[n_z // 2:]
        down_got = swap(down_send, "z", 1)
    if ordered:
        kv_parts, down_got = lax.optimization_barrier((kv_parts, down_got))

    def own_blocks(parts, offsets):
        parts = jnp.take(parts, (jnp.asarray(offsets, jnp.int32) ^ z) * 2 + core, axis=0)
        return [parts[k] for k in range(n_z)]

    out_keep, out_send = out_grads(place, mg_mine, mg_other, tokens, n_out, own_cols, ordered)
    if not ordered:
        out_parts = own_blocks(jnp.concatenate([out_keep, out_send]), halving_order(n_z))
        out_keep, out_send = jnp.stack(out_parts[:n_z // 2]), jnp.stack(out_parts[n_z // 2:])
    out_got = swap(out_send, "z", 1)
    gq, out_got = after((gq, out_got), kv_parts)

    def add_up(keep, got, hold, step=1):
        total = keep.astype(F32) + got.astype(F32)
        n = total.shape[0]
        while n > 1:
            n //= 2
            step *= 2
            kept, got = total[:n], swap(total[n:].astype(BF16), "z", step)
            total = (after(kept, *hold) if n == 1 else kept) + got.astype(F32)
        return total[0]

    side = (out_keep.shape[0], -1, 2 * own_cols)
    ffn_keep = [up_keep, down_keep, out_keep.reshape(side)] if ordered else [up_keep, out_keep.reshape(side)]
    ffn_got = [up_got, down_got, out_got.reshape(side)] if ordered else [up_got, out_got.reshape(side)]
    ffn_keep, ffn_got = jnp.concatenate(ffn_keep, axis=1), jnp.concatenate(ffn_got, axis=1)
    grad_inputs, *gfx = input_grads(
        place, gq, kv_parts, w_fact_t, x, s1, gain_one, gres, gain_two_part, cosine, sine, n_rows
    )
    head = gfx[0].shape[0] - w_fact.shape[1] // n_rows
    gf_same = [gfx[0]] + others(gfx, ROW, n_rows)
    h1_slab = own_slab(place, hg_same, after(h1_other, gfx[0]), n_out, own_cols, ordered)
    gf_all = both_cores(after(gf_same, h1_slab))
    tail_parts = fact_grads(h1_slab, *gf_all, head, n_out, ordered)
    if not ordered:
        tail_parts = own_blocks(jnp.stack(tail_parts), list(range(n_z)))
    total = add_up(ffn_keep, ffn_got, tail_parts)
    tail_got = others(tail_parts, "z", n_z)
    up_total = total[:2 * ff_part]
    grad_out = total[-own_cols * out_keep.shape[1] // (2 * own_cols):].reshape(out_keep.shape[1:]).T
    mine, other = up_total[:, :own_cols], swap(up_total[:, own_cols:].astype(BF16), "core", 1).astype(F32)
    first = jnp.where(core == 0, mine, other)
    second = jnp.where(core == 0, other, mine)
    grad_gate = jnp.concatenate([first[:ff_part], second[:ff_part]], axis=0).T
    grad_up = jnp.concatenate([first[ff_part:], second[ff_part:]], axis=0).T

    if ordered:
        grad_down = total[2 * ff_part:3 * ff_part]
    else:
        down = jnp.stack([part[:ff_part] for part in row_out])
        down = jnp.take(down, jnp.arange(n_rows, dtype=jnp.int32) ^ row, axis=0)
        down = down.reshape(n_rows, per, ff_part // per, width // n_rows).transpose(1, 0, 2, 3)
        down = lax.psum_scatter(down.reshape(n_z, ff_part // per, -1), "z", scatter_dimension=0)
        moves = []
        for r in range(n_rows):
            for c in range(2):
                for p in range(n_z):
                    b, s = p // n_rows, p % n_rows
                    moves.append((r * n_ctx + 2 * p + c, s * n_ctx + (r * 2 + c) * per + b))
        grad_down = lax.ppermute(down, ROW + CTX, moves).astype(F32)

    tail_parts = after(tail_parts, grad_gate, grad_up, grad_out)
    tail = tree_sum([part.astype(F32) for part in [tail_parts[0]] + tail_got])
    grad_fact = tail[head:].T
    if ordered:
        gains = (tail[:head // 2] + tail[head // 2:head]).reshape(2, width)
    else:
        sums = gfx[0][:head // 2].astype(F32) + gfx[0][head // 2:head].astype(F32)
        gains = lax.psum(sums, ROW + CTX).reshape(2, width)

    return (
        block_out.reshape(inputs.shape),
        grad_inputs.reshape(inputs.shape),
        gains[0],
        grad_fact,
        grad_out,
        gains[1],
        grad_gate,
        grad_up,
        grad_down,
    )


def solution(mesh):
    n_rows, n_ctx = mesh.shape["row"], mesh.shape["ctx"]
    fine = Mesh(mesh.devices.reshape(n_rows // 2, 2, n_ctx // 2, 2), ROW + CTX)
    placed = (P(ROW, CTX, None), P(ROW), P(), P(), P(), P(), P(), P(), P(), P(ROW, CTX, None))
    return jax.shard_map(
        body,
        mesh=fine,
        in_specs=placed,
        out_specs=(
            P(ROW, CTX, None), P(ROW, CTX, None), P(), P(CTX, ROW), P(CTX, ROW), P(), P(CTX, ROW), P(CTX, ROW),
            P(CTX, ROW),
        ),
        check_vma=False,
    )
```

```python
import functools

import jax
import jax.numpy as jnp
from jax import lax
from jax.experimental import pallas as pl
from jax.experimental.pallas import tpu as pltpu
from jax.sharding import Mesh
from jax.sharding import PartitionSpec as P

H = 16
DH = 64
RQ = 6
RK = 2
EPS = 1e-06
QA = RQ * H
QF = RQ * (H + DH)
KA = 2 * RK * H
KB = 2 * RK * DH
KF = KA + KB
SCALE = DH ** (-0.5)
F32 = jnp.float32
BF16 = jnp.bfloat16
VMEM_BYTES = 56 * 1024 * 1024

NN = (((1,), (0,)), ((), ()))
NT = (((1,), (1,)), ((), ()))


def mm(a, b, dims=NN):
    return lax.dot_general(a, b, dims, preferred_element_type=F32)


def vmem():
    return pl.BlockSpec(memory_space=pltpu.VMEM)


def smem():
    return pl.BlockSpec(memory_space=pltpu.SMEM)


def hbm():
    return pl.BlockSpec(memory_space=pltpu.HBM)


def call(kernel, outs, ins, args, scratch=(), flops=0, moved=0, name=None):
    return pl.pallas_call(
        kernel,
        out_shape=[jax.ShapeDtypeStruct(s, d) for s, d in outs],
        in_specs=ins,
        out_specs=[vmem() for _ in outs],
        scratch_shapes=list(scratch),
        compiler_params=pltpu.CompilerParams(vmem_limit_bytes=VMEM_BYTES),
        cost_estimate=pl.CostEstimate(flops=flops, transcendentals=0, bytes_accessed=moved),
        name=name,
    )(*args)


def slot_position(index, block_len, slots_all):
    block_id = index // (2 * block_len)
    within = index % (2 * block_len)
    return jnp.where(
        within < block_len,
        block_id * block_len + within,
        (slots_all // block_len - 1 - block_id) * block_len + within - block_len,
    )


def turn(rows, cosine, sine):
    half = DH // 2
    upper, lower = rows[:half], rows[half:]
    return jnp.concatenate([upper * cosine - lower * sine, lower * cosine + upper * sine], axis=0)


def turn_back(rows, cosine, sine):
    half = DH // 2
    upper, lower = rows[:half], rows[half:]
    return jnp.concatenate([upper * cosine + lower * sine, lower * cosine - upper * sine], axis=0)


ROW = ("r1", "r0")
CTX = ("z", "core")
GROUP = ("r1", "r0", "core")


def swap(value, axis, k):
    size = lax.axis_size(axis)
    return lax.ppermute(value, axis, [(j, j ^ k) for j in range(size)])


def tree_sum(parts):
    parts = list(parts)
    while len(parts) > 1:
        parts = [parts[i] + parts[i + 1] for i in range(0, len(parts), 2)]
    return parts[0]


def factor_kernel(
    x_ref, cot_ref, valid_ref, gain_ref, wft_ref, pos_ref,
    hg_ref, s1_ref, q_ref, qt_ref, qf_ref, kv_ref, cos_ref, sin_ref, ft,
):
    x = x_ref[...].astype(F32)
    s1 = lax.rsqrt(jnp.mean(x * x, axis=1, keepdims=True) + EPS)
    s1_ref[...] = s1
    h1 = (x * s1 * gain_ref[...]).astype(BF16)
    hg_ref[:, :x.shape[1]] = h1
    hg_ref[:, x.shape[1]:] = (cot_ref[...].astype(F32) * valid_ref[...]).astype(BF16)
    half = lax.broadcasted_iota(jnp.int32, cos_ref.shape, 0).astype(F32)
    angles = pos_ref[...] * jnp.exp(-jnp.log(10000.0) * (2.0 * half) / DH)
    cosine, sine = jnp.cos(angles), jnp.sin(angles)
    cos_ref[...] = cosine
    sin_ref[...] = sine
    ft[:wft_ref.shape[0], :] = mm(wft_ref[...], h1, NT)
    kv_ref[:KA, :] = ft[QF:QF + KA, :].astype(BF16)
    for r in range(2 * RK):
        rows = ft[QF + KA + r * DH:QF + KA + (r + 1) * DH, :]
        if r < RK:
            rows = turn(rows, cosine, sine)
        kv_ref[KA + r * DH:KA + (r + 1) * DH, :] = rows.astype(BF16)
    qf_ref[:QA, :] = ft[:QA, :]
    for r in range(RQ):
        qf_ref[QA + r * DH:QA + (r + 1) * DH, :] = turn(ft[QA + r * DH:QA + (r + 1) * DH, :], cosine, sine)
    for h in range(H):
        total = None
        for r in range(RQ):
            term = qf_ref[r * H + h:r * H + h + 1, :] * qf_ref[QA + r * DH:QA + (r + 1) * DH, :]
            total = term if total is None else total + term
        ft[h * DH:(h + 1) * DH, :] = total / RQ
    qt = ft[:H * DH, :]
    qt_ref[...] = qt.astype(BF16)
    q_ref[...] = qt.T.astype(BF16)


def project(x, cot, valid, gain, w_fact_t, pos):
    tokens, width = x.shape
    nf = w_fact_t.shape[0]
    angles = ((DH // 2, tokens), F32)
    return call(
        factor_kernel,
        [((tokens, 2 * width), BF16), ((tokens, 1), F32), ((tokens, H * DH), BF16),
         ((H * DH, tokens), BF16), ((QF, tokens), F32), ((KF, tokens), BF16), angles, angles],
        [vmem()] * 6,
        (x, cot, valid, gain, w_fact_t, pos),
        [pltpu.VMEM((max(nf, H * DH), tokens), F32)],
        2 * tokens * width * nf, 2 * width * nf, "factors",
    )


def load_factors(pieces, a_rows, b_rows):
    at = 0
    for piece in pieces:
        n = piece.shape[1]
        a_rows[:, at:at + n] = piece[:KA, :].astype(F32)
        b_rows[:, at:at + n] = piece[KA:, :].astype(F32)
        at += n


def expand_pair(pair, side, a_rows, b_rows):
    halves = []
    for sub in range(2):
        total = None
        for r in range(RK):
            a = a_rows[pl.ds((side * RK + r) * H + 2 * pair + sub, 1), :]
            term = a * b_rows[(side * RK + r) * DH:(side * RK + r + 1) * DH, :]
            total = term if total is None else total + term
        halves.append((total * (1.0 / RK)).astype(BF16))
    return jnp.concatenate(halves, axis=0)


def stack_pair(rows):
    lane = lax.broadcasted_iota(jnp.int32, rows.shape, 1)
    zero = jnp.zeros_like(rows)
    return jnp.concatenate([jnp.where(lane < DH, rows, zero), jnp.where(lane < DH, zero, rows)], axis=0)


def pair_lanes(pair):
    return pl.ds(pl.multiple_of(pair * 2 * DH, 2 * DH), 2 * DH)


def attend_kernel(n_pieces, *refs):
    q_ref, bias_ref, wo_ref, x_ref, gain_ref = refs[:5]
    pieces = refs[5:5 + n_pieces]
    h2_ref, mixed, resid_ref, lse_ref, a_rows, b_rows = refs[5 + n_pieces:]
    tokens, width = x_ref.shape
    load_factors(pieces, a_rows, b_rows)
    bias = bias_ref[...]
    bias = jnp.concatenate([bias, bias], axis=0)

    def step(pair, carry):
        keys = expand_pair(pair, 0, a_rows, b_rows)
        values = expand_pair(pair, 1, a_rows, b_rows)
        q = stack_pair(q_ref[:, pair_lanes(pair)])
        scores = mm(q, keys) * SCALE + bias
        top = jnp.max(scores, axis=1, keepdims=True)
        exponent = jnp.exp(scores - top)
        total = jnp.sum(exponent, axis=1, keepdims=True)
        probs = (exponent * (1.0 / total)).astype(BF16)
        lse_ref[pair] = top + jnp.log(total)
        out = mm(probs, values, NT)
        lane = lax.broadcasted_iota(jnp.int32, (tokens, 2 * DH), 1)
        mixed[:, pair_lanes(pair)] = jnp.where(lane < DH, out[:tokens], out[tokens:]).astype(BF16)
        return carry

    lax.fori_loop(0, H // 2, step, 0)
    resid = x_ref[...].astype(F32) + mm(mixed[...], wo_ref[...])
    resid_ref[...] = resid
    s2 = lax.rsqrt(jnp.mean(resid * resid, axis=1, keepdims=True) + EPS)
    h2_ref[...] = (resid * s2 * gain_ref[...]).astype(BF16)


def attend(q, bias, w_out, x, gain, pieces):
    tokens, width = x.shape
    slots = sum(p.shape[1] for p in pieces)
    return call(
        functools.partial(attend_kernel, len(pieces)),
        [((tokens, width), BF16), ((tokens, H * DH), BF16), ((tokens, width), F32), ((H // 2, 2 * tokens, 1), F32)],
        [vmem()] * (5 + len(pieces)),
        (q, bias, w_out, x, gain, *pieces),
        [pltpu.VMEM((KA, slots), F32), pltpu.VMEM((KB, slots), F32)],
        4 * tokens * slots * H * DH, 2 * width * width, "attend",
    )


def attend_back_kernel(n_pieces, *refs):
    q_ref, qt_ref, gm_ref, gmt_ref, lse_ref, bias_ref, qf_ref, cos_ref, sin_ref = refs[:9]
    pieces = refs[9:9 + n_pieces]
    gq_ref, own_ref, send_ref, a_rows, b_rows, ga_rows, gb_rows, gqb_rows = refs[9 + n_pieces:]
    tokens = q_ref.shape[0]
    load_factors(pieces, a_rows, b_rows)
    gb_rows[...] = jnp.zeros_like(gb_rows)
    gqb_rows[...] = jnp.zeros_like(gqb_rows)

    def spread(rows):
        top = lax.broadcasted_iota(jnp.int32, rows.shape, 0) < DH
        zero = jnp.zeros_like(rows)
        return jnp.concatenate([jnp.where(top, rows, zero), jnp.where(top, zero, rows)], axis=1)

    def step(pair, carry):
        keys = expand_pair(pair, 0, a_rows, b_rows)
        values = expand_pair(pair, 1, a_rows, b_rows)
        rows = pl.ds(pl.multiple_of(pair * 2 * DH, 2 * DH), 2 * DH)
        both = (
            stack_pair(q_ref[:, pair_lanes(pair)]), stack_pair(gm_ref[:, pair_lanes(pair)]),
            spread(qt_ref[rows, :]), spread(gmt_ref[rows, :]), lse_ref[pair],
        )
        takes = [slice(0, 2 * tokens)] if keys.shape[1] <= 2048 else [slice(0, tokens), slice(tokens, 2 * tokens)]
        grad_q, grad_k, grad_v = [], None, None
        for take in takes:
            q, g, qt, gt, lse = both[0][take], both[1][take], both[2][:, take], both[3][:, take], both[4][take]
            heads = q.shape[0] // tokens
            scores = mm(q, keys) * SCALE + jnp.concatenate([bias_ref[...]] * heads, axis=0)
            probs = jnp.exp(scores - lse)
            grad_probs = mm(g, values)
            inner = jnp.sum(probs * grad_probs, axis=1, keepdims=True)
            grad_scores = (probs * (grad_probs - inner)).astype(BF16)
            grad_q.append(mm(keys, grad_scores, NT) * SCALE)
            gk, gv = mm(qt, grad_scores) * SCALE, mm(gt, probs.astype(BF16))
            grad_k, grad_v = (gk, gv) if grad_k is None else (grad_k + gk, grad_v + gv)
        grad_q = jnp.concatenate(grad_q, axis=1)
        for sub in range(2):
            head = 2 * pair + sub
            part = slice(sub * DH, (sub + 1) * DH)
            for side, grad in ((0, grad_k[part]), (1, grad_v[part])):
                for r in range(RK):
                    s = side * RK + r
                    row = pl.ds(s * H + head, 1)
                    seg = slice(s * DH, (s + 1) * DH)
                    ga_rows[row, :] = jnp.sum(grad * b_rows[seg, :], axis=0, keepdims=True) * (1.0 / RK)
                    gb_rows[seg, :] += grad * (a_rows[row, :] * (1.0 / RK))
            dq = grad_q[part, sub * tokens:(sub + 1) * tokens]
            for r in range(RQ):
                row = pl.ds(r * H + head, 1)
                seg = slice(QA + r * DH, QA + (r + 1) * DH)
                gq_ref[row, :] = jnp.sum(dq * qf_ref[seg, :], axis=0, keepdims=True) * (1.0 / RQ)
                gqb_rows[r * DH:(r + 1) * DH, :] += dq * (qf_ref[row, :] * (1.0 / RQ))
        return carry

    lax.fori_loop(0, H // 2, step, 0)
    cosine, sine = cos_ref[...], sin_ref[...]
    for r in range(RQ):
        gq_ref[QA + r * DH:QA + (r + 1) * DH, :] = turn_back(gqb_rows[r * DH:(r + 1) * DH, :], cosine, sine)
    at = 0
    for j in range(n_pieces):
        n = pieces[j].shape[1]
        out_ref = send_ref if j % 2 else own_ref
        out_ref[j // 2, :KA, :] = ga_rows[:, at:at + n].astype(BF16)
        out_ref[j // 2, KA:, :] = gb_rows[:, at:at + n].astype(BF16)
        at += n


def attend_back(q, qt, gm, gmt, lse, bias, qf, cosine, sine, pieces):
    tokens = q.shape[0]
    slots = sum(p.shape[1] for p in pieces)
    n = len(pieces)
    return call(
        functools.partial(attend_back_kernel, n),
        [((QF, tokens), F32)] + [((n // 2, KF, slots // n), BF16)] * 2,
        [vmem()] * (9 + n),
        (q, qt, gm, gmt, lse, bias, qf, cosine, sine, *pieces),
        [pltpu.VMEM((KA, slots), F32), pltpu.VMEM((KB, slots), F32), pltpu.VMEM((KA, slots), F32),
         pltpu.VMEM((KB, slots), F32), pltpu.VMEM((RQ * DH, tokens), F32)],
        10 * tokens * slots * H * DH, 4 * tokens * slots, "attend_back",
    )


def hidden_kernel(go_ref, wd_ref, out_ref):
    out_ref[...] = mm(go_ref[...], wd_ref[...], NT)


def hidden_grads(hg, w_down):
    tokens, width = hg.shape[0], hg.shape[1] // 2
    ff = w_down.shape[0]
    chunk = max(c for c in range(128, ff + 1, 128) if ff % c == 0 and c <= ff // 2)
    return pl.pallas_call(
        hidden_kernel,
        grid=(ff // chunk,),
        in_specs=[pl.BlockSpec((tokens, width), lambda j: (0, 1)), pl.BlockSpec((chunk, width), lambda j: (j, 0))],
        out_specs=pl.BlockSpec((tokens, chunk), lambda j: (0, j)),
        out_shape=jax.ShapeDtypeStruct((tokens, ff), F32),
        compiler_params=pltpu.CompilerParams(vmem_limit_bytes=VMEM_BYTES),
        cost_estimate=pl.CostEstimate(
            flops=2 * tokens * width * ff, transcendentals=0, bytes_accessed=2 * width * ff + 4 * tokens * ff
        ),
        name="hidden_grads",
    )(hg, w_down)


def ffn_kernel(
    place_ref, h2_ref, hg_ref, gh_ref, resid_ref, gain_ref, mixed_ref, wg_hbm, wu_hbm, wd_hbm, wo_hbm, *refs,
):
    out_ref, gain_grad_ref, gres_ref, gm_ref, gmt_ref = refs[:5]
    mgx_refs, (branch, grad_h2, gb_cols, wg, wu, wd, wo, sems) = refs[5:-8], refs[-8:]
    width, ff = wg.shape
    n_chunks = sems.shape[1]
    chunk = ff // n_chunks
    copies = []
    for j in range(n_chunks):
        part = pl.ds(j * chunk, chunk)
        copies.append([
            pltpu.make_async_copy(wg_hbm.at[:, part], wg.at[:, part], sems.at[0, j]),
            pltpu.make_async_copy(wu_hbm.at[:, part], wu.at[:, part], sems.at[1, j]),
            pltpu.make_async_copy(wd_hbm.at[part, :], wd.at[part, :], sems.at[2, j]),
        ])
    wo_copy = pltpu.make_async_copy(wo_hbm, wo, sems.at[3, 0])
    for group in copies:
        for copy in group:
            copy.start()
    wo_copy.start()
    h2 = h2_ref[...]
    for j in range(n_chunks):
        for copy in copies[j]:
            copy.wait()
        part = slice(j * chunk, (j + 1) * chunk)
        gate, up = mm(h2, wg[:, part]), mm(h2, wu[:, part])
        grad_hidden = gh_ref[:, part]
        sig = jax.nn.sigmoid(gate)
        silu = gate * sig
        hidden = (silu * up).astype(BF16)
        grad_gate = (grad_hidden * up * sig * (1.0 + gate * (1.0 - sig))).astype(BF16)
        grad_up = (grad_hidden * silu).astype(BF16)
        more_branch = mm(hidden, wd[part, :])
        more_grad = mm(grad_gate, wg[:, part], NT) + mm(grad_up, wu[:, part], NT)
        if j == 0:
            branch[...] = more_branch
            grad_h2[...] = more_grad
        else:
            branch[...] += more_branch
            grad_h2[...] += more_grad
    resid = resid_ref[...]
    out_ref[...] = (resid + branch[...]).astype(BF16)
    s2 = lax.rsqrt(jnp.mean(resid * resid, axis=1, keepdims=True) + EPS)
    n2 = resid * s2
    gh = grad_h2[...]
    gain_grad_ref[...] = jnp.sum(gh * n2, axis=0, keepdims=True)
    g2 = gh * gain_ref[...]
    gres = hg_ref[:, width:].astype(F32) + s2 * (g2 - n2 * jnp.mean(g2 * n2, axis=1, keepdims=True))
    gres_ref[...] = gres
    gb = gres.astype(BF16)
    gb_cols[...] = gb
    wo_copy.wait()
    gm = mm(gb, wo[...], NT)
    gm_ref[...] = gm.astype(BF16)
    gmt_ref[...] = gm.T.astype(BF16)
    for k, mgx_ref in enumerate(mgx_refs):
        cols = mgx_ref.shape[1] - width
        mgx_ref[:, :width] = mixed_ref[...]
        mgx_ref[:, width:] = gb_cols[:, pl.ds(pl.multiple_of((place_ref[0] ^ k) * cols, cols), cols)]


def feed_forward(place, h2, hg, gh, w_gate, w_up, w_down, resid, gain, w_out, mixed, n_rows):
    tokens, width = resid.shape
    ff = w_gate.shape[1]
    chunk = 256 if ff % 256 == 0 else 128
    return call(
        ffn_kernel,
        [((tokens, width), BF16), ((1, width), F32), ((tokens, width), F32), ((tokens, width), BF16),
         ((width, tokens), BF16)] + [((tokens, width + width // n_rows), BF16)] * n_rows,
        [smem()] + [vmem()] * 6 + [hbm()] * 4,
        (place, h2, hg, gh, resid, gain, mixed, w_gate, w_up, w_down, w_out),
        [pltpu.VMEM((tokens, width), F32), pltpu.VMEM((tokens, width), F32), pltpu.VMEM((tokens, width), BF16),
         pltpu.VMEM((width, ff), BF16), pltpu.VMEM((width, ff), BF16), pltpu.VMEM((ff, width), BF16),
         pltpu.VMEM((width, width), BF16), pltpu.SemaphoreType.DMA((4, ff // chunk))],
        10 * tokens * width * ff, 6 * width * ff, "feed_forward",
    )


def weight_kernel(n_pieces, ordered, place_ref, wg_ref, wu_ref, wd_ref, go_other, *refs):
    h2_pieces, hg_same = refs[:n_pieces], refs[n_pieces:n_pieces + n_pieces // 2]
    up_keep, up_send, down_keep, down_send, h2s, gos, wds, window, turned, sems = refs[n_pieces + n_pieces // 2:]
    tokens, width = h2_pieces[0].shape
    ff, span = wds.shape[0], window.shape[2]
    at = (place_ref[0] * 2 + place_ref[1]) * ff
    start = jnp.minimum(at // 128 * 128, wg_ref.shape[1] - span)
    cut = pl.ds(pl.multiple_of(start, 128), span)
    groups = [[pltpu.make_async_copy(ref.at[:, cut], window.at[i], sems.at[2, i])] for i, ref in enumerate((wg_ref, wu_ref))]
    groups += [[], []]
    for j in range(n_pieces):
        rows = pl.ds(j * tokens, tokens)
        groups[2].append(pltpu.make_async_copy(h2_pieces[j], h2s.at[rows, :], sems.at[0, j]))
        half = n_pieces // 2
        go = hg_same[j].at[:, pl.ds(width, width)] if j < half else go_other.at[j - half]
        groups[3].append(pltpu.make_async_copy(go, gos.at[rows, :], sems.at[1, j]))
    groups[3].append(pltpu.make_async_copy(
        wd_ref.at[pl.ds(pl.multiple_of(at, 32), ff), :], wds, sems.at[1, n_pieces]))
    for group in groups:
        for copy in group:
            copy.start()
    own = pl.ds(pl.multiple_of(at - start, 32), ff)
    for i in range(2):
        groups[i][0].wait()
        turned[i] = window[i].T
    for copy in groups[2]:
        copy.wait()
    gate = mm(turned[0, own, :], h2s[...], NT)
    up = mm(turned[1, own, :], h2s[...], NT)
    for copy in groups[3]:
        copy.wait()
    grad_hidden = mm(wds[...], gos[...], NT)
    sig = jax.nn.sigmoid(gate)
    silu = gate * sig
    hidden = (silu * up).astype(BF16)
    grad_gate = (grad_hidden * up * sig * (1.0 + gate * (1.0 - sig))).astype(BF16)
    grad_up = (grad_hidden * silu).astype(BF16)
    kept = up_keep.shape[0]
    n_z = 2 * kept
    cols = width // n_z
    half = cols // 2
    for slot, k in enumerate(halving_order(n_z)):
        up_ref, down_ref, i = (up_keep, down_keep, slot) if slot < kept else (up_send, down_send, slot - kept)
        if ordered:
            z, core = place_ref[2] ^ k, place_ref[1]
            first = pl.ds(pl.multiple_of(z * cols + core * half, half), half)
            other = pl.ds(pl.multiple_of(z * cols + (1 - core) * half, half), half)
            straight = pl.ds(pl.multiple_of((z ^ place_ref[0]) * cols, cols), cols)
            h2c = jnp.concatenate([h2s[:, first], h2s[:, other]], axis=1)
        else:
            straight = slice(slot * cols, (slot + 1) * cols)
            h2c = h2s[:, straight]
        up_ref[i, :ff, :] = mm(grad_gate, h2c).astype(BF16)
        up_ref[i, ff:, :] = mm(grad_up, h2c).astype(BF16)
        down_ref[i] = mm(hidden, gos[:, straight]).astype(BF16)


def halving_order(n):
    order = [0]
    k = n // 2
    while k >= 1:
        order = order + [o | k for o in order]
        k //= 2
    return order


def weight_grads(place, w_gate, w_up, w_down, h2_pieces, hg_same, go_other, n_z, ordered):
    n = len(h2_pieces)
    tokens, width = h2_pieces[0].shape
    ff = w_gate.shape[1] // n
    span = min(w_gate.shape[1], -(-ff // 128) * 128 + 128)
    total = n * tokens
    return call(
        functools.partial(weight_kernel, n, ordered),
        [((n_z // 2, 2 * ff, width // n_z), BF16)] * 2 + [((n_z // 2, ff, width // n_z), BF16)] * 2,
        [smem()] + [hbm()] * (4 + n + n // 2),
        (place, w_gate, w_up, w_down, go_other, *h2_pieces, *hg_same),
        [pltpu.VMEM((total, width), BF16), pltpu.VMEM((total, width), BF16), pltpu.VMEM((ff, width), BF16),
         pltpu.VMEM((2, width, span), BF16), pltpu.VMEM((2, span, width), BF16), pltpu.SemaphoreType.DMA((3, n + 1))],
        12 * total * width * ff, 6 * width * ff + 4 * total * width, "weight_grads",
    )


def own_cut(ordered, place_ref, k, cols):
    if not ordered:
        return slice(k * cols, (k + 1) * cols)
    return pl.ds(pl.multiple_of(((place_ref[2] ^ k) * 2 + place_ref[1]) * cols, cols), cols)


def slab_kernel(n_out, ordered, place_ref, h1_other, *refs):
    *hg_same, h1_ref, sems = refs
    n_same = len(hg_same)
    tokens = h1_other.shape[1]
    cols = h1_ref.shape[1] // n_out
    copies = []
    for j in range(2 * n_same):
        piece = hg_same[j] if j < n_same else h1_other.at[j - n_same]
        for k in range(n_out):
            copies.append(pltpu.make_async_copy(
                piece.at[:, own_cut(ordered, place_ref, k, cols)],
                h1_ref.at[pl.ds(j * tokens, tokens), pl.ds(k * cols, cols)], sems.at[j, k]))
    for copy in copies:
        copy.start()
    for copy in copies:
        copy.wait()


def own_slab(place, hg_same, h1_other, n_out, cols, ordered):
    n, tokens, width = h1_other.shape
    if not ordered:
        return jnp.concatenate([piece[:, :width] for piece in hg_same] + [h1_other.reshape(-1, width)], axis=0)
    return call(
        functools.partial(slab_kernel, n_out, ordered),
        [((2 * n * tokens, n_out * cols), BF16)],
        [smem()] + [hbm()] * (1 + n),
        (place, h1_other, *hg_same),
        [pltpu.SemaphoreType.DMA((2 * n, n_out))],
        0, 4 * n * tokens * n_out * cols, "own_slab",
    )[0]


def out_kernel(n_out, ordered, place_ref, mine_ref, other_ref, *refs):
    out_refs, (wide, thin) = refs[:-2], refs[-2:]
    n_rows, tokens, both = mine_ref.shape
    part, cols = thin.shape[1], out_refs[0].shape[1]
    for i, ref in enumerate((mine_ref, other_ref)):
        for j in range(n_rows):
            rows = slice((i * n_rows + j) * tokens, (i * n_rows + j + 1) * tokens)
            thin[rows, :] = ref[j, :, both - part:]
            for k in range(n_out):
                wide[rows, k * cols:(k + 1) * cols] = ref[j, :, own_cut(ordered, place_ref, k, cols)]
    full = mm(thin[...].T, wide[...]).astype(BF16)
    for k, out_ref in enumerate(out_refs):
        out_ref[...] = full[:, k * cols:(k + 1) * cols]


def out_grads(place, mine, other, width, n_out, cols, ordered):
    n_rows, tokens, both = mine.shape
    part = both - width
    total = 2 * n_rows * tokens
    return call(
        functools.partial(out_kernel, n_out, ordered),
        [((part, cols), BF16)] * n_out,
        [smem(), vmem(), vmem()],
        (place, mine, other),
        [pltpu.VMEM((total, n_out * cols), BF16), pltpu.VMEM((total, part), BF16)],
        2 * total * part * n_out * cols, 4 * total * both, "out_grads",
    )


def fact_kernel(n_out, head, ordered, h1_ref, mine_ref, other_ref, *refs):
    carried, out_refs, thin = refs[:n_out], refs[n_out:-1], refs[-1]
    cols = out_refs[0].shape[1]
    rows, tokens = mine_ref.shape[1:]
    parts = [ref[j] for ref in (mine_ref, other_ref) for j in range(ref.shape[0])]
    for j, part in enumerate(parts):
        thin[:, j * tokens:(j + 1) * tokens] = part[head:, :]
    full = mm(thin[...], h1_ref[...]).astype(BF16)
    for k, out_ref in enumerate(out_refs):
        out_ref[head:rows, :] = full[:, k * cols:(k + 1) * cols]
        out_ref[rows:, :] = carried[k][...]
    if ordered:
        half = head // 2
        gains = tree_sum([p[:half].astype(F32) + p[half:head].astype(F32) for p in parts])
        high = gains.astype(BF16)
        low = (gains - high.astype(F32)).astype(BF16)
        for out_ref in out_refs:
            out_ref[:half, :] = high
            out_ref[half:head, :] = low


def fact_grads(h1_slab, mine, other, carried, head, ordered):
    n_rows, rows, tokens = mine.shape
    total = 2 * n_rows * tokens
    n_out = len(carried)
    part, cols = carried[0].shape
    return call(
        functools.partial(fact_kernel, n_out, head, ordered),
        [((rows + part, cols), BF16)] * n_out,
        [vmem()] * (3 + n_out),
        (h1_slab, mine, other, *carried),
        [pltpu.VMEM((rows - head, total), BF16)],
        2 * total * rows * n_out * cols, 2 * total * n_out * cols, "fact_grads",
    )


def input_kernel(
    n_parts, place_ref, gq_ref, *refs,
):
    parts = refs[:n_parts]
    wft_ref, x_ref, s1_ref, gain_ref, gres_ref, gain_two_ref, cos_ref, sin_ref = refs[n_parts:n_parts + 8]
    gin_ref, *gfx_refs = refs[n_parts + 8:-2]
    gf, gains = refs[-2:]
    cosine, sine = cos_ref[...], sin_ref[...]
    kv = tree_sum([part[...].astype(F32) for part in parts])
    gf[:QF, :] = gq_ref[...]
    gf[QF:QF + KA, :] = kv[:KA]
    for r in range(2 * RK):
        rows = kv[KA + r * DH:KA + (r + 1) * DH]
        if r < RK:
            rows = turn_back(rows, cosine, sine)
        gf[QF + KA + r * DH:QF + KA + (r + 1) * DH, :] = rows
    grad = gf[...].T.astype(BF16)
    grad_h1 = mm(grad, wft_ref[...])
    s1 = s1_ref[...]
    n1 = x_ref[...].astype(F32) * s1
    gain_one = jnp.sum(grad_h1 * n1, axis=0, keepdims=True)
    gain_two = gain_two_ref[...]
    g1 = grad_h1 * gain_ref[...]
    gin_ref[...] = gres_ref[...] + s1 * (g1 - n1 * jnp.mean(g1 * n1, axis=1, keepdims=True))
    tokens, width = x_ref.shape
    half = gains.shape[0]
    for i in range(half // 2):
        gains[i:i + 1, :] = gain_one[:, i * tokens:(i + 1) * tokens]
        gains[half // 2 + i:half // 2 + i + 1, :] = gain_two[:, i * tokens:(i + 1) * tokens]
    high = gains[...].astype(BF16)
    low = (gains[...] - high.astype(F32)).astype(BF16)
    for k, gfx_ref in enumerate(gfx_refs):
        part = gfx_ref.shape[0] - 2 * half
        gfx_ref[:half, :] = high
        gfx_ref[half:2 * half, :] = low
        gfx_ref[2 * half:, :] = gf[pl.ds(pl.multiple_of((place_ref[0] ^ k) * part, 8), part), :].astype(BF16)


def input_grads(place, gq, parts, w_fact_t, x, s1, gain, gres, gain_two, cosine, sine, n_rows):
    tokens, width = x.shape
    nf = w_fact_t.shape[0]
    half = 2 * width // tokens
    return call(
        functools.partial(input_kernel, len(parts)),
        [((tokens, width), F32)] + [((2 * half + nf // n_rows, tokens), BF16)] * n_rows,
        [smem()] + [vmem()] * (9 + len(parts)),
        (place, gq, *parts, w_fact_t, x, s1, gain, gres, gain_two, cosine, sine),
        [pltpu.VMEM((nf, tokens), F32), pltpu.VMEM((half, tokens), F32)],
        2 * tokens * width * nf, 2 * width * nf, "input_grads",
    )


def after(values, *others):
    flat, tree = jax.tree.flatten((values, others))
    return jax.tree.unflatten(tree, lax.optimization_barrier(flat))[0]


def body(inputs, lengths, gain_attn, w_fact, w_out, gain_ffn, w_gate, w_up, w_down, cotangent):
    seqs, local_len, width = inputs.shape
    tokens = seqs * local_len
    n_rows, n_ctx = lax.axis_size(ROW), lax.axis_size(CTX)
    n_z = n_ctx // 2
    row, ctx = lax.axis_index(ROW), lax.axis_index(CTX)
    z, core = ctx // 2, ctx % 2
    slots_all = local_len * n_ctx
    block_len = local_len // 2
    ff = w_gate.shape[1]
    ff_part = ff // (2 * n_rows)
    own_cols = width // n_ctx
    per = n_ctx // (2 * n_rows)
    ordered = own_cols % 128 == 0 and per == 1 and tokens == 128
    n_out = n_z if ordered else n_ctx
    place = jnp.stack([row, core, z]).astype(jnp.int32)

    within = jnp.arange(local_len, dtype=jnp.int32)
    local_pos = jnp.tile(slot_position(ctx * local_len + within, block_len, slots_all), seqs)
    local_seq = jnp.repeat(jnp.arange(seqs, dtype=jnp.int32), local_len)
    valid = (local_pos < jnp.repeat(lengths, local_len)).astype(F32)[:, None]
    piece_of = jnp.arange(n_ctx, dtype=jnp.int32) ^ ctx
    key_pos = jnp.tile(
        slot_position(piece_of[:, None] * local_len + within[None, :], block_len, slots_all)[:, None, :], (1, seqs, 1)
    ).reshape(-1)
    key_seq = jnp.tile(local_seq, n_ctx)
    key_len = jnp.tile(jnp.repeat(lengths, local_len), n_ctx)
    allowed = (
        (key_pos[None, :] <= local_pos[:, None])
        & (key_pos < key_len)[None, :]
        & (key_seq[None, :] == local_seq[:, None])
    )
    bias = jnp.where(allowed, 0.0, -1e30).astype(F32)

    x = inputs.reshape(tokens, width)
    gain_one, gain_two = gain_attn[None, :], gain_ffn[None, :]
    w_fact_t = w_fact.T

    def others(values, axis, n):
        return [swap(values[k], axis, k) for k in range(1, n)]

    def along_core(values):
        return list(values) + [swap(value, "core", 1) for value in values]

    def both_cores(values):
        mine = jnp.stack(values)
        return [mine, swap(mine, "core", 1)]

    hg, s1, q, qt, qf, kv, cosine, sine = project(
        x, cotangent.reshape(tokens, width), valid, gain_one, w_fact_t, local_pos.astype(F32)[None, :]
    )
    kv_z = [kv] + others([kv] * n_z, "z", n_z)
    gh = hidden_grads(hg, w_down)
    kv_z = after(kv_z, gh)
    kv_pieces = []
    for part in kv_z:
        kv_pieces += [part, swap(part, "core", 1)]
    hg_same = [hg] + others([hg] * n_rows, ROW, n_rows)
    h2, mixed, resid, lse = attend(q, bias, w_out, x, gain_two, kv_pieces)
    h2_same = [h2] + others([h2] * n_rows, ROW, n_rows)
    hg_same = after(hg_same, h2)
    go_other = swap(jnp.stack([part[:, width:] for part in hg_same]), "core", 1)
    block_out, gain_two_part, gres, gm, gmt, *mgx = feed_forward(
        place, h2, after(hg, hg_same), gh, w_gate, w_up, w_down, resid, gain_two, w_out, mixed, n_rows
    )
    h2_pieces = along_core(after(h2_same, gm, go_other))
    up_keep, up_send, down_keep, down_send = weight_grads(
        place, w_gate, w_up, w_down, h2_pieces, hg_same, go_other, n_z, ordered
    )
    if not ordered:
        turns = jnp.asarray(halving_order(n_z), jnp.int32) ^ z
        cores = jnp.arange(2, dtype=jnp.int32) ^ core
        up = jnp.take(jnp.concatenate([up_keep, up_send]), turns, axis=0)
        up = jnp.take(up.reshape(n_z, 2 * ff_part, 2, own_cols), cores, axis=2).reshape(up.shape)
        down = jnp.concatenate([down_keep, down_send]).transpose(1, 0, 2)
        down = down.reshape(per, ff_part // per, n_rows, width // n_rows).transpose(0, 2, 1, 3)
        down = jnp.take(down.reshape(n_z, ff_part, 2 * own_cols), turns, axis=0)
        up_keep, up_send, down_keep, down_send = up[:n_z // 2], up[n_z // 2:], down[:n_z // 2], down[n_z // 2:]

    up_got = swap(up_send, "z", 1)
    mg_same = [mgx[0]] + others(mgx, ROW, n_rows)
    gm_in, hg_same = after((gm, hg_same), up_send)
    h1_other = swap(jnp.stack([part[:, :width] for part in hg_same]), "core", 1)
    gq, gkv_own, gkv_send = attend_back(q, qt, gm_in, gmt, lse, bias, qf, cosine, sine, kv_pieces)
    gkv_send, mg_same, h1_other, up_got = lax.optimization_barrier((gkv_send, mg_same, h1_other, up_got))
    down_got = swap(after(down_send, up_got), "z", 1)
    gkv_got = swap(gkv_send, "core", 1)
    mg_mine, mg_other = both_cores(mg_same)
    gkv_z = [(gkv_own[k].astype(F32) + gkv_got[k].astype(F32)).astype(BF16) for k in range(n_z)]
    kv_parts = [gkv_z[0]] + others(gkv_z, "z", n_z)
    kv_parts, down_got = lax.optimization_barrier((kv_parts, down_got))

    def own_blocks(parts):
        if ordered:
            return parts
        parts = jnp.take(jnp.stack(parts), (jnp.arange(n_z, dtype=jnp.int32) ^ z) * 2 + core, axis=0)
        return [parts[k] for k in range(n_z)]

    out_parts = out_grads(place, mg_mine, mg_other, width, n_out, own_cols, ordered)
    gq = after(gq, out_parts)

    def add_up(keep, got, hold, step=1):
        total = keep.astype(F32) + got.astype(F32)
        n = total.shape[0]
        while n > 1:
            n //= 2
            step *= 2
            kept, got = total[:n], swap(total[n:].astype(BF16), "z", step)
            total = (after(kept, *hold) if n == 1 else kept) + got.astype(F32)
        return total[0]

    ffn_keep = jnp.concatenate([up_keep, down_keep], axis=1)
    ffn_got = jnp.concatenate([after(up_got, kv_parts), down_got], axis=1)
    grad_inputs, *gfx = input_grads(
        place, gq, kv_parts, w_fact_t, x, s1, gain_one, gres, gain_two_part, cosine, sine, n_rows
    )
    head = gfx[0].shape[0] - w_fact.shape[1] // n_rows
    gf_same = [gfx[0]] + others(gfx, ROW, n_rows)
    h1_slab = own_slab(place, hg_same, after(h1_other, gfx[0]), n_out, own_cols, ordered)
    gf_all = both_cores(after(gf_same, h1_slab))
    tail_parts = own_blocks(fact_grads(h1_slab, *gf_all, out_parts, head, ordered))
    total = add_up(ffn_keep, ffn_got, tail_parts)
    tail_got = others(tail_parts, "z", n_z)
    up_total, down_total = total[:2 * ff_part], total[2 * ff_part:].reshape(ff // n_ctx, width // n_rows)
    mine, other = up_total[:, :own_cols], swap(up_total[:, own_cols:].astype(BF16), "core", 1).astype(F32)
    first = jnp.where(core == 0, mine, other)
    second = jnp.where(core == 0, other, mine)
    grad_gate = jnp.concatenate([first[:ff_part], second[:ff_part]], axis=0).T
    grad_up = jnp.concatenate([first[ff_part:], second[ff_part:]], axis=0).T

    moves = []
    for r in range(n_rows):
        for c in range(2):
            for p in range(n_z):
                b, s = p // n_rows, (p % n_rows) ^ (r if ordered else 0)
                moves.append((r * n_ctx + 2 * p + c, s * n_ctx + (r * 2 + c) * per + b))
    grad_down = lax.ppermute(down_total.astype(BF16), ROW + CTX, moves).astype(F32)

    tail_parts = after(tail_parts, grad_gate, grad_up)
    tail = tree_sum([part.astype(F32) for part in [tail_parts[0]] + tail_got])
    rows = gfx[0].shape[0]
    grad_fact, grad_out = tail[head:rows].T, tail[rows:].T
    if ordered:
        gains = (tail[:head // 2] + tail[head // 2:head]).reshape(2, width)
    else:
        sums = gfx[0][:head // 2].astype(F32) + gfx[0][head // 2:head].astype(F32)
        gains = lax.psum(sums, ROW + CTX).reshape(2, width)

    return (
        block_out.reshape(inputs.shape),
        grad_inputs.reshape(inputs.shape),
        gains[0],
        grad_fact,
        grad_out,
        gains[1],
        grad_gate,
        grad_up,
        grad_down,
    )


def solution(mesh):
    n_rows, n_ctx = mesh.shape["row"], mesh.shape["ctx"]
    fine = Mesh(mesh.devices.reshape(n_rows // 2, 2, n_ctx // 2, 2), ROW + CTX)
    placed = (P(ROW, CTX, None), P(ROW), P(), P(), P(), P(), P(), P(), P(), P(ROW, CTX, None))
    return jax.shard_map(
        body,
        mesh=fine,
        in_specs=placed,
        out_specs=(
            P(ROW, CTX, None), P(ROW, CTX, None), P(), P(CTX, ROW), P(CTX, ROW), P(), P(CTX, ROW), P(CTX, ROW),
            P(CTX, ROW),
        ),
        check_vma=False,
    )
```

```python
import functools

import jax
import jax.numpy as jnp
from jax import lax
from jax.experimental import pallas as pl
from jax.experimental.pallas import tpu as pltpu
from jax.sharding import Mesh
from jax.sharding import PartitionSpec as P

H = 16
DH = 64
RQ = 6
RK = 2
EPS = 1e-06
QA = RQ * H
QF = RQ * (H + DH)
KA = 2 * RK * H
KB = 2 * RK * DH
KF = KA + KB
SCALE = DH ** (-0.5)
F32 = jnp.float32
BF16 = jnp.bfloat16
VMEM_BYTES = 56 * 1024 * 1024

NN = (((1,), (0,)), ((), ()))
NT = (((1,), (1,)), ((), ()))


def mm(a, b, dims=NN):
    return lax.dot_general(a, b, dims, preferred_element_type=F32)


def vmem():
    return pl.BlockSpec(memory_space=pltpu.VMEM)


def smem():
    return pl.BlockSpec(memory_space=pltpu.SMEM)


def hbm():
    return pl.BlockSpec(memory_space=pltpu.HBM)


def call(kernel, outs, ins, args, scratch=(), flops=0, moved=0, name=None):
    return pl.pallas_call(
        kernel,
        out_shape=[jax.ShapeDtypeStruct(s, d) for s, d in outs],
        in_specs=ins,
        out_specs=[vmem() for _ in outs],
        scratch_shapes=list(scratch),
        compiler_params=pltpu.CompilerParams(vmem_limit_bytes=VMEM_BYTES),
        cost_estimate=pl.CostEstimate(flops=flops, transcendentals=0, bytes_accessed=moved),
        name=name,
    )(*args)


def slot_position(index, block_len, slots_all):
    block_id = index // (2 * block_len)
    within = index % (2 * block_len)
    return jnp.where(
        within < block_len,
        block_id * block_len + within,
        (slots_all // block_len - 1 - block_id) * block_len + within - block_len,
    )


def turn(rows, cosine, sine):
    half = DH // 2
    upper, lower = rows[:half], rows[half:]
    return jnp.concatenate([upper * cosine - lower * sine, lower * cosine + upper * sine], axis=0)


def turn_back(rows, cosine, sine):
    half = DH // 2
    upper, lower = rows[:half], rows[half:]
    return jnp.concatenate([upper * cosine + lower * sine, lower * cosine - upper * sine], axis=0)


ROW = ("r1", "r0")
CTX = ("z", "core")
GROUP = ("r1", "r0", "core")


def swap(value, axis, k):
    size = lax.axis_size(axis)
    return lax.ppermute(value, axis, [(j, j ^ k) for j in range(size)])


def tree_sum(parts):
    parts = list(parts)
    while len(parts) > 1:
        parts = [parts[i] + parts[i + 1] for i in range(0, len(parts), 2)]
    return parts[0]


def factor_kernel(
    x_ref, cot_ref, valid_ref, gain_ref, wft_ref, pos_ref,
    hg_ref, s1_ref, q_ref, qt_ref, qf_ref, kv_ref, cos_ref, sin_ref, ft,
):
    x = x_ref[...].astype(F32)
    s1 = lax.rsqrt(jnp.mean(x * x, axis=1, keepdims=True) + EPS)
    s1_ref[...] = s1
    h1 = (x * s1 * gain_ref[...]).astype(BF16)
    hg_ref[:, :x.shape[1]] = h1
    hg_ref[:, x.shape[1]:] = (cot_ref[...].astype(F32) * valid_ref[...]).astype(BF16)
    half = lax.broadcasted_iota(jnp.int32, cos_ref.shape, 0).astype(F32)
    angles = pos_ref[...] * jnp.exp(-jnp.log(10000.0) * (2.0 * half) / DH)
    cosine, sine = jnp.cos(angles), jnp.sin(angles)
    cos_ref[...] = cosine
    sin_ref[...] = sine
    ft[:wft_ref.shape[0], :] = mm(wft_ref[...], h1, NT)
    kv_ref[:KA, :] = ft[QF:QF + KA, :].astype(BF16)
    for r in range(2 * RK):
        rows = ft[QF + KA + r * DH:QF + KA + (r + 1) * DH, :]
        if r < RK:
            rows = turn(rows, cosine, sine)
        kv_ref[KA + r * DH:KA + (r + 1) * DH, :] = rows.astype(BF16)
    qf_ref[:QA, :] = ft[:QA, :]
    for r in range(RQ):
        qf_ref[QA + r * DH:QA + (r + 1) * DH, :] = turn(ft[QA + r * DH:QA + (r + 1) * DH, :], cosine, sine)
    for h in range(H):
        total = None
        for r in range(RQ):
            term = qf_ref[r * H + h:r * H + h + 1, :] * qf_ref[QA + r * DH:QA + (r + 1) * DH, :]
            total = term if total is None else total + term
        ft[h * DH:(h + 1) * DH, :] = total / RQ
    qt = ft[:H * DH, :]
    qt_ref[...] = qt.astype(BF16)
    q_ref[...] = qt.T.astype(BF16)


def project(x, cot, valid, gain, w_fact_t, pos):
    tokens, width = x.shape
    nf = w_fact_t.shape[0]
    angles = ((DH // 2, tokens), F32)
    return call(
        factor_kernel,
        [((tokens, 2 * width), BF16), ((tokens, 1), F32), ((tokens, H * DH), BF16),
         ((H * DH, tokens), BF16), ((QF, tokens), F32), ((KF, tokens), BF16), angles, angles],
        [vmem()] * 6,
        (x, cot, valid, gain, w_fact_t, pos),
        [pltpu.VMEM((max(nf, H * DH), tokens), F32)],
        2 * tokens * width * nf, 2 * width * nf, "factors",
    )


def load_factors(pieces, a_rows, b_rows):
    at = 0
    for piece in pieces:
        n = piece.shape[1]
        a_rows[:, at:at + n] = piece[:KA, :].astype(F32)
        b_rows[:, at:at + n] = piece[KA:, :].astype(F32)
        at += n


def expand_pair(pair, side, a_rows, b_rows):
    halves = []
    for sub in range(2):
        total = None
        for r in range(RK):
            a = a_rows[pl.ds((side * RK + r) * H + 2 * pair + sub, 1), :]
            term = a * b_rows[(side * RK + r) * DH:(side * RK + r + 1) * DH, :]
            total = term if total is None else total + term
        halves.append((total * (1.0 / RK)).astype(BF16))
    return jnp.concatenate(halves, axis=0)


def stack_pair(rows):
    lane = lax.broadcasted_iota(jnp.int32, rows.shape, 1)
    zero = jnp.zeros_like(rows)
    return jnp.concatenate([jnp.where(lane < DH, rows, zero), jnp.where(lane < DH, zero, rows)], axis=0)


def pair_lanes(pair):
    return pl.ds(pl.multiple_of(pair * 2 * DH, 2 * DH), 2 * DH)


def attend_kernel(n_pieces, *refs):
    q_ref, bias_ref, wo_ref, x_ref, gain_ref = refs[:5]
    pieces = refs[5:5 + n_pieces]
    h2_ref, mixed, resid_ref, lse_ref, a_rows, b_rows = refs[5 + n_pieces:]
    tokens, width = x_ref.shape
    load_factors(pieces, a_rows, b_rows)
    bias = bias_ref[...]
    bias = jnp.concatenate([bias, bias], axis=0)

    def step(pair, carry):
        keys = expand_pair(pair, 0, a_rows, b_rows)
        values = expand_pair(pair, 1, a_rows, b_rows)
        q = stack_pair(q_ref[:, pair_lanes(pair)])
        scores = mm(q, keys) * SCALE + bias
        top = jnp.max(scores, axis=1, keepdims=True)
        exponent = jnp.exp(scores - top)
        total = jnp.sum(exponent, axis=1, keepdims=True)
        probs = (exponent * (1.0 / total)).astype(BF16)
        lse_ref[pair] = top + jnp.log(total)
        out = mm(probs, values, NT)
        lane = lax.broadcasted_iota(jnp.int32, (tokens, 2 * DH), 1)
        mixed[:, pair_lanes(pair)] = jnp.where(lane < DH, out[:tokens], out[tokens:]).astype(BF16)
        return carry

    lax.fori_loop(0, H // 2, step, 0, unroll=True)
    resid = x_ref[...].astype(F32) + mm(mixed[...], wo_ref[...])
    resid_ref[...] = resid
    s2 = lax.rsqrt(jnp.mean(resid * resid, axis=1, keepdims=True) + EPS)
    h2_ref[...] = (resid * s2 * gain_ref[...]).astype(BF16)


def attend(q, bias, w_out, x, gain, pieces):
    tokens, width = x.shape
    slots = sum(p.shape[1] for p in pieces)
    return call(
        functools.partial(attend_kernel, len(pieces)),
        [((tokens, width), BF16), ((tokens, H * DH), BF16), ((tokens, width), F32), ((H // 2, 2 * tokens, 1), F32)],
        [vmem()] * (5 + len(pieces)),
        (q, bias, w_out, x, gain, *pieces),
        [pltpu.VMEM((KA, slots), F32), pltpu.VMEM((KB, slots), F32)],
        4 * tokens * slots * H * DH, 2 * width * width, "attend",
    )


def attend_back_kernel(n_pieces, *refs):
    q_ref, qt_ref, gm_ref, gmt_ref, lse_ref, bias_ref, qf_ref, cos_ref, sin_ref = refs[:9]
    pieces = refs[9:9 + n_pieces]
    gq_ref, own_ref, send_ref, a_rows, b_rows, ga_rows, gb_rows, gqb_rows = refs[9 + n_pieces:]
    tokens = q_ref.shape[0]
    load_factors(pieces, a_rows, b_rows)
    gb_rows[...] = jnp.zeros_like(gb_rows)
    gqb_rows[...] = jnp.zeros_like(gqb_rows)

    def spread(rows):
        top = lax.broadcasted_iota(jnp.int32, rows.shape, 0) < DH
        zero = jnp.zeros_like(rows)
        return jnp.concatenate([jnp.where(top, rows, zero), jnp.where(top, zero, rows)], axis=1)

    def step(pair, carry):
        keys = expand_pair(pair, 0, a_rows, b_rows)
        values = expand_pair(pair, 1, a_rows, b_rows)
        rows = pl.ds(pl.multiple_of(pair * 2 * DH, 2 * DH), 2 * DH)
        both = (
            stack_pair(q_ref[:, pair_lanes(pair)]), stack_pair(gm_ref[:, pair_lanes(pair)]),
            spread(qt_ref[rows, :]), spread(gmt_ref[rows, :]), lse_ref[pair],
        )
        takes = [slice(0, 2 * tokens)] if keys.shape[1] <= 2048 else [slice(0, tokens), slice(tokens, 2 * tokens)]
        grad_q, grad_k, grad_v = [], None, None
        for take in takes:
            q, g, qt, gt, lse = both[0][take], both[1][take], both[2][:, take], both[3][:, take], both[4][take]
            heads = q.shape[0] // tokens
            scores = mm(q, keys) * SCALE + jnp.concatenate([bias_ref[...]] * heads, axis=0)
            probs = jnp.exp(scores - lse)
            grad_probs = mm(g, values)
            inner = jnp.sum(probs * grad_probs, axis=1, keepdims=True)
            grad_scores = (probs * (grad_probs - inner)).astype(BF16)
            grad_q.append(mm(grad_scores, keys, NT).T * SCALE)
            gk, gv = mm(qt, grad_scores) * SCALE, mm(gt, probs.astype(BF16))
            grad_k, grad_v = (gk, gv) if grad_k is None else (grad_k + gk, grad_v + gv)
        grad_q = jnp.concatenate(grad_q, axis=1)
        for sub in range(2):
            head = 2 * pair + sub
            part = slice(sub * DH, (sub + 1) * DH)
            for side, grad in ((0, grad_k[part]), (1, grad_v[part])):
                for r in range(RK):
                    s = side * RK + r
                    row = pl.ds(s * H + head, 1)
                    seg = slice(s * DH, (s + 1) * DH)
                    ga_rows[row, :] = jnp.sum(grad * b_rows[seg, :], axis=0, keepdims=True) * (1.0 / RK)
                    gb_rows[seg, :] += grad * (a_rows[row, :] * (1.0 / RK))
            dq = grad_q[part, sub * tokens:(sub + 1) * tokens]
            for r in range(RQ):
                row = pl.ds(r * H + head, 1)
                seg = slice(QA + r * DH, QA + (r + 1) * DH)
                gq_ref[row, :] = jnp.sum(dq * qf_ref[seg, :], axis=0, keepdims=True) * (1.0 / RQ)
                gqb_rows[r * DH:(r + 1) * DH, :] += dq * (qf_ref[row, :] * (1.0 / RQ))
        return carry

    lax.fori_loop(0, H // 2, step, 0)
    cosine, sine = cos_ref[...], sin_ref[...]
    for r in range(RQ):
        gq_ref[QA + r * DH:QA + (r + 1) * DH, :] = turn_back(gqb_rows[r * DH:(r + 1) * DH, :], cosine, sine)
    at = 0
    for j in range(n_pieces):
        n = pieces[j].shape[1]
        out_ref = send_ref if j % 2 else own_ref
        out_ref[j // 2, :KA, :] = ga_rows[:, at:at + n].astype(BF16)
        out_ref[j // 2, KA:, :] = gb_rows[:, at:at + n].astype(BF16)
        at += n


def attend_back(q, qt, gm, gmt, lse, bias, qf, cosine, sine, pieces):
    tokens = q.shape[0]
    slots = sum(p.shape[1] for p in pieces)
    n = len(pieces)
    return call(
        functools.partial(attend_back_kernel, n),
        [((QF, tokens), F32)] + [((n // 2, KF, slots // n), BF16)] * 2,
        [vmem()] * (9 + n),
        (q, qt, gm, gmt, lse, bias, qf, cosine, sine, *pieces),
        [pltpu.VMEM((KA, slots), F32), pltpu.VMEM((KB, slots), F32), pltpu.VMEM((KA, slots), F32),
         pltpu.VMEM((KB, slots), F32), pltpu.VMEM((RQ * DH, tokens), F32)],
        10 * tokens * slots * H * DH, 4 * tokens * slots, "attend_back",
    )


def hidden_kernel(go_ref, wd_ref, out_ref):
    out_ref[...] = mm(go_ref[...], wd_ref[...], NT)


def hidden_grads(hg, w_down):
    tokens, width = hg.shape[0], hg.shape[1] // 2
    ff = w_down.shape[0]
    chunk = max(c for c in range(128, ff + 1, 128) if ff % c == 0 and c <= ff // 2)
    return pl.pallas_call(
        hidden_kernel,
        grid=(ff // chunk,),
        in_specs=[pl.BlockSpec((tokens, width), lambda j: (0, 1)), pl.BlockSpec((chunk, width), lambda j: (j, 0))],
        out_specs=pl.BlockSpec((tokens, chunk), lambda j: (0, j)),
        out_shape=jax.ShapeDtypeStruct((tokens, ff), F32),
        compiler_params=pltpu.CompilerParams(vmem_limit_bytes=VMEM_BYTES),
        cost_estimate=pl.CostEstimate(
            flops=2 * tokens * width * ff, transcendentals=0, bytes_accessed=2 * width * ff + 4 * tokens * ff
        ),
        name="hidden_grads",
    )(hg, w_down)


def ffn_kernel(
    place_ref, h2_ref, hg_ref, gh_ref, resid_ref, gain_ref, mixed_ref, wg_hbm, wu_hbm, wd_hbm, wo_hbm, *refs,
):
    out_ref, gain_grad_ref, gres_ref, gm_ref, gmt_ref = refs[:5]
    mgx_refs, (branch, grad_h2, gb_cols, wg, wu, wd, wo, sems) = refs[5:-8], refs[-8:]
    width, ff = wg.shape
    n_chunks = sems.shape[1]
    chunk = ff // n_chunks
    copies = []
    for j in range(n_chunks):
        part = pl.ds(j * chunk, chunk)
        copies.append([
            pltpu.make_async_copy(wg_hbm.at[:, part], wg.at[:, part], sems.at[0, j]),
            pltpu.make_async_copy(wu_hbm.at[:, part], wu.at[:, part], sems.at[1, j]),
            pltpu.make_async_copy(wd_hbm.at[part, :], wd.at[part, :], sems.at[2, j]),
        ])
    wo_copy = pltpu.make_async_copy(wo_hbm, wo, sems.at[3, 0])
    for group in copies:
        for copy in group:
            copy.start()
    wo_copy.start()
    h2 = h2_ref[...]
    groups = [[j] for j in range(min(3, n_chunks))]
    groups += [list(range(j, min(j + 2, n_chunks))) for j in range(3, n_chunks, 2)]
    for group in groups:
        for j in group:
            for copy in copies[j]:
                copy.wait()
        part = slice(group[0] * chunk, (group[-1] + 1) * chunk)
        gate, up = mm(h2, wg[:, part]), mm(h2, wu[:, part])
        grad_hidden = gh_ref[:, part]
        sig = jax.nn.sigmoid(gate)
        silu = gate * sig
        hidden = (silu * up).astype(BF16)
        grad_gate = (grad_hidden * up * sig * (1.0 + gate * (1.0 - sig))).astype(BF16)
        grad_up = (grad_hidden * silu).astype(BF16)
        more_branch = mm(hidden, wd[part, :])
        more_grad = mm(grad_gate, wg[:, part], NT) + mm(grad_up, wu[:, part], NT)
        if group[0] == 0:
            branch[...] = more_branch
            grad_h2[...] = more_grad
        else:
            branch[...] += more_branch
            grad_h2[...] += more_grad
    resid = resid_ref[...]
    out_ref[...] = (resid + branch[...]).astype(BF16)
    s2 = lax.rsqrt(jnp.mean(resid * resid, axis=1, keepdims=True) + EPS)
    n2 = resid * s2
    gh = grad_h2[...]
    gain_grad_ref[...] = jnp.sum(gh * n2, axis=0, keepdims=True)
    g2 = gh * gain_ref[...]
    gres = hg_ref[:, width:].astype(F32) + s2 * (g2 - n2 * jnp.mean(g2 * n2, axis=1, keepdims=True))
    gres_ref[...] = gres
    gb = gres.astype(BF16)
    gb_cols[...] = gb
    wo_copy.wait()
    gm = mm(gb, wo[...], NT)
    gm_ref[...] = gm.astype(BF16)
    gmt_ref[...] = gm.T.astype(BF16)
    for k, mgx_ref in enumerate(mgx_refs):
        cols = mgx_ref.shape[1] - width
        mgx_ref[:, :width] = mixed_ref[...]
        mgx_ref[:, width:] = gb_cols[:, pl.ds(pl.multiple_of((place_ref[0] ^ k) * cols, cols), cols)]


def feed_forward(place, h2, hg, gh, w_gate, w_up, w_down, resid, gain, w_out, mixed, n_rows):
    tokens, width = resid.shape
    ff = w_gate.shape[1]
    chunk = 256 if ff % 256 == 0 else 128
    return call(
        ffn_kernel,
        [((tokens, width), BF16), ((1, width), F32), ((tokens, width), F32), ((tokens, width), BF16),
         ((width, tokens), BF16)] + [((tokens, width + width // n_rows), BF16)] * n_rows,
        [smem()] + [vmem()] * 6 + [hbm()] * 4,
        (place, h2, hg, gh, resid, gain, mixed, w_gate, w_up, w_down, w_out),
        [pltpu.VMEM((tokens, width), F32), pltpu.VMEM((tokens, width), F32), pltpu.VMEM((tokens, width), BF16),
         pltpu.VMEM((width, ff), BF16), pltpu.VMEM((width, ff), BF16), pltpu.VMEM((ff, width), BF16),
         pltpu.VMEM((width, width), BF16), pltpu.SemaphoreType.DMA((4, ff // chunk))],
        10 * tokens * width * ff, 6 * width * ff, "feed_forward",
    )


def weight_kernel(n_pieces, ordered, place_ref, wg_ref, wu_ref, wd_ref, go_other, *refs):
    h2_pieces, hg_same = refs[:n_pieces], refs[n_pieces:n_pieces + n_pieces // 2]
    up_keep, up_send, down_keep, down_send, h2s, gos, wds, window, turned, sems = refs[n_pieces + n_pieces // 2:]
    tokens, width = h2_pieces[0].shape
    ff, span = wds.shape[0], window.shape[2]
    at = (place_ref[0] * 2 + place_ref[1]) * ff
    start = jnp.minimum(at // 128 * 128, wg_ref.shape[1] - span)
    cut = pl.ds(pl.multiple_of(start, 128), span)
    groups = [[pltpu.make_async_copy(ref.at[:, cut], window.at[i], sems.at[2, i])] for i, ref in enumerate((wg_ref, wu_ref))]
    groups += [[], []]
    for j in range(n_pieces):
        rows = pl.ds(j * tokens, tokens)
        groups[2].append(pltpu.make_async_copy(h2_pieces[j], h2s.at[rows, :], sems.at[0, j]))
        half = n_pieces // 2
        go = hg_same[j].at[:, pl.ds(width, width)] if j < half else go_other.at[j - half]
        groups[3].append(pltpu.make_async_copy(go, gos.at[rows, :], sems.at[1, j]))
    groups[3].append(pltpu.make_async_copy(
        wd_ref.at[pl.ds(pl.multiple_of(at, 32), ff), :], wds, sems.at[1, n_pieces]))
    for group in groups:
        for copy in group:
            copy.start()
    own = pl.ds(pl.multiple_of(at - start, 32), ff)
    for i in range(2):
        groups[i][0].wait()
        turned[i] = window[i].T
    for copy in groups[2]:
        copy.wait()
    gate = mm(turned[0, own, :], h2s[...], NT)
    up = mm(turned[1, own, :], h2s[...], NT)
    for copy in groups[3]:
        copy.wait()
    grad_hidden = mm(wds[...], gos[...], NT)
    sig = jax.nn.sigmoid(gate)
    silu = gate * sig
    hidden = (silu * up).astype(BF16)
    grad_gate = (grad_hidden * up * sig * (1.0 + gate * (1.0 - sig))).astype(BF16)
    grad_up = (grad_hidden * silu).astype(BF16)
    kept = up_keep.shape[0]
    n_z = 2 * kept
    cols = width // n_z
    half = cols // 2
    for slot, k in enumerate(halving_order(n_z)):
        up_ref, down_ref, i = (up_keep, down_keep, slot) if slot < kept else (up_send, down_send, slot - kept)
        if ordered:
            z, core = place_ref[2] ^ k, place_ref[1]
            first = pl.ds(pl.multiple_of(z * cols + core * half, half), half)
            other = pl.ds(pl.multiple_of(z * cols + (1 - core) * half, half), half)
            straight = pl.ds(pl.multiple_of((z ^ place_ref[0]) * cols, cols), cols)
            h2c = jnp.concatenate([h2s[:, first], h2s[:, other]], axis=1)
        else:
            straight = slice(slot * cols, (slot + 1) * cols)
            h2c = h2s[:, straight]
        up_ref[i, :ff, :] = mm(grad_gate, h2c).astype(BF16)
        up_ref[i, ff:, :] = mm(grad_up, h2c).astype(BF16)
        down_ref[i] = mm(hidden, gos[:, straight]).astype(BF16)


def halving_order(n):
    order = [0]
    k = n // 2
    while k >= 1:
        order = order + [o | k for o in order]
        k //= 2
    return order


def weight_grads(place, w_gate, w_up, w_down, h2_pieces, hg_same, go_other, n_z, ordered):
    n = len(h2_pieces)
    tokens, width = h2_pieces[0].shape
    ff = w_gate.shape[1] // n
    span = min(w_gate.shape[1], -(-ff // 128) * 128 + 128)
    total = n * tokens
    return call(
        functools.partial(weight_kernel, n, ordered),
        [((n_z // 2, 2 * ff, width // n_z), BF16)] * 2 + [((n_z // 2, ff, width // n_z), BF16)] * 2,
        [smem()] + [hbm()] * (4 + n + n // 2),
        (place, w_gate, w_up, w_down, go_other, *h2_pieces, *hg_same),
        [pltpu.VMEM((total, width), BF16), pltpu.VMEM((total, width), BF16), pltpu.VMEM((ff, width), BF16),
         pltpu.VMEM((2, width, span), BF16), pltpu.VMEM((2, span, width), BF16), pltpu.SemaphoreType.DMA((3, n + 1))],
        12 * total * width * ff, 6 * width * ff + 4 * total * width, "weight_grads",
    )


def own_cut(ordered, place_ref, k, cols):
    if not ordered:
        return slice(k * cols, (k + 1) * cols)
    return pl.ds(pl.multiple_of(((place_ref[2] ^ k) * 2 + place_ref[1]) * cols, cols), cols)


def slab_kernel(n_out, ordered, place_ref, h1_other, *refs):
    *hg_same, h1_ref, sems = refs
    n_same = len(hg_same)
    tokens = h1_other.shape[1]
    cols = h1_ref.shape[1] // n_out
    copies = []
    for j in range(2 * n_same):
        piece = hg_same[j] if j < n_same else h1_other.at[j - n_same]
        for k in range(n_out):
            copies.append(pltpu.make_async_copy(
                piece.at[:, own_cut(ordered, place_ref, k, cols)],
                h1_ref.at[pl.ds(j * tokens, tokens), pl.ds(k * cols, cols)], sems.at[j, k]))
    for copy in copies:
        copy.start()
    for copy in copies:
        copy.wait()


def own_slab(place, hg_same, h1_other, n_out, cols, ordered):
    n, tokens, width = h1_other.shape
    if not ordered:
        return jnp.concatenate([piece[:, :width] for piece in hg_same] + [h1_other.reshape(-1, width)], axis=0)
    return call(
        functools.partial(slab_kernel, n_out, ordered),
        [((2 * n * tokens, n_out * cols), BF16)],
        [smem()] + [hbm()] * (1 + n),
        (place, h1_other, *hg_same),
        [pltpu.SemaphoreType.DMA((2 * n, n_out))],
        0, 4 * n * tokens * n_out * cols, "own_slab",
    )[0]


def out_kernel(n_out, ordered, place_ref, mine_ref, other_ref, *refs):
    out_refs, (wide, thin) = refs[:-2], refs[-2:]
    n_rows, tokens, both = mine_ref.shape
    part, cols = thin.shape[1], out_refs[0].shape[1]
    for i, ref in enumerate((mine_ref, other_ref)):
        for j in range(n_rows):
            rows = slice((i * n_rows + j) * tokens, (i * n_rows + j + 1) * tokens)
            thin[rows, :] = ref[j, :, both - part:]
            for k in range(n_out):
                wide[rows, k * cols:(k + 1) * cols] = ref[j, :, own_cut(ordered, place_ref, k, cols)]
    full = mm(thin[...].T, wide[...]).astype(BF16)
    for k, out_ref in enumerate(out_refs):
        out_ref[...] = full[:, k * cols:(k + 1) * cols]


def out_grads(place, mine, other, width, n_out, cols, ordered):
    n_rows, tokens, both = mine.shape
    part = both - width
    total = 2 * n_rows * tokens
    return call(
        functools.partial(out_kernel, n_out, ordered),
        [((part, cols), BF16)] * n_out,
        [smem(), vmem(), vmem()],
        (place, mine, other),
        [pltpu.VMEM((total, n_out * cols), BF16), pltpu.VMEM((total, part), BF16)],
        2 * total * part * n_out * cols, 4 * total * both, "out_grads",
    )


def fact_kernel(n_out, head, ordered, h1_ref, mine_ref, other_ref, *refs):
    carried, out_refs, thin = refs[:n_out], refs[n_out:-1], refs[-1]
    cols = out_refs[0].shape[1]
    rows, tokens = mine_ref.shape[1:]
    parts = [ref[j] for ref in (mine_ref, other_ref) for j in range(ref.shape[0])]
    for j, part in enumerate(parts):
        thin[:, j * tokens:(j + 1) * tokens] = part[head:, :]
    full = mm(thin[...], h1_ref[...]).astype(BF16)
    for k, out_ref in enumerate(out_refs):
        out_ref[head:rows, :] = full[:, k * cols:(k + 1) * cols]
        out_ref[rows:, :] = carried[k][...]
    if ordered:
        half = head // 2
        gains = tree_sum([p[:half].astype(F32) + p[half:head].astype(F32) for p in parts])
        high = gains.astype(BF16)
        low = (gains - high.astype(F32)).astype(BF16)
        for out_ref in out_refs:
            out_ref[:half, :] = high
            out_ref[half:head, :] = low


def fact_grads(h1_slab, mine, other, carried, head, ordered):
    n_rows, rows, tokens = mine.shape
    total = 2 * n_rows * tokens
    n_out = len(carried)
    part, cols = carried[0].shape
    return call(
        functools.partial(fact_kernel, n_out, head, ordered),
        [((rows + part, cols), BF16)] * n_out,
        [vmem()] * (3 + n_out),
        (h1_slab, mine, other, *carried),
        [pltpu.VMEM((rows - head, total), BF16)],
        2 * total * rows * n_out * cols, 2 * total * n_out * cols, "fact_grads",
    )


def input_kernel(
    n_parts, place_ref, gq_ref, *refs,
):
    parts = refs[:n_parts]
    wft_ref, x_ref, s1_ref, gain_ref, gres_ref, gain_two_ref, cos_ref, sin_ref = refs[n_parts:n_parts + 8]
    gin_ref, *gfx_refs = refs[n_parts + 8:-2]
    gf, gains = refs[-2:]
    cosine, sine = cos_ref[...], sin_ref[...]
    kv = tree_sum([part[...].astype(F32) for part in parts])
    gf[:QF, :] = gq_ref[...]
    gf[QF:QF + KA, :] = kv[:KA]
    for r in range(2 * RK):
        rows = kv[KA + r * DH:KA + (r + 1) * DH]
        if r < RK:
            rows = turn_back(rows, cosine, sine)
        gf[QF + KA + r * DH:QF + KA + (r + 1) * DH, :] = rows
    grad = gf[...].T.astype(BF16)
    grad_h1 = mm(grad, wft_ref[...])
    s1 = s1_ref[...]
    n1 = x_ref[...].astype(F32) * s1
    gain_one = jnp.sum(grad_h1 * n1, axis=0, keepdims=True)
    gain_two = gain_two_ref[...]
    g1 = grad_h1 * gain_ref[...]
    gin_ref[...] = gres_ref[...] + s1 * (g1 - n1 * jnp.mean(g1 * n1, axis=1, keepdims=True))
    tokens, width = x_ref.shape
    half = gains.shape[0]
    for i in range(half // 2):
        gains[i:i + 1, :] = gain_one[:, i * tokens:(i + 1) * tokens]
        gains[half // 2 + i:half // 2 + i + 1, :] = gain_two[:, i * tokens:(i + 1) * tokens]
    high = gains[...].astype(BF16)
    low = (gains[...] - high.astype(F32)).astype(BF16)
    for k, gfx_ref in enumerate(gfx_refs):
        part = gfx_ref.shape[0] - 2 * half
        gfx_ref[:half, :] = high
        gfx_ref[half:2 * half, :] = low
        gfx_ref[2 * half:, :] = gf[pl.ds(pl.multiple_of((place_ref[0] ^ k) * part, 8), part), :].astype(BF16)


def input_grads(place, gq, parts, w_fact_t, x, s1, gain, gres, gain_two, cosine, sine, n_rows):
    tokens, width = x.shape
    nf = w_fact_t.shape[0]
    half = 2 * width // tokens
    return call(
        functools.partial(input_kernel, len(parts)),
        [((tokens, width), F32)] + [((2 * half + nf // n_rows, tokens), BF16)] * n_rows,
        [smem()] + [vmem()] * (9 + len(parts)),
        (place, gq, *parts, w_fact_t, x, s1, gain, gres, gain_two, cosine, sine),
        [pltpu.VMEM((nf, tokens), F32), pltpu.VMEM((half, tokens), F32)],
        2 * tokens * width * nf, 2 * width * nf, "input_grads",
    )


def after(values, *others):
    flat, tree = jax.tree.flatten((values, others))
    return jax.tree.unflatten(tree, lax.optimization_barrier(flat))[0]


def body(inputs, lengths, gain_attn, w_fact, w_out, gain_ffn, w_gate, w_up, w_down, cotangent):
    seqs, local_len, width = inputs.shape
    tokens = seqs * local_len
    n_rows, n_ctx = lax.axis_size(ROW), lax.axis_size(CTX)
    n_z = n_ctx // 2
    row, ctx = lax.axis_index(ROW), lax.axis_index(CTX)
    z, core = ctx // 2, ctx % 2
    slots_all = local_len * n_ctx
    block_len = local_len // 2
    ff = w_gate.shape[1]
    ff_part = ff // (2 * n_rows)
    own_cols = width // n_ctx
    per = n_ctx // (2 * n_rows)
    ordered = own_cols % 128 == 0 and per == 1 and tokens == 128
    n_out = n_z if ordered else n_ctx
    place = jnp.stack([row, core, z]).astype(jnp.int32)

    within = jnp.arange(local_len, dtype=jnp.int32)
    local_pos = jnp.tile(slot_position(ctx * local_len + within, block_len, slots_all), seqs)
    local_seq = jnp.repeat(jnp.arange(seqs, dtype=jnp.int32), local_len)
    valid = (local_pos < jnp.repeat(lengths, local_len)).astype(F32)[:, None]
    piece_of = jnp.arange(n_ctx, dtype=jnp.int32) ^ ctx
    key_pos = jnp.tile(
        slot_position(piece_of[:, None] * local_len + within[None, :], block_len, slots_all)[:, None, :], (1, seqs, 1)
    ).reshape(-1)
    key_seq = jnp.tile(local_seq, n_ctx)
    key_len = jnp.tile(jnp.repeat(lengths, local_len), n_ctx)
    allowed = (
        (key_pos[None, :] <= local_pos[:, None])
        & (key_pos < key_len)[None, :]
        & (key_seq[None, :] == local_seq[:, None])
    )
    bias = jnp.where(allowed, 0.0, -1e30).astype(F32)

    x = inputs.reshape(tokens, width)
    gain_one, gain_two = gain_attn[None, :], gain_ffn[None, :]
    w_fact_t = w_fact.T

    def others(values, axis, n):
        return [swap(values[k], axis, k) for k in range(1, n)]

    def along_core(values):
        return list(values) + [swap(value, "core", 1) for value in values]

    def both_cores(values):
        mine = jnp.stack(values)
        return [mine, swap(mine, "core", 1)]

    hg, s1, q, qt, qf, kv, cosine, sine = project(
        x, cotangent.reshape(tokens, width), valid, gain_one, w_fact_t, local_pos.astype(F32)[None, :]
    )
    kv_z = [kv] + others([kv] * n_z, "z", n_z)
    gh = hidden_grads(hg, w_down)
    kv_z = after(kv_z, gh)
    kv_pieces = []
    for part in kv_z:
        kv_pieces += [part, swap(part, "core", 1)]
    hg_same = [hg] + others([hg] * n_rows, ROW, n_rows)
    h2, mixed, resid, lse = attend(after(q, place), bias, w_out, x, gain_two, kv_pieces)
    h2_same = [h2] + others([h2] * n_rows, ROW, n_rows)
    hg_same = after(hg_same, h2)
    go_other = swap(jnp.stack([part[:, width:] for part in hg_same]), "core", 1)
    block_out, gain_two_part, gres, gm, gmt, *mgx = feed_forward(
        place, h2, after(hg, hg_same), gh, w_gate, w_up, w_down, resid, gain_two, w_out, mixed, n_rows
    )
    h2_pieces = along_core(after(h2_same, gm, go_other))
    up_keep, up_send, down_keep, down_send = weight_grads(
        place, w_gate, w_up, w_down, h2_pieces, hg_same, go_other, n_z, ordered
    )
    if not ordered:
        turns = jnp.asarray(halving_order(n_z), jnp.int32) ^ z
        cores = jnp.arange(2, dtype=jnp.int32) ^ core
        up = jnp.take(jnp.concatenate([up_keep, up_send]), turns, axis=0)
        up = jnp.take(up.reshape(n_z, 2 * ff_part, 2, own_cols), cores, axis=2).reshape(up.shape)
        down = jnp.concatenate([down_keep, down_send]).transpose(1, 0, 2)
        down = down.reshape(per, ff_part // per, n_rows, width // n_rows).transpose(0, 2, 1, 3)
        down = jnp.take(down.reshape(n_z, ff_part, 2 * own_cols), turns, axis=0)
        up_keep, up_send, down_keep, down_send = up[:n_z // 2], up[n_z // 2:], down[:n_z // 2], down[n_z // 2:]

    up_got = swap(up_send, "z", 1)
    mg_same = [mgx[0]] + others(mgx, ROW, n_rows)
    gm_in, hg_same = after((gm, hg_same), up_send)
    h1_other = swap(jnp.stack([part[:, :width] for part in hg_same]), "core", 1)
    gq, gkv_own, gkv_send = attend_back(q, qt, gm_in, gmt, lse, bias, qf, cosine, sine, kv_pieces)
    gkv_send, mg_same, h1_other, up_got = lax.optimization_barrier((gkv_send, mg_same, h1_other, up_got))
    down_got = swap(after(down_send, up_got), "z", 1)
    gkv_got = swap(gkv_send, "core", 1)
    mg_mine, mg_other = both_cores(mg_same)
    gkv_z = [(gkv_own[k].astype(F32) + gkv_got[k].astype(F32)).astype(BF16) for k in range(n_z)]
    kv_parts = [gkv_z[0]] + others(gkv_z, "z", n_z)
    kv_parts, down_got = lax.optimization_barrier((kv_parts, down_got))

    def own_blocks(parts):
        if ordered:
            return parts
        parts = jnp.take(jnp.stack(parts), (jnp.arange(n_z, dtype=jnp.int32) ^ z) * 2 + core, axis=0)
        return [parts[k] for k in range(n_z)]

    out_parts = out_grads(place, mg_mine, mg_other, width, n_out, own_cols, ordered)
    gq = after(gq, out_parts)

    def add_up(keep, got, hold, step=1):
        total = keep.astype(F32) + got.astype(F32)
        n = total.shape[0]
        while n > 1:
            n //= 2
            step *= 2
            kept, got = total[:n], swap(total[n:].astype(BF16), "z", step)
            total = (after(kept, *hold) if n == 1 else kept) + got.astype(F32)
        return total[0]

    ffn_keep = jnp.concatenate([up_keep, down_keep], axis=1)
    ffn_got = jnp.concatenate([after(up_got, kv_parts), down_got], axis=1)
    grad_inputs, *gfx = input_grads(
        place, gq, kv_parts, w_fact_t, x, s1, gain_one, gres, gain_two_part, cosine, sine, n_rows
    )
    head = gfx[0].shape[0] - w_fact.shape[1] // n_rows
    gf_same = [gfx[0]] + others(gfx, ROW, n_rows)
    h1_slab = own_slab(place, hg_same, after(h1_other, gfx[0]), n_out, own_cols, ordered)
    gf_all = both_cores(after(gf_same, h1_slab))
    tail_parts = own_blocks(fact_grads(h1_slab, *gf_all, out_parts, head, ordered))
    total = add_up(ffn_keep, ffn_got, tail_parts)
    tail_got = others(tail_parts, "z", n_z)
    up_total, down_total = total[:2 * ff_part], total[2 * ff_part:].reshape(ff // n_ctx, width // n_rows)
    mine, other = up_total[:, :own_cols], swap(up_total[:, own_cols:].astype(BF16), "core", 1).astype(F32)
    first = jnp.where(core == 0, mine, other)
    second = jnp.where(core == 0, other, mine)
    grad_gate = jnp.concatenate([first[:ff_part], second[:ff_part]], axis=0).T
    grad_up = jnp.concatenate([first[ff_part:], second[ff_part:]], axis=0).T

    moves = []
    for r in range(n_rows):
        for c in range(2):
            for p in range(n_z):
                b, s = p // n_rows, (p % n_rows) ^ (r if ordered else 0)
                moves.append((r * n_ctx + 2 * p + c, s * n_ctx + (r * 2 + c) * per + b))
    grad_down = lax.ppermute(down_total.astype(BF16), ROW + CTX, moves).astype(F32)

    tail_parts = after(tail_parts, grad_gate, grad_up)
    tail = tree_sum([part.astype(F32) for part in [tail_parts[0]] + tail_got])
    rows = gfx[0].shape[0]
    grad_fact, grad_out = tail[head:rows].T, tail[rows:].T
    if ordered:
        gains = (tail[:head // 2] + tail[head // 2:head]).reshape(2, width)
    else:
        sums = gfx[0][:head // 2].astype(F32) + gfx[0][head // 2:head].astype(F32)
        gains = lax.psum(sums, ROW + CTX).reshape(2, width)

    return (
        block_out.reshape(inputs.shape),
        grad_inputs.reshape(inputs.shape),
        gains[0],
        grad_fact,
        grad_out,
        gains[1],
        grad_gate,
        grad_up,
        grad_down,
    )


def solution(mesh):
    n_rows, n_ctx = mesh.shape["row"], mesh.shape["ctx"]
    fine = Mesh(mesh.devices.reshape(n_rows // 2, 2, n_ctx // 2, 2), ROW + CTX)
    placed = (P(ROW, CTX, None), P(ROW), P(), P(), P(), P(), P(), P(), P(), P(ROW, CTX, None))
    return jax.shard_map(
        body,
        mesh=fine,
        in_specs=placed,
        out_specs=(
            P(ROW, CTX, None), P(ROW, CTX, None), P(), P(CTX, ROW), P(CTX, ROW), P(), P(CTX, ROW), P(CTX, ROW),
            P(CTX, ROW),
        ),
        check_vma=False,
    )
```

```python
import functools

import jax
import jax.numpy as jnp
from jax import lax
from jax.experimental import pallas as pl
from jax.experimental.pallas import tpu as pltpu
from jax.sharding import Mesh
from jax.sharding import PartitionSpec as P

H = 16
DH = 64
RQ = 6
RK = 2
EPS = 1e-06
QA = RQ * H
QF = RQ * (H + DH)
KA = 2 * RK * H
KB = 2 * RK * DH
KF = KA + KB
SCALE = DH ** (-0.5)
F32 = jnp.float32
BF16 = jnp.bfloat16
VMEM_BYTES = 56 * 1024 * 1024

NN = (((1,), (0,)), ((), ()))
NT = (((1,), (1,)), ((), ()))


def mm(a, b, dims=NN):
    return lax.dot_general(a, b, dims, preferred_element_type=F32)


def vmem():
    return pl.BlockSpec(memory_space=pltpu.VMEM)


def smem():
    return pl.BlockSpec(memory_space=pltpu.SMEM)


def hbm():
    return pl.BlockSpec(memory_space=pltpu.HBM)


def call(kernel, outs, ins, args, scratch=(), flops=0, moved=0, name=None):
    return pl.pallas_call(
        kernel,
        out_shape=[jax.ShapeDtypeStruct(s, d) for s, d in outs],
        in_specs=ins,
        out_specs=[vmem() for _ in outs],
        scratch_shapes=list(scratch),
        compiler_params=pltpu.CompilerParams(vmem_limit_bytes=VMEM_BYTES),
        cost_estimate=pl.CostEstimate(flops=flops, transcendentals=0, bytes_accessed=moved),
        name=name,
    )(*args)


def slot_position(index, block_len, slots_all):
    block_id = index // (2 * block_len)
    within = index % (2 * block_len)
    return jnp.where(
        within < block_len,
        block_id * block_len + within,
        (slots_all // block_len - 1 - block_id) * block_len + within - block_len,
    )


def turn(rows, cosine, sine):
    half = DH // 2
    upper, lower = rows[:half], rows[half:]
    return jnp.concatenate([upper * cosine - lower * sine, lower * cosine + upper * sine], axis=0)


def turn_back(rows, cosine, sine):
    half = DH // 2
    upper, lower = rows[:half], rows[half:]
    return jnp.concatenate([upper * cosine + lower * sine, lower * cosine - upper * sine], axis=0)


ROW = ("r1", "r0")
CTX = ("z", "core")
GROUP = ("r1", "r0", "core")


def swap(value, axis, k):
    size = lax.axis_size(axis)
    return lax.ppermute(value, axis, [(j, j ^ k) for j in range(size)])


def tree_sum(parts):
    parts = list(parts)
    while len(parts) > 1:
        parts = [parts[i] + parts[i + 1] for i in range(0, len(parts), 2)]
    return parts[0]


def factor_kernel(
    x_ref, cot_ref, valid_ref, gain_ref, wft_ref, pos_ref,
    h1_ref, go_ref, s1_ref, q_ref, qt_ref, qf_ref, kv_ref, cos_ref, sin_ref, ft,
):
    x = x_ref[...].astype(F32)
    s1 = lax.rsqrt(jnp.mean(x * x, axis=1, keepdims=True) + EPS)
    s1_ref[...] = s1
    h1 = (x * s1 * gain_ref[...]).astype(BF16)
    h1_ref[...] = h1
    go_ref[...] = (cot_ref[...].astype(F32) * valid_ref[...]).astype(BF16)
    half = lax.broadcasted_iota(jnp.int32, cos_ref.shape, 0).astype(F32)
    angles = pos_ref[...] * jnp.exp(-jnp.log(10000.0) * (2.0 * half) / DH)
    cosine, sine = jnp.cos(angles), jnp.sin(angles)
    cos_ref[...] = cosine
    sin_ref[...] = sine
    ft[:wft_ref.shape[0], :] = mm(wft_ref[...], h1, NT)
    kv_ref[:KA, :] = ft[QF:QF + KA, :].astype(BF16)
    for r in range(2 * RK):
        rows = ft[QF + KA + r * DH:QF + KA + (r + 1) * DH, :]
        if r < RK:
            rows = turn(rows, cosine, sine)
        kv_ref[KA + r * DH:KA + (r + 1) * DH, :] = rows.astype(BF16)
    qf_ref[:QA, :] = ft[:QA, :]
    for r in range(RQ):
        qf_ref[QA + r * DH:QA + (r + 1) * DH, :] = turn(ft[QA + r * DH:QA + (r + 1) * DH, :], cosine, sine)
    for h in range(H):
        total = None
        for r in range(RQ):
            term = qf_ref[r * H + h:r * H + h + 1, :] * qf_ref[QA + r * DH:QA + (r + 1) * DH, :]
            total = term if total is None else total + term
        ft[h * DH:(h + 1) * DH, :] = total / RQ
    qt = ft[:H * DH, :]
    qt_ref[...] = qt.astype(BF16)
    q_ref[...] = qt.T.astype(BF16)


def project(x, cot, valid, gain, w_fact_t, pos):
    tokens, width = x.shape
    nf = w_fact_t.shape[0]
    angles = ((DH // 2, tokens), F32)
    return call(
        factor_kernel,
        [((tokens, width), BF16), ((tokens, width), BF16), ((tokens, 1), F32), ((tokens, H * DH), BF16),
         ((H * DH, tokens), BF16), ((QF, tokens), F32), ((KF, tokens), BF16), angles, angles],
        [vmem()] * 6,
        (x, cot, valid, gain, w_fact_t, pos),
        [pltpu.VMEM((max(nf, H * DH), tokens), F32)],
        2 * tokens * width * nf, 2 * width * nf, "factors",
    )


def load_factors(pieces, a_rows, b_rows):
    at = 0
    for piece in pieces:
        n = piece.shape[1]
        a_rows[:, at:at + n] = piece[:KA, :].astype(F32)
        b_rows[:, at:at + n] = piece[KA:, :].astype(F32)
        at += n


def expand_pair(pair, side, a_rows, b_rows):
    halves = []
    for sub in range(2):
        total = None
        for r in range(RK):
            a = a_rows[pl.ds((side * RK + r) * H + 2 * pair + sub, 1), :]
            term = a * b_rows[(side * RK + r) * DH:(side * RK + r + 1) * DH, :]
            total = term if total is None else total + term
        halves.append((total * (1.0 / RK)).astype(BF16))
    return jnp.concatenate(halves, axis=0)


def stack_pair(rows):
    lane = lax.broadcasted_iota(jnp.int32, rows.shape, 1)
    zero = jnp.zeros_like(rows)
    return jnp.concatenate([jnp.where(lane < DH, rows, zero), jnp.where(lane < DH, zero, rows)], axis=0)


def pair_lanes(pair):
    return pl.ds(pl.multiple_of(pair * 2 * DH, 2 * DH), 2 * DH)


def attend_kernel(n_pieces, *refs):
    q_ref, bias_ref, wo_ref, x_ref, gain_ref = refs[:5]
    pieces = refs[5:5 + n_pieces]
    h2_ref, mixed, resid_ref, lse_ref, a_rows, b_rows = refs[5 + n_pieces:]
    tokens, width = x_ref.shape
    load_factors(pieces, a_rows, b_rows)
    bias = bias_ref[...]
    bias = jnp.concatenate([bias, bias], axis=0)

    def step(pair, carry):
        keys = expand_pair(pair, 0, a_rows, b_rows)
        values = expand_pair(pair, 1, a_rows, b_rows)
        q = stack_pair(q_ref[:, pair_lanes(pair)])
        scores = mm(q, keys) * SCALE + bias
        top = jnp.max(scores, axis=1, keepdims=True)
        exponent = jnp.exp(scores - top)
        total = jnp.sum(exponent, axis=1, keepdims=True)
        probs = (exponent * (1.0 / total)).astype(BF16)
        lse_ref[pair] = top + jnp.log(total)
        out = mm(probs, values, NT)
        lane = lax.broadcasted_iota(jnp.int32, (tokens, 2 * DH), 1)
        mixed[:, pair_lanes(pair)] = jnp.where(lane < DH, out[:tokens], out[tokens:]).astype(BF16)
        return carry

    lax.fori_loop(0, H // 2, step, 0, unroll=True)
    resid = x_ref[...].astype(F32) + mm(mixed[...], wo_ref[...])
    resid_ref[...] = resid
    s2 = lax.rsqrt(jnp.mean(resid * resid, axis=1, keepdims=True) + EPS)
    h2_ref[...] = (resid * s2 * gain_ref[...]).astype(BF16)


def attend(q, bias, w_out, x, gain, pieces):
    tokens, width = x.shape
    slots = sum(p.shape[1] for p in pieces)
    return call(
        functools.partial(attend_kernel, len(pieces)),
        [((tokens, width), BF16), ((tokens, H * DH), BF16), ((tokens, width), F32), ((H // 2, 2 * tokens, 1), F32)],
        [vmem()] * (5 + len(pieces)),
        (q, bias, w_out, x, gain, *pieces),
        [pltpu.VMEM((KA, slots), F32), pltpu.VMEM((KB, slots), F32)],
        4 * tokens * slots * H * DH, 2 * width * width, "attend",
    )


def attend_back_kernel(n_pieces, *refs):
    q_ref, qt_ref, gm_ref, gmt_ref, lse_ref, bias_ref, qf_ref, cos_ref, sin_ref = refs[:9]
    pieces = refs[9:9 + n_pieces]
    gq_ref, own_ref, send_ref, a_rows, b_rows, ga_rows, gb_rows, gqb_rows = refs[9 + n_pieces:]
    tokens = q_ref.shape[0]
    load_factors(pieces, a_rows, b_rows)
    gb_rows[...] = jnp.zeros_like(gb_rows)
    gqb_rows[...] = jnp.zeros_like(gqb_rows)

    def spread(rows):
        top = lax.broadcasted_iota(jnp.int32, rows.shape, 0) < DH
        zero = jnp.zeros_like(rows)
        return jnp.concatenate([jnp.where(top, rows, zero), jnp.where(top, zero, rows)], axis=1)

    def step(pair, carry):
        keys = expand_pair(pair, 0, a_rows, b_rows)
        values = expand_pair(pair, 1, a_rows, b_rows)
        rows = pl.ds(pl.multiple_of(pair * 2 * DH, 2 * DH), 2 * DH)
        both = (
            stack_pair(q_ref[:, pair_lanes(pair)]), stack_pair(gm_ref[:, pair_lanes(pair)]),
            spread(qt_ref[rows, :]), spread(gmt_ref[rows, :]), lse_ref[pair],
        )
        takes = [slice(0, 2 * tokens)] if keys.shape[1] <= 2048 else [slice(0, tokens), slice(tokens, 2 * tokens)]
        grad_q, grad_k, grad_v = [], None, None
        for take in takes:
            q, g, qt, gt, lse = both[0][take], both[1][take], both[2][:, take], both[3][:, take], both[4][take]
            heads = q.shape[0] // tokens
            scores = mm(q, keys) * SCALE + jnp.concatenate([bias_ref[...]] * heads, axis=0)
            probs = jnp.exp(scores - lse)
            grad_probs = mm(g, values)
            inner = jnp.sum(probs * grad_probs, axis=1, keepdims=True)
            grad_scores = (probs * (grad_probs - inner)).astype(BF16)
            grad_q.append(mm(grad_scores, keys, NT).T * SCALE)
            gk, gv = mm(qt, grad_scores) * SCALE, mm(gt, probs.astype(BF16))
            grad_k, grad_v = (gk, gv) if grad_k is None else (grad_k + gk, grad_v + gv)
        grad_q = jnp.concatenate(grad_q, axis=1)
        for sub in range(2):
            head = 2 * pair + sub
            part = slice(sub * DH, (sub + 1) * DH)
            for side, grad in ((0, grad_k[part]), (1, grad_v[part])):
                for r in range(RK):
                    s = side * RK + r
                    row = pl.ds(s * H + head, 1)
                    seg = slice(s * DH, (s + 1) * DH)
                    ga_rows[row, :] = jnp.sum(grad * b_rows[seg, :], axis=0, keepdims=True) * (1.0 / RK)
                    gb_rows[seg, :] += grad * (a_rows[row, :] * (1.0 / RK))
            dq = grad_q[part, sub * tokens:(sub + 1) * tokens]
            for r in range(RQ):
                row = pl.ds(r * H + head, 1)
                seg = slice(QA + r * DH, QA + (r + 1) * DH)
                gq_ref[row, :] = jnp.sum(dq * qf_ref[seg, :], axis=0, keepdims=True) * (1.0 / RQ)
                gqb_rows[r * DH:(r + 1) * DH, :] += dq * (qf_ref[row, :] * (1.0 / RQ))
        return carry

    lax.fori_loop(0, H // 2, step, 0)
    cosine, sine = cos_ref[...], sin_ref[...]
    for r in range(RQ):
        gq_ref[QA + r * DH:QA + (r + 1) * DH, :] = turn_back(gqb_rows[r * DH:(r + 1) * DH, :], cosine, sine)
    at = 0
    for j in range(n_pieces):
        n = pieces[j].shape[1]
        out_ref = send_ref if j % 2 else own_ref
        out_ref[j // 2, :KA, :] = ga_rows[:, at:at + n].astype(BF16)
        out_ref[j // 2, KA:, :] = gb_rows[:, at:at + n].astype(BF16)
        at += n


def attend_back(q, qt, gm, gmt, lse, bias, qf, cosine, sine, pieces):
    tokens = q.shape[0]
    slots = sum(p.shape[1] for p in pieces)
    n = len(pieces)
    return call(
        functools.partial(attend_back_kernel, n),
        [((QF, tokens), F32)] + [((n // 2, KF, slots // n), BF16)] * 2,
        [vmem()] * (9 + n),
        (q, qt, gm, gmt, lse, bias, qf, cosine, sine, *pieces),
        [pltpu.VMEM((KA, slots), F32), pltpu.VMEM((KB, slots), F32), pltpu.VMEM((KA, slots), F32),
         pltpu.VMEM((KB, slots), F32), pltpu.VMEM((RQ * DH, tokens), F32)],
        10 * tokens * slots * H * DH, 4 * tokens * slots, "attend_back",
    )


def ffn_kernel(
    place_ref, h2_ref, go_ref, resid_ref, gain_ref, mixed_ref, wg_hbm, wu_hbm, wd_hbm, wo_hbm, *refs,
):
    out_ref, gain_grad_ref, gres_ref, gm_ref, gmt_ref = refs[:5]
    mgx_refs, (branch, grad_h2, gb_cols, wg, wu, wd, wo, sems) = refs[5:-8], refs[-8:]
    width, ff = wg.shape
    n_chunks = sems.shape[1]
    chunk = ff // n_chunks
    copies = []
    for j in range(n_chunks):
        part = pl.ds(j * chunk, chunk)
        copies.append([
            pltpu.make_async_copy(wg_hbm.at[:, part], wg.at[:, part], sems.at[0, j]),
            pltpu.make_async_copy(wu_hbm.at[:, part], wu.at[:, part], sems.at[1, j]),
            pltpu.make_async_copy(wd_hbm.at[part, :], wd.at[part, :], sems.at[2, j]),
        ])
    wo_copy = pltpu.make_async_copy(wo_hbm, wo, sems.at[3, 0])
    for group in copies:
        for copy in group:
            copy.start()
    wo_copy.start()
    h2, go = h2_ref[...], go_ref[...]
    groups = [list(range(0, min(3, n_chunks)))]
    groups += [list(range(j, min(j + 4, n_chunks))) for j in range(3, n_chunks, 4)]
    for group in groups:
        for j in group:
            for copy in copies[j]:
                copy.wait()
        part = slice(group[0] * chunk, (group[-1] + 1) * chunk)
        gate, up = mm(h2, wg[:, part]), mm(h2, wu[:, part])
        grad_hidden = mm(go, wd[part, :], NT)
        sig = jax.nn.sigmoid(gate)
        silu = gate * sig
        hidden = (silu * up).astype(BF16)
        grad_gate = (grad_hidden * up * sig * (1.0 + gate * (1.0 - sig))).astype(BF16)
        grad_up = (grad_hidden * silu).astype(BF16)
        more_branch = mm(hidden, wd[part, :])
        more_grad = mm(grad_gate, wg[:, part], NT) + mm(grad_up, wu[:, part], NT)
        if group[0] == 0:
            branch[...] = more_branch
            grad_h2[...] = more_grad
        else:
            branch[...] += more_branch
            grad_h2[...] += more_grad
    resid = resid_ref[...]
    out_ref[...] = (resid + branch[...]).astype(BF16)
    s2 = lax.rsqrt(jnp.mean(resid * resid, axis=1, keepdims=True) + EPS)
    n2 = resid * s2
    gh = grad_h2[...]
    gain_grad_ref[...] = jnp.sum(gh * n2, axis=0, keepdims=True)
    g2 = gh * gain_ref[...]
    gres = go.astype(F32) + s2 * (g2 - n2 * jnp.mean(g2 * n2, axis=1, keepdims=True))
    gres_ref[...] = gres
    gb = gres.astype(BF16)
    gb_cols[...] = gb
    wo_copy.wait()
    gm = mm(gb, wo[...], NT)
    gm_ref[...] = gm.astype(BF16)
    gmt_ref[...] = gm.T.astype(BF16)
    for k, mgx_ref in enumerate(mgx_refs):
        cols = mgx_ref.shape[1] - width
        mgx_ref[:, :width] = mixed_ref[...]
        mgx_ref[:, width:] = gb_cols[:, pl.ds(pl.multiple_of((place_ref[0] ^ k) * cols, cols), cols)]


def feed_forward(place, h2, go, w_gate, w_up, w_down, resid, gain, w_out, mixed, n_rows):
    tokens, width = resid.shape
    ff = w_gate.shape[1]
    chunk = 256 if ff % 256 == 0 else 128
    return call(
        ffn_kernel,
        [((tokens, width), BF16), ((1, width), F32), ((tokens, width), F32), ((tokens, width), BF16),
         ((width, tokens), BF16)] + [((tokens, width + width // n_rows), BF16)] * n_rows,
        [smem()] + [vmem()] * 5 + [hbm()] * 4,
        (place, h2, go, resid, gain, mixed, w_gate, w_up, w_down, w_out),
        [pltpu.VMEM((tokens, width), F32), pltpu.VMEM((tokens, width), F32), pltpu.VMEM((tokens, width), BF16),
         pltpu.VMEM((width, ff), BF16), pltpu.VMEM((width, ff), BF16), pltpu.VMEM((ff, width), BF16),
         pltpu.VMEM((width, width), BF16), pltpu.SemaphoreType.DMA((4, ff // chunk))],
        12 * tokens * width * ff, 6 * width * ff, "feed_forward",
    )


def weight_kernel(n_pieces, ordered, place_ref, wg_ref, wu_ref, wd_ref, go_other, *refs):
    h2_pieces, go_same = refs[:n_pieces], refs[n_pieces:n_pieces + n_pieces // 2]
    up_keep, up_send, down_keep, down_send, h2s, gos, wds, window, turned, sems = refs[n_pieces + n_pieces // 2:]
    tokens, width = h2_pieces[0].shape
    ff, span = wds.shape[0], window.shape[2]
    at = (place_ref[0] * 2 + place_ref[1]) * ff
    start = jnp.minimum(at // 128 * 128, wg_ref.shape[1] - span)
    cut = pl.ds(pl.multiple_of(start, 128), span)
    groups = [[pltpu.make_async_copy(ref.at[:, cut], window.at[i], sems.at[2, i])] for i, ref in enumerate((wg_ref, wu_ref))]
    groups += [[], []]
    for j in range(n_pieces):
        rows = pl.ds(j * tokens, tokens)
        groups[2].append(pltpu.make_async_copy(h2_pieces[j], h2s.at[rows, :], sems.at[0, j]))
        half = n_pieces // 2
        go = go_same[j] if j < half else go_other.at[j - half]
        groups[3].append(pltpu.make_async_copy(go, gos.at[rows, :], sems.at[1, j]))
    groups[3].append(pltpu.make_async_copy(
        wd_ref.at[pl.ds(pl.multiple_of(at, 32), ff), :], wds, sems.at[1, n_pieces]))
    for group in groups:
        for copy in group:
            copy.start()
    own = pl.ds(pl.multiple_of(at - start, 32), ff)
    for i in range(2):
        groups[i][0].wait()
        turned[i] = window[i].T
    for copy in groups[2]:
        copy.wait()
    gate = mm(turned[0, own, :], h2s[...], NT)
    up = mm(turned[1, own, :], h2s[...], NT)
    for copy in groups[3]:
        copy.wait()
    grad_hidden = mm(wds[...], gos[...], NT)
    sig = jax.nn.sigmoid(gate)
    silu = gate * sig
    hidden = (silu * up).astype(BF16)
    grad_gate = (grad_hidden * up * sig * (1.0 + gate * (1.0 - sig))).astype(BF16)
    grad_up = (grad_hidden * silu).astype(BF16)
    kept = up_keep.shape[0]
    n_z = 2 * kept
    cols = width // n_z
    half = cols // 2
    for slot, k in enumerate(halving_order(n_z)):
        up_ref, down_ref, i = (up_keep, down_keep, slot) if slot < kept else (up_send, down_send, slot - kept)
        if ordered:
            z, core = place_ref[2] ^ k, place_ref[1]
            first = pl.ds(pl.multiple_of(z * cols + core * half, half), half)
            other = pl.ds(pl.multiple_of(z * cols + (1 - core) * half, half), half)
            straight = pl.ds(pl.multiple_of((z ^ place_ref[0]) * cols, cols), cols)
            h2c = jnp.concatenate([h2s[:, first], h2s[:, other]], axis=1)
        else:
            straight = slice(slot * cols, (slot + 1) * cols)
            h2c = h2s[:, straight]
        up_ref[i, :ff, :] = mm(grad_gate, h2c).astype(BF16)
        up_ref[i, ff:, :] = mm(grad_up, h2c).astype(BF16)
        down_ref[i] = mm(hidden, gos[:, straight]).astype(BF16)


def halving_order(n):
    order = [0]
    k = n // 2
    while k >= 1:
        order = order + [o | k for o in order]
        k //= 2
    return order


def weight_grads(place, w_gate, w_up, w_down, h2_pieces, go_same, go_other, n_z, ordered):
    n = len(h2_pieces)
    tokens, width = h2_pieces[0].shape
    ff = w_gate.shape[1] // n
    span = min(w_gate.shape[1], -(-ff // 128) * 128 + 128)
    total = n * tokens
    return call(
        functools.partial(weight_kernel, n, ordered),
        [((n_z // 2, 2 * ff, width // n_z), BF16)] * 2 + [((n_z // 2, ff, width // n_z), BF16)] * 2,
        [smem()] + [hbm()] * (4 + n + n // 2),
        (place, w_gate, w_up, w_down, go_other, *h2_pieces, *go_same),
        [pltpu.VMEM((total, width), BF16), pltpu.VMEM((total, width), BF16), pltpu.VMEM((ff, width), BF16),
         pltpu.VMEM((2, width, span), BF16), pltpu.VMEM((2, span, width), BF16), pltpu.SemaphoreType.DMA((3, n + 1))],
        12 * total * width * ff, 6 * width * ff + 4 * total * width, "weight_grads",
    )


def own_cut(ordered, place_ref, k, cols):
    if not ordered:
        return slice(k * cols, (k + 1) * cols)
    return pl.ds(pl.multiple_of(((place_ref[2] ^ k) * 2 + place_ref[1]) * cols, cols), cols)


def slab_kernel(n_out, ordered, place_ref, h1_other, *refs):
    *h1_same, h1_ref, sems = refs
    n_same = len(h1_same)
    tokens = h1_other.shape[1]
    cols = h1_ref.shape[1] // n_out
    copies = []
    for j in range(2 * n_same):
        piece = h1_same[j] if j < n_same else h1_other.at[j - n_same]
        for k in range(n_out):
            copies.append(pltpu.make_async_copy(
                piece.at[:, own_cut(ordered, place_ref, k, cols)],
                h1_ref.at[pl.ds(j * tokens, tokens), pl.ds(k * cols, cols)], sems.at[j, k]))
    for copy in copies:
        copy.start()
    for copy in copies:
        copy.wait()


def own_slab(place, h1_same, h1_other, n_out, cols, ordered):
    n, tokens, width = h1_other.shape
    if not ordered:
        return jnp.concatenate([piece[:, :width] for piece in h1_same] + [h1_other.reshape(-1, width)], axis=0)
    return call(
        functools.partial(slab_kernel, n_out, ordered),
        [((2 * n * tokens, n_out * cols), BF16)],
        [smem()] + [hbm()] * (1 + n),
        (place, h1_other, *h1_same),
        [pltpu.SemaphoreType.DMA((2 * n, n_out))],
        0, 4 * n * tokens * n_out * cols, "own_slab",
    )[0]


def out_kernel(n_out, ordered, place_ref, mine_ref, other_ref, *refs):
    out_refs, (wide, thin) = refs[:-2], refs[-2:]
    n_rows, tokens, both = mine_ref.shape
    part, cols = thin.shape[1], out_refs[0].shape[1]
    for i, ref in enumerate((mine_ref, other_ref)):
        for j in range(n_rows):
            rows = slice((i * n_rows + j) * tokens, (i * n_rows + j + 1) * tokens)
            thin[rows, :] = ref[j, :, both - part:]
            for k in range(n_out):
                wide[rows, k * cols:(k + 1) * cols] = ref[j, :, own_cut(ordered, place_ref, k, cols)]
    full = mm(thin[...].T, wide[...]).astype(BF16)
    for k, out_ref in enumerate(out_refs):
        out_ref[...] = full[:, k * cols:(k + 1) * cols]


def out_grads(place, mine, other, width, n_out, cols, ordered):
    n_rows, tokens, both = mine.shape
    part = both - width
    total = 2 * n_rows * tokens
    return call(
        functools.partial(out_kernel, n_out, ordered),
        [((part, cols), BF16)] * n_out,
        [smem(), vmem(), vmem()],
        (place, mine, other),
        [pltpu.VMEM((total, n_out * cols), BF16), pltpu.VMEM((total, part), BF16)],
        2 * total * part * n_out * cols, 4 * total * both, "out_grads",
    )


def fact_kernel(n_out, head, ordered, h1_ref, mine_ref, other_ref, *refs):
    carried, out_refs, thin = refs[:n_out], refs[n_out:-1], refs[-1]
    cols = out_refs[0].shape[1]
    rows, tokens = mine_ref.shape[1:]
    parts = [ref[j] for ref in (mine_ref, other_ref) for j in range(ref.shape[0])]
    for j, part in enumerate(parts):
        thin[:, j * tokens:(j + 1) * tokens] = part[head:, :]
    full = mm(thin[...], h1_ref[...]).astype(BF16)
    for k, out_ref in enumerate(out_refs):
        out_ref[head:rows, :] = full[:, k * cols:(k + 1) * cols]
        out_ref[rows:, :] = carried[k][...]
    if ordered:
        half = head // 2
        gains = tree_sum([p[:half].astype(F32) + p[half:head].astype(F32) for p in parts])
        high = gains.astype(BF16)
        low = (gains - high.astype(F32)).astype(BF16)
        for out_ref in out_refs:
            out_ref[:half, :] = high
            out_ref[half:head, :] = low


def fact_grads(h1_slab, mine, other, carried, head, ordered):
    n_rows, rows, tokens = mine.shape
    total = 2 * n_rows * tokens
    n_out = len(carried)
    part, cols = carried[0].shape
    return call(
        functools.partial(fact_kernel, n_out, head, ordered),
        [((rows + part, cols), BF16)] * n_out,
        [vmem()] * (3 + n_out),
        (h1_slab, mine, other, *carried),
        [pltpu.VMEM((rows - head, total), BF16)],
        2 * total * rows * n_out * cols, 2 * total * n_out * cols, "fact_grads",
    )


def input_kernel(
    n_parts, place_ref, gq_ref, *refs,
):
    parts = refs[:n_parts]
    wft_ref, x_ref, s1_ref, gain_ref, gres_ref, gain_two_ref, cos_ref, sin_ref = refs[n_parts:n_parts + 8]
    gin_ref, *gfx_refs = refs[n_parts + 8:-2]
    gf, gains = refs[-2:]
    cosine, sine = cos_ref[...], sin_ref[...]
    kv = tree_sum([part[...].astype(F32) for part in parts])
    gf[:QF, :] = gq_ref[...]
    gf[QF:QF + KA, :] = kv[:KA]
    for r in range(2 * RK):
        rows = kv[KA + r * DH:KA + (r + 1) * DH]
        if r < RK:
            rows = turn_back(rows, cosine, sine)
        gf[QF + KA + r * DH:QF + KA + (r + 1) * DH, :] = rows
    grad = gf[...].T.astype(BF16)
    grad_h1 = mm(grad, wft_ref[...])
    s1 = s1_ref[...]
    n1 = x_ref[...].astype(F32) * s1
    gain_one = jnp.sum(grad_h1 * n1, axis=0, keepdims=True)
    gain_two = gain_two_ref[...]
    g1 = grad_h1 * gain_ref[...]
    gin_ref[...] = gres_ref[...] + s1 * (g1 - n1 * jnp.mean(g1 * n1, axis=1, keepdims=True))
    tokens, width = x_ref.shape
    half = gains.shape[0]
    for i in range(half // 2):
        gains[i:i + 1, :] = gain_one[:, i * tokens:(i + 1) * tokens]
        gains[half // 2 + i:half // 2 + i + 1, :] = gain_two[:, i * tokens:(i + 1) * tokens]
    high = gains[...].astype(BF16)
    low = (gains[...] - high.astype(F32)).astype(BF16)
    for k, gfx_ref in enumerate(gfx_refs):
        part = gfx_ref.shape[0] - 2 * half
        gfx_ref[:half, :] = high
        gfx_ref[half:2 * half, :] = low
        gfx_ref[2 * half:, :] = gf[pl.ds(pl.multiple_of((place_ref[0] ^ k) * part, 8), part), :].astype(BF16)


def input_grads(place, gq, parts, w_fact_t, x, s1, gain, gres, gain_two, cosine, sine, n_rows):
    tokens, width = x.shape
    nf = w_fact_t.shape[0]
    half = 2 * width // tokens
    return call(
        functools.partial(input_kernel, len(parts)),
        [((tokens, width), F32)] + [((2 * half + nf // n_rows, tokens), BF16)] * n_rows,
        [smem()] + [vmem()] * (9 + len(parts)),
        (place, gq, *parts, w_fact_t, x, s1, gain, gres, gain_two, cosine, sine),
        [pltpu.VMEM((nf, tokens), F32), pltpu.VMEM((half, tokens), F32)],
        2 * tokens * width * nf, 2 * width * nf, "input_grads",
    )


def after(values, *others):
    flat, tree = jax.tree.flatten((values, others))
    return jax.tree.unflatten(tree, lax.optimization_barrier(flat))[0]


def body(inputs, lengths, gain_attn, w_fact, w_out, gain_ffn, w_gate, w_up, w_down, cotangent):
    seqs, local_len, width = inputs.shape
    tokens = seqs * local_len
    n_rows, n_ctx = lax.axis_size(ROW), lax.axis_size(CTX)
    n_z = n_ctx // 2
    row, ctx = lax.axis_index(ROW), lax.axis_index(CTX)
    z, core = ctx // 2, ctx % 2
    slots_all = local_len * n_ctx
    block_len = local_len // 2
    ff = w_gate.shape[1]
    ff_part = ff // (2 * n_rows)
    own_cols = width // n_ctx
    per = n_ctx // (2 * n_rows)
    ordered = own_cols % 128 == 0 and per == 1 and tokens == 128
    n_out = n_z if ordered else n_ctx
    place = jnp.stack([row, core, z]).astype(jnp.int32)

    within = jnp.arange(local_len, dtype=jnp.int32)
    local_pos = jnp.tile(slot_position(ctx * local_len + within, block_len, slots_all), seqs)
    local_seq = jnp.repeat(jnp.arange(seqs, dtype=jnp.int32), local_len)
    valid = (local_pos < jnp.repeat(lengths, local_len)).astype(F32)[:, None]
    piece_of = jnp.arange(n_ctx, dtype=jnp.int32) ^ ctx
    key_pos = jnp.tile(
        slot_position(piece_of[:, None] * local_len + within[None, :], block_len, slots_all)[:, None, :], (1, seqs, 1)
    ).reshape(-1)
    key_seq = jnp.tile(local_seq, n_ctx)
    key_len = jnp.tile(jnp.repeat(lengths, local_len), n_ctx)
    allowed = (
        (key_pos[None, :] <= local_pos[:, None])
        & (key_pos < key_len)[None, :]
        & (key_seq[None, :] == local_seq[:, None])
    )
    bias = jnp.where(allowed, 0.0, -1e30).astype(F32)

    x = inputs.reshape(tokens, width)
    gain_one, gain_two = gain_attn[None, :], gain_ffn[None, :]
    w_fact_t = w_fact.T

    def others(values, axis, n):
        return [swap(values[k], axis, k) for k in range(1, n)]

    def along_core(values):
        return list(values) + [swap(value, "core", 1) for value in values]

    def both_cores(values):
        mine = jnp.stack(values)
        return [mine, swap(mine, "core", 1)]

    h1, go, s1, q, qt, qf, kv, cosine, sine = project(
        x, cotangent.reshape(tokens, width), valid, gain_one, w_fact_t, local_pos.astype(F32)[None, :]
    )
    kv_z = [kv] + others([kv] * n_z, "z", n_z)
    kv_pieces = []
    for part in kv_z:
        kv_pieces += [part, swap(part, "core", 1)]
    go_same = [go] + others([go] * n_rows, ROW, n_rows)
    h2, mixed, resid, lse = attend(after(q, place), bias, w_out, x, gain_two, kv_pieces)
    h2_same = [h2] + others([h2] * n_rows, ROW, n_rows)
    go_same = after(go_same, h2)
    go_other = swap(jnp.stack(go_same), "core", 1)
    block_out, gain_two_part, gres, gm, gmt, *mgx = feed_forward(
        place, h2, after(go, go_same), w_gate, w_up, w_down, resid, gain_two, w_out, mixed, n_rows
    )
    h2_pieces = along_core(after(h2_same, gm, go_other))
    h1_same = [h1] + others(after([h1] * n_rows, gm), ROW, n_rows)
    up_keep, up_send, down_keep, down_send = weight_grads(
        place, w_gate, w_up, w_down, h2_pieces, go_same, go_other, n_z, ordered
    )
    if not ordered:
        turns = jnp.asarray(halving_order(n_z), jnp.int32) ^ z
        cores = jnp.arange(2, dtype=jnp.int32) ^ core
        up = jnp.take(jnp.concatenate([up_keep, up_send]), turns, axis=0)
        up = jnp.take(up.reshape(n_z, 2 * ff_part, 2, own_cols), cores, axis=2).reshape(up.shape)
        down = jnp.concatenate([down_keep, down_send]).transpose(1, 0, 2)
        down = down.reshape(per, ff_part // per, n_rows, width // n_rows).transpose(0, 2, 1, 3)
        down = jnp.take(down.reshape(n_z, ff_part, 2 * own_cols), turns, axis=0)
        up_keep, up_send, down_keep, down_send = up[:n_z // 2], up[n_z // 2:], down[:n_z // 2], down[n_z // 2:]

    h1_same = after(h1_same, up_send)
    up_got = swap(up_send, "z", 1)
    mg_same = [mgx[0]] + others(mgx, ROW, n_rows)
    gm_in = after(gm, up_send)
    h1_other = swap(jnp.stack(h1_same), "core", 1)
    gq, gkv_own, gkv_send = attend_back(q, qt, gm_in, gmt, lse, bias, qf, cosine, sine, kv_pieces)
    gkv_send, mg_same, h1_other, up_got = lax.optimization_barrier((gkv_send, mg_same, h1_other, up_got))
    down_got = swap(after(down_send, up_got), "z", 1)
    gkv_got = swap(gkv_send, "core", 1)
    mg_mine, mg_other = both_cores(mg_same)
    gkv_z = [(gkv_own[k].astype(F32) + gkv_got[k].astype(F32)).astype(BF16) for k in range(n_z)]
    kv_parts = [gkv_z[0]] + others(gkv_z, "z", n_z)
    kv_parts, down_got = lax.optimization_barrier((kv_parts, down_got))

    def own_blocks(parts):
        if ordered:
            return parts
        parts = jnp.take(jnp.stack(parts), (jnp.arange(n_z, dtype=jnp.int32) ^ z) * 2 + core, axis=0)
        return [parts[k] for k in range(n_z)]

    out_parts = out_grads(place, mg_mine, mg_other, width, n_out, own_cols, ordered)
    gq = after(gq, out_parts)

    def add_up(keep, got, hold, step=1):
        total = keep.astype(F32) + got.astype(F32)
        n = total.shape[0]
        while n > 1:
            n //= 2
            step *= 2
            kept, got = total[:n], swap(total[n:].astype(BF16), "z", step)
            total = (after(kept, *hold) if n == 1 else kept) + got.astype(F32)
        return total[0]

    ffn_keep = jnp.concatenate([up_keep, down_keep], axis=1)
    ffn_got = jnp.concatenate([after(up_got, kv_parts), down_got], axis=1)
    grad_inputs, *gfx = input_grads(
        place, gq, kv_parts, w_fact_t, x, s1, gain_one, gres, gain_two_part, cosine, sine, n_rows
    )
    head = gfx[0].shape[0] - w_fact.shape[1] // n_rows
    gf_same = [gfx[0]] + others(gfx, ROW, n_rows)
    h1_slab = own_slab(place, h1_same, after(h1_other, gfx[0]), n_out, own_cols, ordered)
    gf_all = both_cores(after(gf_same, h1_slab))
    tail_parts = own_blocks(fact_grads(h1_slab, *gf_all, out_parts, head, ordered))
    total = add_up(ffn_keep, ffn_got, tail_parts)
    tail_got = others(tail_parts, "z", n_z)
    up_total, down_total = total[:2 * ff_part], total[2 * ff_part:].reshape(ff // n_ctx, width // n_rows)
    mine, other = up_total[:, :own_cols], swap(up_total[:, own_cols:].astype(BF16), "core", 1).astype(F32)
    first = jnp.where(core == 0, mine, other)
    second = jnp.where(core == 0, other, mine)
    grad_gate = jnp.concatenate([first[:ff_part], second[:ff_part]], axis=0).T
    grad_up = jnp.concatenate([first[ff_part:], second[ff_part:]], axis=0).T

    moves = []
    for r in range(n_rows):
        for c in range(2):
            for p in range(n_z):
                b, s = p // n_rows, (p % n_rows) ^ (r if ordered else 0)
                moves.append((r * n_ctx + 2 * p + c, s * n_ctx + (r * 2 + c) * per + b))
    grad_down = lax.ppermute(down_total.astype(BF16), ROW + CTX, moves).astype(F32)

    tail_parts = after(tail_parts, grad_gate, grad_up)
    tail = tree_sum([part.astype(F32) for part in [tail_parts[0]] + tail_got])
    rows = gfx[0].shape[0]
    grad_fact, grad_out = tail[head:rows].T, tail[rows:].T
    if ordered:
        gains = (tail[:head // 2] + tail[head // 2:head]).reshape(2, width)
    else:
        sums = gfx[0][:head // 2].astype(F32) + gfx[0][head // 2:head].astype(F32)
        gains = lax.psum(sums, ROW + CTX).reshape(2, width)

    return (
        block_out.reshape(inputs.shape),
        grad_inputs.reshape(inputs.shape),
        gains[0],
        grad_fact,
        grad_out,
        gains[1],
        grad_gate,
        grad_up,
        grad_down,
    )


def solution(mesh):
    n_rows, n_ctx = mesh.shape["row"], mesh.shape["ctx"]
    fine = Mesh(mesh.devices.reshape(n_rows // 2, 2, n_ctx // 2, 2), ROW + CTX)
    placed = (P(ROW, CTX, None), P(ROW), P(), P(), P(), P(), P(), P(), P(), P(ROW, CTX, None))
    return jax.shard_map(
        body,
        mesh=fine,
        in_specs=placed,
        out_specs=(
            P(ROW, CTX, None), P(ROW, CTX, None), P(), P(CTX, ROW), P(CTX, ROW), P(), P(CTX, ROW), P(CTX, ROW),
            P(CTX, ROW),
        ),
        check_vma=False,
    )
```

```python
import functools

import jax
import jax.numpy as jnp
from jax import lax
from jax.experimental import pallas as pl
from jax.experimental.pallas import tpu as pltpu
from jax.sharding import Mesh
from jax.sharding import PartitionSpec as P

H = 16
DH = 64
RQ = 6
RK = 2
EPS = 1e-06
QA = RQ * H
QF = RQ * (H + DH)
KA = 2 * RK * H
KB = 2 * RK * DH
KF = KA + KB
SCALE = DH ** (-0.5)
F32 = jnp.float32
BF16 = jnp.bfloat16
VMEM_BYTES = 56 * 1024 * 1024

NN = (((1,), (0,)), ((), ()))
NT = (((1,), (1,)), ((), ()))


def mm(a, b, dims=NN):
    return lax.dot_general(a, b, dims, preferred_element_type=F32)


def vmem():
    return pl.BlockSpec(memory_space=pltpu.VMEM)


def smem():
    return pl.BlockSpec(memory_space=pltpu.SMEM)


def hbm():
    return pl.BlockSpec(memory_space=pltpu.HBM)


def call(kernel, outs, ins, args, scratch=(), flops=0, moved=0, name=None):
    return pl.pallas_call(
        kernel,
        out_shape=[jax.ShapeDtypeStruct(s, d) for s, d in outs],
        in_specs=ins,
        out_specs=[vmem() for _ in outs],
        scratch_shapes=list(scratch),
        compiler_params=pltpu.CompilerParams(vmem_limit_bytes=VMEM_BYTES),
        cost_estimate=pl.CostEstimate(flops=flops, transcendentals=0, bytes_accessed=moved),
        name=name,
    )(*args)


def slot_position(index, block_len, slots_all):
    block_id = index // (2 * block_len)
    within = index % (2 * block_len)
    return jnp.where(
        within < block_len,
        block_id * block_len + within,
        (slots_all // block_len - 1 - block_id) * block_len + within - block_len,
    )


def turn(rows, cosine, sine):
    half = DH // 2
    upper, lower = rows[:half], rows[half:]
    return jnp.concatenate([upper * cosine - lower * sine, lower * cosine + upper * sine], axis=0)


def turn_back(rows, cosine, sine):
    half = DH // 2
    upper, lower = rows[:half], rows[half:]
    return jnp.concatenate([upper * cosine + lower * sine, lower * cosine - upper * sine], axis=0)


ROW = ("r1", "r0")
CTX = ("z", "core")
GROUP = ("r1", "r0", "core")


def swap(value, axis, k):
    size = lax.axis_size(axis)
    return lax.ppermute(value, axis, [(j, j ^ k) for j in range(size)])


def tree_sum(parts):
    parts = list(parts)
    while len(parts) > 1:
        parts = [parts[i] + parts[i + 1] for i in range(0, len(parts), 2)]
    return parts[0]


def factor_kernel(
    x_ref, cot_ref, valid_ref, gain_ref, wft_ref, pos_ref,
    h1_ref, go_ref, s1_ref, q_ref, qt_ref, qf_ref, kv_ref, cos_ref, sin_ref, ft,
):
    x = x_ref[...].astype(F32)
    s1 = lax.rsqrt(jnp.mean(x * x, axis=1, keepdims=True) + EPS)
    s1_ref[...] = s1
    h1 = (x * s1 * gain_ref[...]).astype(BF16)
    h1_ref[...] = h1
    go_ref[...] = (cot_ref[...].astype(F32) * valid_ref[...]).astype(BF16)
    half = lax.broadcasted_iota(jnp.int32, cos_ref.shape, 0).astype(F32)
    angles = pos_ref[...] * jnp.exp(-jnp.log(10000.0) * (2.0 * half) / DH)
    cosine, sine = jnp.cos(angles), jnp.sin(angles)
    cos_ref[...] = cosine
    sin_ref[...] = sine
    ft[:wft_ref.shape[0], :] = mm(wft_ref[...], h1, NT)
    kv_ref[:KA, :] = ft[QF:QF + KA, :].astype(BF16)
    for r in range(2 * RK):
        rows = ft[QF + KA + r * DH:QF + KA + (r + 1) * DH, :]
        if r < RK:
            rows = turn(rows, cosine, sine)
        kv_ref[KA + r * DH:KA + (r + 1) * DH, :] = rows.astype(BF16)
    qf_ref[:QA, :] = ft[:QA, :]
    for r in range(RQ):
        qf_ref[QA + r * DH:QA + (r + 1) * DH, :] = turn(ft[QA + r * DH:QA + (r + 1) * DH, :], cosine, sine)
    for h in range(H):
        total = None
        for r in range(RQ):
            term = qf_ref[r * H + h:r * H + h + 1, :] * qf_ref[QA + r * DH:QA + (r + 1) * DH, :]
            total = term if total is None else total + term
        ft[h * DH:(h + 1) * DH, :] = total / RQ
    qt = ft[:H * DH, :]
    qt_ref[...] = qt.astype(BF16)
    q_ref[...] = qt.T.astype(BF16)


def project(x, cot, valid, gain, w_fact_t, pos):
    tokens, width = x.shape
    nf = w_fact_t.shape[0]
    angles = ((DH // 2, tokens), F32)
    return call(
        factor_kernel,
        [((tokens, width), BF16), ((tokens, width), BF16), ((tokens, 1), F32), ((tokens, H * DH), BF16),
         ((H * DH, tokens), BF16), ((QF, tokens), F32), ((KF, tokens), BF16), angles, angles],
        [vmem()] * 6,
        (x, cot, valid, gain, w_fact_t, pos),
        [pltpu.VMEM((max(nf, H * DH), tokens), F32)],
        2 * tokens * width * nf, 2 * width * nf, "factors",
    )


def load_factors(pieces, a_rows, b_rows):
    at = 0
    for piece in pieces:
        n = piece.shape[1]
        a_rows[:, at:at + n] = piece[:KA, :].astype(F32)
        b_rows[:, at:at + n] = piece[KA:, :].astype(F32)
        at += n


def expand_pair(pair, side, a_rows, b_rows):
    halves = []
    for sub in range(2):
        total = None
        for r in range(RK):
            a = a_rows[pl.ds((side * RK + r) * H + 2 * pair + sub, 1), :]
            term = a * b_rows[(side * RK + r) * DH:(side * RK + r + 1) * DH, :]
            total = term if total is None else total + term
        halves.append((total * (1.0 / RK)).astype(BF16))
    return jnp.concatenate(halves, axis=0)


def stack_pair(rows):
    lane = lax.broadcasted_iota(jnp.int32, rows.shape, 1)
    zero = jnp.zeros_like(rows)
    return jnp.concatenate([jnp.where(lane < DH, rows, zero), jnp.where(lane < DH, zero, rows)], axis=0)


def pair_lanes(pair):
    return pl.ds(pl.multiple_of(pair * 2 * DH, 2 * DH), 2 * DH)


def attend_kernel(n_pieces, *refs):
    q_ref, bias_ref, wo_ref, x_ref, gain_ref = refs[:5]
    pieces = refs[5:5 + n_pieces]
    h2_ref, mixed, resid_ref, lse_ref, a_rows, b_rows = refs[5 + n_pieces:]
    tokens, width = x_ref.shape
    load_factors(pieces, a_rows, b_rows)
    bias = bias_ref[...]
    bias = jnp.concatenate([bias, bias], axis=0)

    def step(pair, carry):
        keys = expand_pair(pair, 0, a_rows, b_rows)
        values = expand_pair(pair, 1, a_rows, b_rows)
        q = stack_pair(q_ref[:, pair_lanes(pair)] * SCALE)
        scores = mm(q, keys) + bias
        top = jnp.max(scores, axis=1, keepdims=True)
        exponent = jnp.exp(scores - top)
        total = jnp.sum(exponent, axis=1, keepdims=True)
        probs = (exponent * (1.0 / total)).astype(BF16)
        lse_ref[pair] = top + jnp.log(total)
        out = mm(probs, values, NT)
        lane = lax.broadcasted_iota(jnp.int32, (tokens, 2 * DH), 1)
        mixed[:, pair_lanes(pair)] = jnp.where(lane < DH, out[:tokens], out[tokens:]).astype(BF16)
        return carry

    lax.fori_loop(0, H // 2, step, 0, unroll=True)
    resid = x_ref[...].astype(F32) + mm(mixed[...], wo_ref[...])
    resid_ref[...] = resid
    s2 = lax.rsqrt(jnp.mean(resid * resid, axis=1, keepdims=True) + EPS)
    h2_ref[...] = (resid * s2 * gain_ref[...]).astype(BF16)


def attend(q, bias, w_out, x, gain, pieces):
    tokens, width = x.shape
    slots = sum(p.shape[1] for p in pieces)
    return call(
        functools.partial(attend_kernel, len(pieces)),
        [((tokens, width), BF16), ((tokens, H * DH), BF16), ((tokens, width), F32), ((H // 2, 2 * tokens, 1), F32)],
        [vmem()] * (5 + len(pieces)),
        (q, bias, w_out, x, gain, *pieces),
        [pltpu.VMEM((KA, slots), F32), pltpu.VMEM((KB, slots), F32)],
        4 * tokens * slots * H * DH, 2 * width * width, "attend",
    )


def attend_back_kernel(n_pieces, *refs):
    q_ref, qt_ref, gm_ref, gmt_ref, lse_ref, bias_ref, qf_ref, cos_ref, sin_ref = refs[:9]
    pieces = refs[9:9 + n_pieces]
    gq_ref, own_ref, send_ref, a_rows, b_rows, ga_rows, gb_rows, gqb_rows = refs[9 + n_pieces:]
    tokens = q_ref.shape[0]
    load_factors(pieces, a_rows, b_rows)
    gb_rows[...] = jnp.zeros_like(gb_rows)
    gqb_rows[...] = jnp.zeros_like(gqb_rows)

    def spread(rows):
        top = lax.broadcasted_iota(jnp.int32, rows.shape, 0) < DH
        zero = jnp.zeros_like(rows)
        return jnp.concatenate([jnp.where(top, rows, zero), jnp.where(top, zero, rows)], axis=1)

    def step(pair, carry):
        keys = expand_pair(pair, 0, a_rows, b_rows)
        values = expand_pair(pair, 1, a_rows, b_rows)
        rows = pl.ds(pl.multiple_of(pair * 2 * DH, 2 * DH), 2 * DH)
        both = (
            stack_pair(q_ref[:, pair_lanes(pair)] * SCALE), stack_pair(gm_ref[:, pair_lanes(pair)]),
            spread(qt_ref[rows, :] * SCALE), spread(gmt_ref[rows, :]), lse_ref[pair],
        )
        takes = [slice(0, 2 * tokens)] if keys.shape[1] <= 2048 else [slice(0, tokens), slice(tokens, 2 * tokens)]
        grad_q, grad_k, grad_v = [], None, None
        for take in takes:
            q, g, qt, gt, lse = both[0][take], both[1][take], both[2][:, take], both[3][:, take], both[4][take]
            heads = q.shape[0] // tokens
            scores = mm(q, keys) + jnp.concatenate([bias_ref[...]] * heads, axis=0)
            probs = jnp.exp(scores - lse)
            grad_probs = mm(g, values)
            inner = jnp.sum(probs * grad_probs, axis=1, keepdims=True)
            grad_scores = (probs * (grad_probs - inner)).astype(BF16)
            grad_q.append(mm(grad_scores, keys, NT).T * SCALE)
            gk, gv = mm(qt, grad_scores), mm(gt, probs.astype(BF16))
            grad_k, grad_v = (gk, gv) if grad_k is None else (grad_k + gk, grad_v + gv)
        grad_q = jnp.concatenate(grad_q, axis=1)
        for sub in range(2):
            head = 2 * pair + sub
            part = slice(sub * DH, (sub + 1) * DH)
            for side, grad in ((0, grad_k[part]), (1, grad_v[part])):
                for r in range(RK):
                    s = side * RK + r
                    row = pl.ds(s * H + head, 1)
                    seg = slice(s * DH, (s + 1) * DH)
                    ga_rows[row, :] = jnp.sum(grad * b_rows[seg, :], axis=0, keepdims=True) * (1.0 / RK)
                    gb_rows[seg, :] += grad * (a_rows[row, :] * (1.0 / RK))
            dq = grad_q[part, sub * tokens:(sub + 1) * tokens]
            for r in range(RQ):
                row = pl.ds(r * H + head, 1)
                seg = slice(QA + r * DH, QA + (r + 1) * DH)
                gq_ref[row, :] = jnp.sum(dq * qf_ref[seg, :], axis=0, keepdims=True) * (1.0 / RQ)
                gqb_rows[r * DH:(r + 1) * DH, :] += dq * (qf_ref[row, :] * (1.0 / RQ))
        return carry

    lax.fori_loop(0, H // 2, step, 0)
    cosine, sine = cos_ref[...], sin_ref[...]
    for r in range(RQ):
        gq_ref[QA + r * DH:QA + (r + 1) * DH, :] = turn_back(gqb_rows[r * DH:(r + 1) * DH, :], cosine, sine)
    at = 0
    for j in range(n_pieces):
        n = pieces[j].shape[1]
        out_ref = send_ref if j % 2 else own_ref
        out_ref[j // 2, :KA, :] = ga_rows[:, at:at + n].astype(BF16)
        out_ref[j // 2, KA:, :] = gb_rows[:, at:at + n].astype(BF16)
        at += n


def attend_back(q, qt, gm, gmt, lse, bias, qf, cosine, sine, pieces):
    tokens = q.shape[0]
    slots = sum(p.shape[1] for p in pieces)
    n = len(pieces)
    return call(
        functools.partial(attend_back_kernel, n),
        [((QF, tokens), F32)] + [((n // 2, KF, slots // n), BF16)] * 2,
        [vmem()] * (9 + n),
        (q, qt, gm, gmt, lse, bias, qf, cosine, sine, *pieces),
        [pltpu.VMEM((KA, slots), F32), pltpu.VMEM((KB, slots), F32), pltpu.VMEM((KA, slots), F32),
         pltpu.VMEM((KB, slots), F32), pltpu.VMEM((RQ * DH, tokens), F32)],
        10 * tokens * slots * H * DH, 4 * tokens * slots, "attend_back",
    )


def ffn_kernel(
    place_ref, h2_ref, go_ref, resid_ref, gain_ref, mixed_ref, wg_hbm, wu_hbm, wd_hbm, wo_hbm, *refs,
):
    out_ref, gain_grad_ref, gres_ref, gm_ref, gmt_ref = refs[:5]
    mgx_refs, (branch, grad_h2, gb_cols, wg, wu, wd, wo, sems) = refs[5:-8], refs[-8:]
    width, ff = wg.shape
    n_chunks = sems.shape[1]
    chunk = ff // n_chunks
    copies = []
    for j in range(n_chunks):
        part = pl.ds(j * chunk, chunk)
        copies.append([
            pltpu.make_async_copy(wg_hbm.at[:, part], wg.at[:, part], sems.at[0, j]),
            pltpu.make_async_copy(wu_hbm.at[:, part], wu.at[:, part], sems.at[1, j]),
            pltpu.make_async_copy(wd_hbm.at[part, :], wd.at[part, :], sems.at[2, j]),
        ])
    wo_copy = pltpu.make_async_copy(wo_hbm, wo, sems.at[3, 0])
    for group in copies:
        for copy in group:
            copy.start()
    wo_copy.start()
    h2, go = h2_ref[...], go_ref[...]
    groups = [list(range(0, min(3, n_chunks)))]
    groups += [list(range(j, min(j + 4, n_chunks))) for j in range(3, n_chunks, 4)]
    for group in groups:
        for j in group:
            for copy in copies[j]:
                copy.wait()
        part = slice(group[0] * chunk, (group[-1] + 1) * chunk)
        gate, up = mm(h2, wg[:, part]), mm(h2, wu[:, part])
        grad_hidden = mm(go, wd[part, :], NT)
        sig = jax.nn.sigmoid(gate)
        silu = gate * sig
        hidden = (silu * up).astype(BF16)
        grad_gate = (grad_hidden * up * sig * (1.0 + gate * (1.0 - sig))).astype(BF16)
        grad_up = (grad_hidden * silu).astype(BF16)
        more_branch = mm(hidden, wd[part, :])
        more_grad = mm(grad_gate, wg[:, part], NT) + mm(grad_up, wu[:, part], NT)
        if group[0] == 0:
            branch[...] = more_branch
            grad_h2[...] = more_grad
        else:
            branch[...] += more_branch
            grad_h2[...] += more_grad
    resid = resid_ref[...]
    out_ref[...] = (resid + branch[...]).astype(BF16)
    s2 = lax.rsqrt(jnp.mean(resid * resid, axis=1, keepdims=True) + EPS)
    n2 = resid * s2
    gh = grad_h2[...]
    gain_grad_ref[...] = jnp.sum(gh * n2, axis=0, keepdims=True)
    g2 = gh * gain_ref[...]
    gres = go.astype(F32) + s2 * (g2 - n2 * jnp.mean(g2 * n2, axis=1, keepdims=True))
    gres_ref[...] = gres
    gb = gres.astype(BF16)
    gb_cols[...] = gb
    wo_copy.wait()
    gm = mm(gb, wo[...], NT)
    gm_ref[...] = gm.astype(BF16)
    gmt_ref[...] = gm.T.astype(BF16)
    for k, mgx_ref in enumerate(mgx_refs):
        cols = mgx_ref.shape[1] - width
        mgx_ref[:, :width] = mixed_ref[...]
        mgx_ref[:, width:] = gb_cols[:, pl.ds(pl.multiple_of((place_ref[0] ^ k) * cols, cols), cols)]


def feed_forward(place, h2, go, w_gate, w_up, w_down, resid, gain, w_out, mixed, n_rows):
    tokens, width = resid.shape
    ff = w_gate.shape[1]
    chunk = 256 if ff % 256 == 0 else 128
    return call(
        ffn_kernel,
        [((tokens, width), BF16), ((1, width), F32), ((tokens, width), F32), ((tokens, width), BF16),
         ((width, tokens), BF16)] + [((tokens, width + width // n_rows), BF16)] * n_rows,
        [smem()] + [vmem()] * 5 + [hbm()] * 4,
        (place, h2, go, resid, gain, mixed, w_gate, w_up, w_down, w_out),
        [pltpu.VMEM((tokens, width), F32), pltpu.VMEM((tokens, width), F32), pltpu.VMEM((tokens, width), BF16),
         pltpu.VMEM((width, ff), BF16), pltpu.VMEM((width, ff), BF16), pltpu.VMEM((ff, width), BF16),
         pltpu.VMEM((width, width), BF16), pltpu.SemaphoreType.DMA((4, ff // chunk))],
        12 * tokens * width * ff, 6 * width * ff, "feed_forward",
    )


def weight_kernel(n_pieces, ordered, place_ref, wg_ref, wu_ref, wd_ref, go_other, *refs):
    h2_pieces, go_same = refs[:n_pieces], refs[n_pieces:n_pieces + n_pieces // 2]
    up_keep, up_send, down_keep, down_send, h2s, gos, wds, window, turned, sems = refs[n_pieces + n_pieces // 2:]
    tokens, width = h2_pieces[0].shape
    ff, span = wds.shape[0], window.shape[2]
    at = (place_ref[0] * 2 + place_ref[1]) * ff
    start = jnp.minimum(at // 128 * 128, wg_ref.shape[1] - span)
    cut = pl.ds(pl.multiple_of(start, 128), span)
    groups = [[pltpu.make_async_copy(ref.at[:, cut], window.at[i], sems.at[2, i])] for i, ref in enumerate((wg_ref, wu_ref))]
    groups += [[], []]
    for j in range(n_pieces):
        rows = pl.ds(j * tokens, tokens)
        groups[2].append(pltpu.make_async_copy(h2_pieces[j], h2s.at[rows, :], sems.at[0, j]))
        half = n_pieces // 2
        go = go_same[j] if j < half else go_other.at[j - half]
        groups[3].append(pltpu.make_async_copy(go, gos.at[rows, :], sems.at[1, j]))
    groups[3].append(pltpu.make_async_copy(
        wd_ref.at[pl.ds(pl.multiple_of(at, 32), ff), :], wds, sems.at[1, n_pieces]))
    for group in groups:
        for copy in group:
            copy.start()
    own = pl.ds(pl.multiple_of(at - start, 32), ff)
    for i in range(2):
        groups[i][0].wait()
        turned[i] = window[i].T
    for copy in groups[2]:
        copy.wait()
    gate = mm(turned[0, own, :], h2s[...], NT)
    up = mm(turned[1, own, :], h2s[...], NT)
    for copy in groups[3]:
        copy.wait()
    grad_hidden = mm(wds[...], gos[...], NT)
    sig = jax.nn.sigmoid(gate)
    silu = gate * sig
    hidden = (silu * up).astype(BF16)
    grad_gate = (grad_hidden * up * sig * (1.0 + gate * (1.0 - sig))).astype(BF16)
    grad_up = (grad_hidden * silu).astype(BF16)
    kept = up_keep.shape[0]
    n_z = 2 * kept
    cols = width // n_z
    half = cols // 2
    for slot, k in enumerate(halving_order(n_z)):
        up_ref, down_ref, i = (up_keep, down_keep, slot) if slot < kept else (up_send, down_send, slot - kept)
        if ordered:
            z, core = place_ref[2] ^ k, place_ref[1]
            first = pl.ds(pl.multiple_of(z * cols + core * half, half), half)
            other = pl.ds(pl.multiple_of(z * cols + (1 - core) * half, half), half)
            straight = pl.ds(pl.multiple_of((z ^ place_ref[0]) * cols, cols), cols)
            h2c = jnp.concatenate([h2s[:, first], h2s[:, other]], axis=1)
        else:
            straight = slice(slot * cols, (slot + 1) * cols)
            h2c = h2s[:, straight]
        up_ref[i, :ff, :] = mm(grad_gate, h2c).astype(BF16)
        up_ref[i, ff:, :] = mm(grad_up, h2c).astype(BF16)
        down_ref[i] = mm(hidden, gos[:, straight]).astype(BF16)


def halving_order(n):
    order = [0]
    k = n // 2
    while k >= 1:
        order = order + [o | k for o in order]
        k //= 2
    return order


def weight_grads(place, w_gate, w_up, w_down, h2_pieces, go_same, go_other, n_z, ordered):
    n = len(h2_pieces)
    tokens, width = h2_pieces[0].shape
    ff = w_gate.shape[1] // n
    span = min(w_gate.shape[1], -(-ff // 128) * 128 + 128)
    total = n * tokens
    return call(
        functools.partial(weight_kernel, n, ordered),
        [((n_z // 2, 2 * ff, width // n_z), BF16)] * 2 + [((n_z // 2, ff, width // n_z), BF16)] * 2,
        [smem()] + [hbm()] * (4 + n + n // 2),
        (place, w_gate, w_up, w_down, go_other, *h2_pieces, *go_same),
        [pltpu.VMEM((total, width), BF16), pltpu.VMEM((total, width), BF16), pltpu.VMEM((ff, width), BF16),
         pltpu.VMEM((2, width, span), BF16), pltpu.VMEM((2, span, width), BF16), pltpu.SemaphoreType.DMA((3, n + 1))],
        12 * total * width * ff, 6 * width * ff + 4 * total * width, "weight_grads",
    )


def own_cut(ordered, place_ref, k, cols):
    if not ordered:
        return slice(k * cols, (k + 1) * cols)
    return pl.ds(pl.multiple_of(((place_ref[2] ^ k) * 2 + place_ref[1]) * cols, cols), cols)


def slab_kernel(n_out, ordered, place_ref, h1_other, *refs):
    *h1_same, h1_ref, sems = refs
    n_same = len(h1_same)
    tokens = h1_other.shape[1]
    cols = h1_ref.shape[1] // n_out
    copies = []
    for j in range(2 * n_same):
        piece = h1_same[j] if j < n_same else h1_other.at[j - n_same]
        for k in range(n_out):
            copies.append(pltpu.make_async_copy(
                piece.at[:, own_cut(ordered, place_ref, k, cols)],
                h1_ref.at[pl.ds(j * tokens, tokens), pl.ds(k * cols, cols)], sems.at[j, k]))
    for copy in copies:
        copy.start()
    for copy in copies:
        copy.wait()


def own_slab(place, h1_same, h1_other, n_out, cols, ordered):
    n, tokens, width = h1_other.shape
    if not ordered:
        return jnp.concatenate([piece[:, :width] for piece in h1_same] + [h1_other.reshape(-1, width)], axis=0)
    return call(
        functools.partial(slab_kernel, n_out, ordered),
        [((2 * n * tokens, n_out * cols), BF16)],
        [smem()] + [hbm()] * (1 + n),
        (place, h1_other, *h1_same),
        [pltpu.SemaphoreType.DMA((2 * n, n_out))],
        0, 4 * n * tokens * n_out * cols, "own_slab",
    )[0]


def out_kernel(n_out, ordered, place_ref, mine_ref, other_ref, *refs):
    out_refs, (wide, thin) = refs[:-2], refs[-2:]
    n_rows, tokens, both = mine_ref.shape
    part, cols = thin.shape[1], out_refs[0].shape[1]
    for i, ref in enumerate((mine_ref, other_ref)):
        for j in range(n_rows):
            rows = slice((i * n_rows + j) * tokens, (i * n_rows + j + 1) * tokens)
            thin[rows, :] = ref[j, :, both - part:]
            for k in range(n_out):
                wide[rows, k * cols:(k + 1) * cols] = ref[j, :, own_cut(ordered, place_ref, k, cols)]
    full = mm(thin[...].T, wide[...]).astype(BF16)
    for k, out_ref in enumerate(out_refs):
        out_ref[...] = full[:, k * cols:(k + 1) * cols]


def out_grads(place, mine, other, width, n_out, cols, ordered):
    n_rows, tokens, both = mine.shape
    part = both - width
    total = 2 * n_rows * tokens
    return call(
        functools.partial(out_kernel, n_out, ordered),
        [((part, cols), BF16)] * n_out,
        [smem(), vmem(), vmem()],
        (place, mine, other),
        [pltpu.VMEM((total, n_out * cols), BF16), pltpu.VMEM((total, part), BF16)],
        2 * total * part * n_out * cols, 4 * total * both, "out_grads",
    )


def fact_kernel(n_out, head, ordered, h1_ref, mine_ref, other_ref, *refs):
    carried, out_refs, thin = refs[:n_out], refs[n_out:-1], refs[-1]
    cols = out_refs[0].shape[1]
    rows, tokens = mine_ref.shape[1:]
    parts = [ref[j] for ref in (mine_ref, other_ref) for j in range(ref.shape[0])]
    for j, part in enumerate(parts):
        thin[:, j * tokens:(j + 1) * tokens] = part[head:, :]
    full = mm(thin[...], h1_ref[...]).astype(BF16)
    for k, out_ref in enumerate(out_refs):
        out_ref[head:rows, :] = full[:, k * cols:(k + 1) * cols]
        out_ref[rows:, :] = carried[k][...]
    if ordered:
        half = head // 2
        gains = tree_sum([p[:half].astype(F32) + p[half:head].astype(F32) for p in parts])
        high = gains.astype(BF16)
        low = (gains - high.astype(F32)).astype(BF16)
        for out_ref in out_refs:
            out_ref[:half, :] = high
            out_ref[half:head, :] = low


def fact_grads(h1_slab, mine, other, carried, head, ordered):
    n_rows, rows, tokens = mine.shape
    total = 2 * n_rows * tokens
    n_out = len(carried)
    part, cols = carried[0].shape
    return call(
        functools.partial(fact_kernel, n_out, head, ordered),
        [((rows + part, cols), BF16)] * n_out,
        [vmem()] * (3 + n_out),
        (h1_slab, mine, other, *carried),
        [pltpu.VMEM((rows - head, total), BF16)],
        2 * total * rows * n_out * cols, 2 * total * n_out * cols, "fact_grads",
    )


def input_kernel(
    n_parts, place_ref, gq_ref, *refs,
):
    parts = refs[:n_parts]
    wft_ref, x_ref, s1_ref, gain_ref, gres_ref, gain_two_ref, cos_ref, sin_ref = refs[n_parts:n_parts + 8]
    gin_ref, *gfx_refs = refs[n_parts + 8:-2]
    gf, gains = refs[-2:]
    cosine, sine = cos_ref[...], sin_ref[...]
    kv = tree_sum([part[...].astype(F32) for part in parts])
    gf[:QF, :] = gq_ref[...]
    gf[QF:QF + KA, :] = kv[:KA]
    for r in range(2 * RK):
        rows = kv[KA + r * DH:KA + (r + 1) * DH]
        if r < RK:
            rows = turn_back(rows, cosine, sine)
        gf[QF + KA + r * DH:QF + KA + (r + 1) * DH, :] = rows
    grad = gf[...].T.astype(BF16)
    grad_h1 = mm(grad, wft_ref[...])
    s1 = s1_ref[...]
    n1 = x_ref[...].astype(F32) * s1
    gain_one = jnp.sum(grad_h1 * n1, axis=0, keepdims=True)
    gain_two = gain_two_ref[...]
    g1 = grad_h1 * gain_ref[...]
    gin_ref[...] = gres_ref[...] + s1 * (g1 - n1 * jnp.mean(g1 * n1, axis=1, keepdims=True))
    tokens, width = x_ref.shape
    half = gains.shape[0]
    for i in range(half // 2):
        gains[i:i + 1, :] = gain_one[:, i * tokens:(i + 1) * tokens]
        gains[half // 2 + i:half // 2 + i + 1, :] = gain_two[:, i * tokens:(i + 1) * tokens]
    high = gains[...].astype(BF16)
    low = (gains[...] - high.astype(F32)).astype(BF16)
    for k, gfx_ref in enumerate(gfx_refs):
        part = gfx_ref.shape[0] - 2 * half
        gfx_ref[:half, :] = high
        gfx_ref[half:2 * half, :] = low
        gfx_ref[2 * half:, :] = gf[pl.ds(pl.multiple_of((place_ref[0] ^ k) * part, 8), part), :].astype(BF16)


def input_grads(place, gq, parts, w_fact_t, x, s1, gain, gres, gain_two, cosine, sine, n_rows):
    tokens, width = x.shape
    nf = w_fact_t.shape[0]
    half = 2 * width // tokens
    return call(
        functools.partial(input_kernel, len(parts)),
        [((tokens, width), F32)] + [((2 * half + nf // n_rows, tokens), BF16)] * n_rows,
        [smem()] + [vmem()] * (9 + len(parts)),
        (place, gq, *parts, w_fact_t, x, s1, gain, gres, gain_two, cosine, sine),
        [pltpu.VMEM((nf, tokens), F32), pltpu.VMEM((half, tokens), F32)],
        2 * tokens * width * nf, 2 * width * nf, "input_grads",
    )


def after(values, *others):
    flat, tree = jax.tree.flatten((values, others))
    return jax.tree.unflatten(tree, lax.optimization_barrier(flat))[0]


def body(inputs, lengths, gain_attn, w_fact, w_out, gain_ffn, w_gate, w_up, w_down, cotangent):
    seqs, local_len, width = inputs.shape
    tokens = seqs * local_len
    n_rows, n_ctx = lax.axis_size(ROW), lax.axis_size(CTX)
    n_z = n_ctx // 2
    row, ctx = lax.axis_index(ROW), lax.axis_index(CTX)
    z, core = ctx // 2, ctx % 2
    slots_all = local_len * n_ctx
    block_len = local_len // 2
    ff = w_gate.shape[1]
    ff_part = ff // (2 * n_rows)
    own_cols = width // n_ctx
    per = n_ctx // (2 * n_rows)
    ordered = own_cols % 128 == 0 and per == 1 and tokens == 128
    n_out = n_z if ordered else n_ctx
    place = jnp.stack([row, core, z]).astype(jnp.int32)

    within = jnp.arange(local_len, dtype=jnp.int32)
    local_pos = jnp.tile(slot_position(ctx * local_len + within, block_len, slots_all), seqs)
    local_seq = jnp.repeat(jnp.arange(seqs, dtype=jnp.int32), local_len)
    valid = (local_pos < jnp.repeat(lengths, local_len)).astype(F32)[:, None]
    piece_of = jnp.arange(n_ctx, dtype=jnp.int32) ^ ctx
    key_pos = jnp.tile(
        slot_position(piece_of[:, None] * local_len + within[None, :], block_len, slots_all)[:, None, :], (1, seqs, 1)
    ).reshape(-1)
    key_seq = jnp.tile(local_seq, n_ctx)
    key_len = jnp.tile(jnp.repeat(lengths, local_len), n_ctx)
    allowed = (
        (key_pos[None, :] <= local_pos[:, None])
        & (key_pos < key_len)[None, :]
        & (key_seq[None, :] == local_seq[:, None])
    )
    bias = jnp.where(allowed, 0.0, -1e30).astype(F32)

    x = inputs.reshape(tokens, width)
    gain_one, gain_two = gain_attn[None, :], gain_ffn[None, :]
    w_fact_t = w_fact.T

    def others(values, axis, n):
        return [swap(values[k], axis, k) for k in range(1, n)]

    def along_core(values):
        return list(values) + [swap(value, "core", 1) for value in values]

    def both_cores(values):
        mine = jnp.stack(values)
        return [mine, swap(mine, "core", 1)]

    h1, go, s1, q, qt, qf, kv, cosine, sine = project(
        x, cotangent.reshape(tokens, width), valid, gain_one, w_fact_t, local_pos.astype(F32)[None, :]
    )
    kv_z = [kv] + others([kv] * n_z, "z", n_z)
    kv_pieces = []
    for part in kv_z:
        kv_pieces += [part, swap(part, "core", 1)]
    go_same = [go] + others([go] * n_rows, ROW, n_rows)
    h2, mixed, resid, lse = attend(after(q, place), bias, w_out, x, gain_two, kv_pieces)
    h2_same = [h2] + others([h2] * n_rows, ROW, n_rows)
    go_same = after(go_same, h2)
    go_other = swap(jnp.stack(go_same), "core", 1)
    block_out, gain_two_part, gres, gm, gmt, *mgx = feed_forward(
        place, h2, after(go, go_same), w_gate, w_up, w_down, resid, gain_two, w_out, mixed, n_rows
    )
    h2_pieces = along_core(after(h2_same, gm, go_other))
    h1_same = [h1] + others(after([h1] * n_rows, gm), ROW, n_rows)
    up_keep, up_send, down_keep, down_send = weight_grads(
        place, w_gate, w_up, w_down, h2_pieces, go_same, go_other, n_z, ordered
    )
    if not ordered:
        turns = jnp.asarray(halving_order(n_z), jnp.int32) ^ z
        cores = jnp.arange(2, dtype=jnp.int32) ^ core
        up = jnp.take(jnp.concatenate([up_keep, up_send]), turns, axis=0)
        up = jnp.take(up.reshape(n_z, 2 * ff_part, 2, own_cols), cores, axis=2).reshape(up.shape)
        down = jnp.concatenate([down_keep, down_send]).transpose(1, 0, 2)
        down = down.reshape(per, ff_part // per, n_rows, width // n_rows).transpose(0, 2, 1, 3)
        down = jnp.take(down.reshape(n_z, ff_part, 2 * own_cols), turns, axis=0)
        up_keep, up_send, down_keep, down_send = up[:n_z // 2], up[n_z // 2:], down[:n_z // 2], down[n_z // 2:]

    h1_same = after(h1_same, up_send)
    up_got = swap(up_send, "z", 1)
    mg_same = [mgx[0]] + others(mgx, ROW, n_rows)
    gm_in = after(gm, up_send)
    h1_other = swap(jnp.stack(h1_same), "core", 1)
    gq, gkv_own, gkv_send = attend_back(q, qt, gm_in, gmt, lse, bias, qf, cosine, sine, kv_pieces)
    gkv_send, mg_same, h1_other, up_got = lax.optimization_barrier((gkv_send, mg_same, h1_other, up_got))
    down_got = swap(after(down_send, up_got), "z", 1)
    gkv_got = swap(gkv_send, "core", 1)
    mg_mine, mg_other = both_cores(mg_same)
    gkv_z = [(gkv_own[k].astype(F32) + gkv_got[k].astype(F32)).astype(BF16) for k in range(n_z)]
    kv_parts = [gkv_z[0]] + others(gkv_z, "z", n_z)
    kv_parts, down_got = lax.optimization_barrier((kv_parts, down_got))

    def own_blocks(parts):
        if ordered:
            return parts
        parts = jnp.take(jnp.stack(parts), (jnp.arange(n_z, dtype=jnp.int32) ^ z) * 2 + core, axis=0)
        return [parts[k] for k in range(n_z)]

    out_parts = out_grads(place, mg_mine, mg_other, width, n_out, own_cols, ordered)
    gq = after(gq, out_parts)

    def add_up(keep, got, hold, step=1):
        total = keep.astype(F32) + got.astype(F32)
        n = total.shape[0]
        while n > 1:
            n //= 2
            step *= 2
            kept, got = total[:n], swap(total[n:].astype(BF16), "z", step)
            total = (after(kept, *hold) if n == 1 else kept) + got.astype(F32)
        return total[0]

    ffn_keep = jnp.concatenate([up_keep, down_keep], axis=1)
    ffn_got = jnp.concatenate([after(up_got, kv_parts), down_got], axis=1)
    grad_inputs, *gfx = input_grads(
        place, gq, kv_parts, w_fact_t, x, s1, gain_one, gres, gain_two_part, cosine, sine, n_rows
    )
    head = gfx[0].shape[0] - w_fact.shape[1] // n_rows
    gf_same = [gfx[0]] + others(gfx, ROW, n_rows)
    h1_slab = own_slab(place, h1_same, after(h1_other, gfx[0]), n_out, own_cols, ordered)
    gf_all = both_cores(after(gf_same, h1_slab))
    tail_parts = own_blocks(fact_grads(h1_slab, *gf_all, out_parts, head, ordered))
    total = add_up(ffn_keep, ffn_got, tail_parts)
    tail_got = others(tail_parts, "z", n_z)
    up_total, down_total = total[:2 * ff_part], total[2 * ff_part:].reshape(ff // n_ctx, width // n_rows)
    mine, other = up_total[:, :own_cols], swap(up_total[:, own_cols:].astype(BF16), "core", 1).astype(F32)
    first = jnp.where(core == 0, mine, other)
    second = jnp.where(core == 0, other, mine)
    grad_gate = jnp.concatenate([first[:ff_part], second[:ff_part]], axis=0).T
    grad_up = jnp.concatenate([first[ff_part:], second[ff_part:]], axis=0).T

    moves = []
    for r in range(n_rows):
        for c in range(2):
            for p in range(n_z):
                b, s = p // n_rows, (p % n_rows) ^ (r if ordered else 0)
                moves.append((r * n_ctx + 2 * p + c, s * n_ctx + (r * 2 + c) * per + b))
    grad_down = lax.ppermute(down_total.astype(BF16), ROW + CTX, moves).astype(F32)

    tail_parts = after(tail_parts, grad_gate, grad_up)
    tail = tree_sum([part.astype(F32) for part in [tail_parts[0]] + tail_got])
    rows = gfx[0].shape[0]
    grad_fact, grad_out = tail[head:rows].T, tail[rows:].T
    if ordered:
        gains = (tail[:head // 2] + tail[head // 2:head]).reshape(2, width)
    else:
        sums = gfx[0][:head // 2].astype(F32) + gfx[0][head // 2:head].astype(F32)
        gains = lax.psum(sums, ROW + CTX).reshape(2, width)

    return (
        block_out.reshape(inputs.shape),
        grad_inputs.reshape(inputs.shape),
        gains[0],
        grad_fact,
        grad_out,
        gains[1],
        grad_gate,
        grad_up,
        grad_down,
    )


def solution(mesh):
    n_rows, n_ctx = mesh.shape["row"], mesh.shape["ctx"]
    fine = Mesh(mesh.devices.reshape(n_rows // 2, 2, n_ctx // 2, 2), ROW + CTX)
    placed = (P(ROW, CTX, None), P(ROW), P(), P(), P(), P(), P(), P(), P(), P(ROW, CTX, None))
    return jax.shard_map(
        body,
        mesh=fine,
        in_specs=placed,
        out_specs=(
            P(ROW, CTX, None), P(ROW, CTX, None), P(), P(CTX, ROW), P(CTX, ROW), P(), P(CTX, ROW), P(CTX, ROW),
            P(CTX, ROW),
        ),
        check_vma=False,
    )
```
